256 devices in a mesh: bead: 64 (over x, z, y_hi), slab: 4 (over y_lo, core).
Axes of the slice: x: 4, y: 4 (y_hi: 2, y_lo: 2; y = y_hi * 2 + y_lo), z: 8, core: 2. Of those that a mesh axis runs over, the one named last changes fastest.
Arguments:
- section: float32 [64, 3, 16384], P('bead', None, 'slab'), may hold values from -0.4 to 12, as said below
- momentum: float32 [64, 3, 16384], P('bead', None, 'slab'), may hold values from -6 to 6
- neighbours: int32 [4, 32, 8], P('slab'), may hold values from 0 to 39
- border_rows: int32 [4, 2, 512], P('slab'), may hold values from 0 to 2047
- counts: int32 [4], P('slab'), may hold values from 2048 to 4096
Outputs:
- new_section: float32 [64, 3, 16384], P('bead', None, 'slab')
- new_momentum: float32 [64, 3, 16384], P('bead', None, 'slab')
The draws below stay inside these ranges and needn't reach their ends.
Inputs may be any that keep to these rules, and one draw needn't show every extreme that they name: section[0] holds positions whose component 0 lies in its slab's range [3 s, 3 s + 3) and components 1 and 2 in [0, 3); the other beads hold displacements within 0.4. `border_rows`: every listed halo row is below the sending slab's count.
All inputs are finite; a program needn't handle non-finite values.
Results may differ from the reference program's by a relative error of at most 0.0003.
Values sent between devices are 32-bit elements; how exact they have to be, the bound alone decides.
A program may use at most 64 MiB of HBM per device.

```python
import math
import jax
import jax.numpy as jnp
from jax import lax

ATOM_DEV = 4096
NBR = 8
BEADS = 64
ATOMS = 16384
TILES = 32
HALO = 512
EXT_TILES = 40
N_SLAB = 4


def draw_section(key, part):
    first_key = jax.random.fold_in(key, 11)
    second_key = jax.random.fold_in(key, 12)
    third_key = jax.random.fold_in(key, 13)
    atom = jnp.arange(ATOMS, dtype=jnp.int32)
    slab = (atom // ATOM_DEV).astype(jnp.float32)
    base_x = slab * 3.0 + jax.random.uniform(first_key, (ATOMS,), jnp.float32, 0.0, 2.999)
    base_rest = jax.random.uniform(second_key, (2, ATOMS), jnp.float32, 0.0, 2.999)
    anchor = jnp.concatenate([base_x[None], base_rest], axis=0)
    shifted = 0.1 * jax.random.truncated_normal(third_key, -4.0, 4.0, (BEADS - 1, 3, ATOMS), jnp.float32)
    return jnp.concatenate([anchor[None], shifted], axis=0)


def plant(values, rng, smallest, largest):
    longest = values.shape.index(max(values.shape))
    spots = []
    for shift in (0, 1):
        where = [jax.random.randint(jax.random.fold_in(rng, axis), (), 0, length) for axis, length in enumerate(values.shape)]
        where[longest] = (where[longest] + shift) % values.shape[longest]
        spots.append(tuple(where))
    return values.at[spots[0]].set(smallest).at[spots[1]].set(largest)


def levels(stream_key, dims, cuts, low, largest):
    def one(position, parts):
        heights = jax.random.uniform(jax.random.fold_in(jax.random.fold_in(stream_key, 6), position), (parts,), jnp.float32, low / len(cuts), largest / len(cuts))
        return jnp.repeat(jnp.exp(heights), dims[position] // parts).reshape((-1,) + (1,) * (len(dims) - position - 1))

    level = one(*cuts[0])
    for cut in cuts[1:]:
        level = level * one(*cut)
    return level


def gaussian(rng, shape, deviation, bound, cuts=(), kind=jnp.bfloat16):
    gain = levels(rng, shape, cuts, -0.22, 0.18) if cuts else 1.0
    values = jax.random.normal(rng, shape, jnp.float32) * deviation * gain
    return jnp.minimum(jnp.maximum(values, -bound), bound).astype(kind)


def setup_inputs(seed: int = 0) -> dict:
    arg_keys = jax.random.split(jax.random.key(seed), 6)
    section = draw_section(jax.random.fold_in(arg_keys[5], 71), 0)
    momentum = gaussian(arg_keys[1], (BEADS, 3, ATOMS), 1.0, 6.0, ((0, 64), (2, 4)), jnp.float32)
    neighbours = plant(jax.random.randint(arg_keys[2], (N_SLAB, TILES, NBR), 0, EXT_TILES), jax.random.fold_in(arg_keys[2], 1), 0, EXT_TILES - 1).astype(jnp.int32)
    border_rows = plant(jax.random.randint(arg_keys[3], (N_SLAB, 2, HALO), 0, ATOM_DEV // 2), jax.random.fold_in(arg_keys[3], 1), 0, (ATOM_DEV // 2) - 1).astype(jnp.int32)
    counts = plant(jax.random.randint(arg_keys[4], (N_SLAB,), ATOM_DEV // 2, ATOM_DEV + 1), jax.random.fold_in(arg_keys[4], 1), ATOM_DEV // 2, ATOM_DEV).astype(jnp.int32)
    return {"section": section, "momentum": momentum, "neighbours": neighbours, "border_rows": border_rows, "counts": counts}


time_step = 0.1
omega_sq = 4.0
slab_width = 3.0
cut_sq = 16.0


def pair_forces(atom_places, lower, upper, neighbours, count):
    tile = 128
    layer_width = atom_places.shape[1]
    halo = lower.shape[1]
    extended = jnp.concatenate([lower, atom_places, upper], axis=1)
    rows = jnp.arange(extended.shape[1], dtype=jnp.int32)
    live = jnp.logical_or(rows < halo, rows >= halo + layer_width)
    live = jnp.logical_or(live, rows - halo < count)
    ext_mask = live.astype(jnp.float32).reshape(-1, tile)
    ext_tiles = extended.reshape(3, -1, tile)
    tiles = layer_width // tile
    group = math.gcd(tiles, 8)
    own = atom_places.reshape(3, tiles // group, group, tile).transpose(1, 0, 2, 3)
    lists = neighbours.reshape(tiles // group, group, -1)

    def block(item):
        own_block, list_block = item
        partner = ext_tiles[:, list_block].reshape(3, group, -1)
        weight = ext_mask[list_block].reshape(group, -1)
        diff = own_block[:, :, :, None] - partner[:, :, None, :]
        dist = jnp.sum(diff * diff, axis=0)
        inverse = 1.0 / (dist + 1.0)
        inv_two = inverse * inverse
        inv_four = inv_two * inv_two
        inv_seven = inv_four * inv_two * inverse
        cutoff = jnp.maximum(1.0 - dist / cut_sq, 0.0)
        factor = (48.0 * inv_seven - 24.0 * inv_four) * cutoff * cutoff * weight[:, None, :]
        return jnp.sum(diff * factor[None], axis=-1)

    result = lax.map(block, (own, lists))
    force = result.transpose(1, 0, 2, 3).reshape(3, layer_width)
    own_live = (jnp.arange(layer_width, dtype=jnp.int32) < count).astype(jnp.float32)
    return force * own_live[None, :]


def reference(section, momentum, neighbours, border_rows, counts):
    bead_replicas = section.shape[0]
    slab_layers = N_SLAB
    layer_width = section.shape[2] // slab_layers
    level = jnp.arange(bead_replicas, dtype=jnp.int32).astype(jnp.float32)[:, None, None]
    scaled = jnp.where(level > 0, section / jnp.maximum(level, 1.0), 0.0)
    suffix = jnp.cumsum(scaled[::-1], axis=0)[::-1]
    atom_places = jnp.where(level > 0, section[0][None] + level * suffix, section)
    slab_split = atom_places.reshape(bead_replicas, 3, slab_layers, layer_width)
    upward_send = jnp.take_along_axis(slab_split, border_rows[:, 0][None, None], axis=3)
    downward_send = jnp.take_along_axis(slab_split, border_rows[:, 1][None, None], axis=3)
    box = slab_width * slab_layers
    slab_ids = jnp.arange(slab_layers, dtype=jnp.int32)
    first_axis = jnp.array([1.0, 0.0, 0.0], dtype=jnp.float32)[None, :, None, None]
    low_shift = jnp.where(slab_ids == 0, box, 0.0).astype(jnp.float32)[None, None, :, None]
    up_shift = jnp.where(slab_ids == slab_layers - 1, box, 0.0).astype(jnp.float32)[None, None, :, None]
    lower = jnp.roll(upward_send, 1, axis=2) - low_shift * first_axis
    upper = jnp.roll(downward_send, -1, axis=2) + up_shift * first_axis

    item_positions = slab_split.transpose(0, 2, 1, 3).reshape(bead_replicas * slab_layers, 3, layer_width)
    items_low = lower.transpose(0, 2, 1, 3).reshape(bead_replicas * slab_layers, 3, -1)
    items_up = upper.transpose(0, 2, 1, 3).reshape(bead_replicas * slab_layers, 3, -1)
    items_nbr = jnp.broadcast_to(neighbours[None], (bead_replicas,) + neighbours.shape).reshape((bead_replicas * slab_layers,) + neighbours.shape[1:])
    items_cnt = jnp.broadcast_to(counts[None], (bead_replicas, slab_layers)).reshape(-1)

    def one(item):
        return pair_forces(item[0], item[1], item[2], item[3], item[4])

    forces = lax.map(one, (item_positions, items_low, items_up, items_nbr, items_cnt))
    forces = forces.reshape(bead_replicas, slab_layers, 3, layer_width).transpose(0, 2, 1, 3).reshape(bead_replicas, 3, slab_layers * layer_width)
    bead_force = forces / float(bead_replicas)
    prefix = jnp.cumsum(level * bead_force, axis=0)
    total = jnp.sum(bead_force, axis=0)
    section_force = jnp.where(level > 0, prefix / jnp.maximum(level, 1.0), total[None])
    mass = jnp.where(level > 0, (level + 1.0) / jnp.maximum(level, 1.0), 1.0)
    spring = jnp.where(level > 0, omega_sq * mass, 0.0)
    step = time_step / 3.0
    p = momentum + 0.5 * time_step * section_force
    u = section
    for turn in range(3):
        p = p - 0.5 * step * spring * u
        u = u + step * p / mass
        p = p - 0.5 * step * spring * u
    return u, p
```

```python
import functools

import jax
import jax.numpy as jnp
from jax import lax
from jax.experimental import pallas as pl
from jax.experimental.pallas import tpu as pltpu
from jax.sharding import PartitionSpec as P

MESH = pl.DeviceIdType.MESH
time_step = 0.1
omega_sq = 4.0
slab_width = 3.0
NX, NZ, NY = 4, 8, 2
TILE = 128
KROWS = 32
F32 = jnp.float32
BF16 = jnp.bfloat16


def place():
    bead = lax.axis_index("bead")
    x = bead // (NZ * NY)
    z = (bead // NY) % NZ
    y = bead % NY
    return x, z, y


def bead_of(x, z, y):
    return (x * NZ + z) * NY + y


def to_bead(bead):
    return (bead, lax.axis_index("slab"))


def group_steps():
    return [(dz, dy) for dz in range(NZ) for dy in range(NY) if dz or dy]


def greet(extra=()):
    x, z, y = place()
    barrier = pltpu.get_barrier_semaphore()
    count = 0
    for dz, dy in group_steps():
        target = bead_of(x, (z + dz) % NZ, (y + dy) % NY)
        pl.semaphore_signal(barrier, inc=1, device_id=to_bead(target), device_id_type=MESH)
        count += 1
    for dx in range(1, NX):
        target = bead_of((x + dx) % NX, z, y)
        pl.semaphore_signal(barrier, inc=1, device_id=to_bead(target), device_id_type=MESH)
        count += 1
    for device in extra:
        pl.semaphore_signal(barrier, inc=1, device_id=device, device_id_type=MESH)
        count += 1
    pl.semaphore_wait(barrier, count)


def slot_of(dz, dy):
    return dz * NY + dy


def scatter_chunks(src, r1, send_sem, recv_sem, width):
    x, z, y = place()
    copies = []
    for k, (dz, dy) in enumerate(group_steps()):
        tz = (z + dz) % NZ
        copy = pltpu.make_async_remote_copy(
            src_ref=src.at[:, pl.ds(pl.multiple_of(tz * width, width), width)],
            dst_ref=r1.at[slot_of(dz, dy)],
            send_sem=send_sem.at[k],
            recv_sem=recv_sem.at[k],
            device_id=to_bead(bead_of(x, tz, (y + dy) % NY)),
            device_id_type=MESH,
        )
        copy.start()
        copies.append(copy)
    return copies


def exchange_x(t2, r2, send_sem, recv_sem):
    x, z, y = place()
    copies = []
    for dx in range(1, NX):
        copy = pltpu.make_async_remote_copy(
            src_ref=t2,
            dst_ref=r2.at[dx],
            send_sem=send_sem.at[dx],
            recv_sem=recv_sem.at[dx],
            device_id=to_bead(bead_of((x + dx) % NX, z, y)),
            device_id_type=MESH,
        )
        copy.start()
        copies.append(copy)
    return copies


def return_chunk(px, full, tz, dz, send_sem, recv_sem, width):
    x, z, y = place()
    copy = pltpu.make_async_remote_copy(
        src_ref=px.at[tz],
        dst_ref=full.at[:, pl.ds(pl.multiple_of(z * width, width), width)],
        send_sem=send_sem.at[dz],
        recv_sem=recv_sem.at[dz],
        device_id=to_bead(bead_of(x, tz, y)),
        device_id_type=MESH,
    )
    copy.start()
    return copy


def level_rows(bead, shape):
    return jnp.full(shape, bead.astype(F32), F32)


def forward_scan(section, r1, t2, r2, px, full, sems):
    s1, q1, s2, q2, s3, q3 = sems
    x, z, y = place()
    width = section.shape[1] // NZ
    shape = (3, width)
    sent = scatter_chunks(section, r1, s1, q1, width)
    r1[0] = section[:, pl.ds(pl.multiple_of(z * width, width), width)]
    for copy in sent:
        copy.wait_recv()

    def source(zs, ys):
        slot = ((z + (NZ - zs)) % NZ) * NY + (y + (NY - ys)) % NY
        return r1[slot]

    total = jnp.zeros(shape, F32)
    for zs in reversed(range(NZ)):
        kept = None
        for ys in reversed(range(NY)):
            level = level_rows(bead_of(x, zs, ys), (1, width))
            inverse = jnp.where(level > 0, 1.0 / jnp.maximum(level, 1.0), 0.0)
            total = total + source(zs, ys) * inverse
            kept = total if kept is None else jnp.where(y == ys, total, kept)
        px[zs] = kept
    t2[0] = total
    t2[1] = source(0, 0)
    swapped = exchange_x(t2, r2, s2, q2)
    for copy in swapped:
        copy.wait_recv()
    base = jnp.zeros(shape, F32)
    first = source(0, 0)
    for dx in range(1, NX):
        xs = (x + (NX - dx)) % NX
        base = base + jnp.where(xs > x, r2[dx, 0], 0.0)
        first = jnp.where(xs == 0, r2[dx, 1], first)
    returned = []
    for dz in list(range(1, NZ)) + [0]:
        tz = (z + dz) % NZ
        level = level_rows(bead_of(x, tz, y), (1, width))
        places = first + level * (px[tz] + base)
        if dz:
            px[tz] = places
            returned.append(return_chunk(px, full, tz, dz, s3, q3, width))
        else:
            full[:, pl.ds(pl.multiple_of(z * width, width), width)] = places
    for copy in returned:
        copy.wait_recv()
    for copy in sent + swapped + returned:
        copy.wait_send()


def backward_scan(force, r1, t2, r2, px, full, sems):
    s1, q1, s2, q2, s3, q3 = sems
    x, z, y = place()
    width = force.shape[1] // NZ
    shape = (3, width)
    sent = scatter_chunks(force, r1, s1, q1, width)
    r1[0] = force[:, pl.ds(pl.multiple_of(z * width, width), width)]
    for copy in sent:
        copy.wait_recv()

    def source(zs, ys):
        slot = ((z + (NZ - zs)) % NZ) * NY + (y + (NY - ys)) % NY
        return r1[slot]

    total = jnp.zeros(shape, F32)
    plain = jnp.zeros(shape, F32)
    for zs in range(NZ):
        kept = None
        for ys in range(NY):
            level = level_rows(bead_of(x, zs, ys), (1, width))
            one = source(zs, ys)
            plain = plain + one
            total = total + one * level
            kept = total if kept is None else jnp.where(y == ys, total, kept)
        px[zs] = kept
    t2[0] = total
    t2[1] = plain
    swapped = exchange_x(t2, r2, s2, q2)
    for copy in swapped:
        copy.wait_recv()
    base = jnp.zeros(shape, F32)
    for dx in range(1, NX):
        xs = (x + (NX - dx)) % NX
        base = base + jnp.where(xs < x, r2[dx, 0], 0.0)
        plain = plain + r2[dx, 1]
    returned = []
    for dz in list(range(1, NZ)) + [0]:
        tz = (z + dz) % NZ
        level = level_rows(bead_of(x, tz, y), (1, width))
        inverse = 1.0 / jnp.maximum(level, 1.0)
        result = jnp.where(level > 0, (px[tz] + base) * inverse, plain)
        if dz:
            px[tz] = result
            returned.append(return_chunk(px, full, tz, dz, s3, q3, width))
        else:
            full[:, pl.ds(pl.multiple_of(z * width, width), width)] = result
    for copy in returned:
        copy.wait_recv()
    for copy in sent + swapped + returned:
        copy.wait_send()


def gather_rows(full, border, which, reach):
    halo = border.shape[1]
    parts = []
    for n in range(halo // TILE):
        index = jnp.broadcast_to(border[pl.ds(which, 1), pl.ds(n * TILE, TILE)], (8, TILE))
        lane, block = index % TILE, index // TILE
        out = jnp.zeros((8, TILE), F32)
        for m in range(reach // TILE):
            piece = full[:, pl.ds(m * TILE, TILE)]
            piece = jnp.concatenate([piece, jnp.zeros((5, TILE), F32)], axis=0)
            taken = jnp.take_along_axis(piece, lane, axis=1, mode="promise_in_bounds")
            out = jnp.where(block == m, taken, out)
        parts.append(out[0:3])
    return jnp.concatenate(parts, axis=1)


def slab_peers():
    slab, count = lax.axis_index("slab"), lax.axis_size("slab")
    bead = lax.axis_index("bead")
    return (bead, (slab + 1) % count), (bead, (slab + count - 1) % count)


def halo_exchange(full, border, out, edge, landed, send_sem, recv_sem):
    up_peer, down_peer = slab_peers()
    edge[0] = gather_rows(full, border, 0, full.shape[1] // 2)
    edge[1] = gather_rows(full, border, 1, full.shape[1] // 2)
    copies = []
    for k, peer in enumerate((up_peer, down_peer)):
        copy = pltpu.make_async_remote_copy(
            src_ref=edge.at[k],
            dst_ref=landed.at[k],
            send_sem=send_sem.at[k],
            recv_sem=recv_sem.at[k],
            device_id=peer,
            device_id_type=MESH,
        )
        copy.start()
        copies.append(copy)
    return copies


def forward_kernel(section, border, out, r1, t2, r2, px, full, edge, landed, *sems):
    slab, count = lax.axis_index("slab"), lax.axis_size("slab")
    greet(slab_peers())
    forward_scan(section.at[0], r1, t2, r2, px, full, sems[:6])
    copies = halo_exchange(full, border.at[0], out, edge, landed, *sems[6:])
    halo = edge.shape[2]
    rows = full.shape[1]
    out[:, pl.ds(halo, rows)] = full[...]
    for copy in copies:
        copy.wait_recv()
    box = slab_width * count
    axis = lax.broadcasted_iota(jnp.int32, (3, halo), 0)
    low = jnp.where(slab == 0, -box, 0.0)
    high = jnp.where(slab == count - 1, box, 0.0)
    out[:, pl.ds(0, halo)] = landed[0] + jnp.where(axis == 0, low, 0.0)
    out[:, pl.ds(halo + rows, halo)] = landed[1] + jnp.where(axis == 0, high, 0.0)
    for copy in copies:
        copy.wait_send()


def backward_kernel(force, section, momentum, new_section, new_momentum, r1, t2, r2, px, full, *sems):
    greet()
    backward_scan(force, r1, t2, r2, px, full, sems[:6])
    bead = lax.axis_index("bead")
    shape = (1, full.shape[1])
    level = level_rows(bead, shape)
    safe = jnp.maximum(level, 1.0)
    mass = jnp.where(level > 0, (level + 1.0) / safe, 1.0)
    spring = jnp.where(level > 0, omega_sq * mass, 0.0)
    step = time_step / 3.0
    p = momentum[0] + (0.5 * time_step) * full[...]
    u = section[0]
    push = 0.5 * step * spring
    drift = step / mass
    for turn in range(3):
        p = p - push * u
        u = u + drift * p
        p = p - push * u
    new_section[0] = u
    new_momentum[0] = p


def split3(value):
    high = value.astype(BF16).astype(F32)
    rest = value - high
    middle = rest.astype(BF16).astype(F32)
    low = rest - middle
    return high, middle, low


def prepare_tile(places, centre, live):
    p = places - centre
    norm = jnp.sum(p * p, axis=0, keepdims=True)
    high, middle, low = split3(p)
    far = jnp.where(live, norm, 4096.0)
    ones = jnp.ones((3, TILE), F32)
    pad = jnp.zeros((KROWS - 24, TILE), F32)
    left = jnp.concatenate([high, high, middle, middle, high, low, *split3(far), ones, pad], axis=0)
    h2, m2, l2 = -2.0 * high, -2.0 * middle, -2.0 * low
    right = jnp.concatenate([h2, m2, h2, m2, l2, h2, ones, *split3(norm + 1.0), pad], axis=0)
    return left, right


def force_kernel(counts, neighbours, ext, out, lefts, lefts_t, rights):
    slab = lax.axis_index("slab")
    rows = out.shape[1]
    tiles = rows // TILE
    ext_tiles = ext.shape[1] // TILE
    halo_tiles = (ext_tiles - tiles) // 2
    count = counts[0]
    axis = lax.broadcasted_iota(jnp.int32, (3, TILE), 0)
    middle = (slab.astype(F32) + 0.5) * slab_width
    centre = jnp.where(axis == 0, middle, 0.5 * slab_width)
    lane = lax.broadcasted_iota(jnp.int32, (1, TILE), 1)

    def prepare(t, carry):
        places = ext[:, pl.ds(pl.multiple_of(t * TILE, TILE), TILE)]
        row = (t - halo_tiles) * TILE + lane
        live = (row < 0) | (row >= rows) | (row < count)
        left, right = prepare_tile(places, centre, live)
        lefts[t] = left.astype(BF16)
        lefts_t[t] = left.T.astype(BF16)
        rights[t] = right.astype(BF16)
        return carry

    lax.fori_loop(0, ext_tiles, prepare, 0)
    listed = neighbours.shape[2]

    def tile_force(i, carry):
        right = rights[i + halo_tiles]
        total = jnp.zeros((KROWS, TILE), F32)
        for n in range(0, listed, 2):
            pair = [neighbours[0, i, n], neighbours[0, i, n + 1]]
            factors = []
            for t in pair:
                q = jnp.dot(lefts_t[t], right, preferred_element_type=F32)
                r = 1.0 / q
                r2 = r * r
                c = jnp.maximum(17.0 - q, 0.0) * r2
                factors.append(((c * c) * (r2 * r - 0.5)).astype(BF16))
            f = jnp.concatenate(factors, axis=0)
            x = jnp.concatenate([lefts[t] for t in pair], axis=1)
            total = total + jnp.dot(x, f, preferred_element_type=F32)
        first = pl.multiple_of(i * TILE, TILE)
        mine = ext[:, pl.ds(pl.multiple_of(first + halo_tiles * TILE, TILE), TILE)] - centre
        moved = total[0:3] + total[6:9] + total[15:18]
        scale = jnp.where(first + lane < count, 48.0 / 256.0 / lax.axis_size("bead"), 0.0)
        out[:, pl.ds(first, TILE)] = (mine * total[21:22] - moved) * scale
        return carry

    lax.fori_loop(0, tiles, tile_force, 0)


def scan_scratch(rows):
    width = rows // NZ
    dma = pltpu.SemaphoreType.DMA
    return [
        pltpu.VMEM((NZ * NY, 3, width), F32),
        pltpu.VMEM((2, 3, width), F32),
        pltpu.VMEM((NX, 2, 3, width), F32),
        pltpu.VMEM((NZ, 3, width), F32),
        pltpu.VMEM((3, rows), F32),
    ], [
        dma((NZ * NY,)), dma((NZ * NY,)), dma((NX,)), dma((NX,)), dma((NZ,)), dma((NZ,)),
    ]


VM = pl.BlockSpec(memory_space=pltpu.VMEM)
SM = pl.BlockSpec(memory_space=pltpu.SMEM)


def forward(section, border_rows):
    rows, halo = section.shape[2], border_rows.shape[2]
    buffers, sems = scan_scratch(rows)
    dma = pltpu.SemaphoreType.DMA
    return pl.pallas_call(
        forward_kernel,
        out_shape=jax.ShapeDtypeStruct((3, rows + 2 * halo), F32),
        in_specs=[VM, VM],
        out_specs=VM,
        scratch_shapes=buffers
        + [pltpu.VMEM((2, 3, halo), F32)] * 2
        + sems
        + [dma((2,)), dma((2,))],
        compiler_params=pltpu.CompilerParams(collective_id=0, has_side_effects=True),
        name="forward_scan",
    )(section, border_rows)


def forces(ext, neighbours, counts, rows):
    ext_tiles = ext.shape[1] // TILE
    return pl.pallas_call(
        force_kernel,
        out_shape=jax.ShapeDtypeStruct((3, rows), F32),
        in_specs=[SM, SM, VM],
        out_specs=VM,
        scratch_shapes=[
            pltpu.VMEM((ext_tiles, KROWS, TILE), BF16),
            pltpu.VMEM((ext_tiles, TILE, KROWS), BF16),
            pltpu.VMEM((ext_tiles, KROWS, TILE), BF16),
        ],
        name="pair_forces",
    )(counts, neighbours, ext)


def backward(force, section, momentum):
    rows = section.shape[2]
    buffers, sems = scan_scratch(rows)
    like = jax.ShapeDtypeStruct(section.shape, F32)
    return pl.pallas_call(
        backward_kernel,
        out_shape=(like, like),
        in_specs=[VM, VM, VM],
        out_specs=(VM, VM),
        scratch_shapes=buffers + sems,
        compiler_params=pltpu.CompilerParams(collective_id=1, has_side_effects=True),
        name="backward_scan",
    )(force, section, momentum)


def body(section, momentum, neighbours, border_rows, counts):
    ext = forward(section, border_rows)
    force = forces(ext, neighbours, counts, section.shape[2])
    return backward(force, section, momentum)


def solution(mesh):
    return jax.shard_map(
        body,
        mesh=mesh,
        in_specs=(
            P("bead", None, "slab"),
            P("bead", None, "slab"),
            P("slab", None, None),
            P("slab", None, None),
            P("slab"),
        ),
        out_specs=(P("bead", None, "slab"), P("bead", None, "slab")),
        check_vma=False,
    )
```

```python
import functools
import math

import jax
import jax.numpy as jnp
from jax import lax
from jax.experimental import pallas as pl
from jax.experimental.pallas import tpu as pltpu
from jax.sharding import PartitionSpec as P

MESH = pl.DeviceIdType.MESH
time_step = 0.1
omega_sq = 4.0
slab_width = 3.0
reach_sq = 17.0
shrink = 1.0 / math.sqrt(reach_sq)
NX, NZ, NY = 4, 8, 2
TILE = 128
KROWS = 32
F32 = jnp.float32
BF16 = jnp.bfloat16
DMA = pltpu.SemaphoreType.DMA


def place():
    bead = lax.axis_index("bead")
    return bead // (NZ * NY), (bead // NY) % NZ, bead % NY


def bead_of(x, z, y):
    return (x * NZ + z) * NY + y


def to_bead(bead):
    return (bead, lax.axis_index("slab"))


def group_steps():
    return [(dz, dy) for dz in range(NZ) for dy in range(NY) if dz or dy]


def slab_peers():
    slab, count = lax.axis_index("slab"), lax.axis_size("slab")
    bead = lax.axis_index("bead")
    return (bead, (slab + 1) % count), (bead, (slab + count - 1) % count)


def partners():
    x, z, y = place()
    found = [to_bead(bead_of(x, (z + dz) % NZ, (y + dy) % NY)) for dz, dy in group_steps()]
    found += [to_bead(bead_of((x + dx) % NX, z, y)) for dx in range(1, NX)]
    return found + list(slab_peers())


def send(src, dst, send_sem, recv_sem, device):
    copy = pltpu.make_async_remote_copy(
        src_ref=src,
        dst_ref=dst,
        send_sem=send_sem,
        recv_sem=recv_sem,
        device_id=device,
        device_id_type=MESH,
    )
    copy.start()
    return copy


def scatter_chunks(chunk, r1, send_sem, recv_sem):
    x, z, y = place()
    copies = []
    for dz, dy in group_steps():
        tz = (z + dz) % NZ
        slot = dz * NY + dy
        device = to_bead(bead_of(x, tz, (y + dy) % NY))
        copies.append(send(chunk(tz), r1.at[slot], send_sem.at[slot], recv_sem.at[slot], device))
    return copies


def exchange_x(t2, r2, send_sem, recv_sem):
    x, z, y = place()
    return [
        send(t2, r2.at[dx], send_sem.at[dx], recv_sem.at[dx], to_bead(bead_of((x + dx) % NX, z, y)))
        for dx in range(1, NX)
    ]


def level_rows(bead):
    return jnp.full((1, 1, TILE), bead.astype(F32), F32)


def slot_from(zs, ys):
    x, z, y = place()
    return ((z + (NZ - zs)) % NZ) * NY + (y + (NY - ys)) % NY


def forward_scan(section, r1, t2, r2, px, land, sems):
    s1, q1, s2, q2, s3, q3 = sems
    x, z, y = place()
    sent = scatter_chunks(lambda c: section.at[:, c], r1, s1, q1)
    r1[0] = section[:, z]
    for copy in sent:
        copy.wait_recv()
    total = jnp.zeros(r1.shape[1:], F32)
    for zs in reversed(range(NZ)):
        kept = None
        for ys in reversed(range(NY)):
            level = level_rows(bead_of(x, zs, ys))
            inverse = jnp.where(level > 0, 1.0 / jnp.maximum(level, 1.0), 0.0)
            total = total + r1[slot_from(zs, ys)] * inverse
            kept = total if kept is None else jnp.where(y == ys, total, kept)
        px[zs] = kept
    first = r1[slot_from(0, 0)]
    t2[0] = total
    t2[1] = first
    swapped = exchange_x(t2, r2, s2, q2)
    for copy in swapped:
        copy.wait_recv()
    base = jnp.zeros(r1.shape[1:], F32)
    for dx in range(1, NX):
        xs = (x + (NX - dx)) % NX
        base = base + jnp.where(xs > x, r2[dx, 0], 0.0)
        first = jnp.where(xs == 0, r2[dx, 1], first)
    returned = []
    for dz in list(range(1, NZ)) + [0]:
        tz = (z + dz) % NZ
        level = level_rows(bead_of(x, tz, y))
        places = first + level * (px[tz] + base)
        if dz:
            px[tz] = places
            device = to_bead(bead_of(x, tz, y))
            returned.append(send(px.at[tz], land.at[1 + z], s3.at[dz], q3.at[dz], device))
        else:
            land[1 + z] = places
    for copy in returned:
        copy.wait_recv()
    return sent + swapped + returned


def backward_scan(force, r1, t2, r2, px, full, sems):
    s1, q1, s2, q2, s3, q3 = sems
    x, z, y = place()
    sent = scatter_chunks(lambda c: force.at[c], r1, s1, q1)
    r1[0] = force[z]
    for copy in sent:
        copy.wait_recv()
    total = jnp.zeros(r1.shape[1:], F32)
    plain = jnp.zeros(r1.shape[1:], F32)
    for zs in range(NZ):
        kept = None
        for ys in range(NY):
            one = r1[slot_from(zs, ys)]
            plain = plain + one
            total = total + one * level_rows(bead_of(x, zs, ys))
            kept = total if kept is None else jnp.where(y == ys, total, kept)
        px[zs] = kept
    t2[0] = total
    t2[1] = plain
    swapped = exchange_x(t2, r2, s2, q2)
    for copy in swapped:
        copy.wait_recv()
    base = jnp.zeros(r1.shape[1:], F32)
    for dx in range(1, NX):
        xs = (x + (NX - dx)) % NX
        base = base + jnp.where(xs < x, r2[dx, 0], 0.0)
        plain = plain + r2[dx, 1]
    returned = []
    for dz in list(range(1, NZ)) + [0]:
        tz = (z + dz) % NZ
        level = level_rows(bead_of(x, tz, y))
        inverse = 1.0 / jnp.maximum(level, 1.0)
        result = jnp.where(level > 0, (px[tz] + base) * inverse, plain)
        if dz:
            px[tz] = result
            device = to_bead(bead_of(x, tz, y))
            returned.append(send(px.at[tz], full.at[z], s3.at[dz], q3.at[dz], device))
        else:
            full[z] = result
    for copy in returned:
        copy.wait_recv()
    return sent + swapped + returned


def gather_rows(land, border, edge):
    tpc = land.shape[2]
    sub = lax.broadcasted_iota(jnp.int32, (8, TILE), 0)
    blocks = NZ // 2 * tpc // 8
    pieces = []
    for c in range(3):
        for b in range(blocks):
            rows = [land[1 + b * (8 // tpc) + m, c] for m in range(8 // tpc)]
            pieces.append(jnp.concatenate(rows, axis=0))
    for k in range(2):
        for n in range(tpc):
            index = jnp.broadcast_to(border[k : k + 1, n * TILE : (n + 1) * TILE], (8, TILE))
            lane, block = index % TILE, index // TILE
            for c in range(3):
                out = jnp.zeros((8, TILE), F32)
                for b in range(blocks):
                    taken = jnp.take_along_axis(
                        pieces[c * blocks + b], lane, axis=1, mode="promise_in_bounds"
                    )
                    out = jnp.where(block == b * 8 + sub, taken, out)
                edge[k, c, n : n + 1, :] = jnp.sum(out, axis=0, keepdims=True)


def halo_exchange(edge, land, send_sem, recv_sem):
    up_peer, down_peer = slab_peers()
    return [
        send(edge.at[0], land.at[0], send_sem.at[0], recv_sem.at[0], up_peer),
        send(edge.at[1], land.at[NZ + 1], send_sem.at[1], recv_sem.at[1], down_peer),
    ]


def split3(value):
    high = value.astype(BF16).astype(F32)
    rest = value - high
    middle = rest.astype(BF16).astype(F32)
    return high, middle, rest - middle


def prepare_tile(m, n, own, land, places, lefts, lefts_t, rights, centre_x, count):
    tpc = land.shape[2]
    t = m * tpc + n
    sub = lax.broadcasted_iota(jnp.int32, (8, TILE), 0)
    comp = sub % 4
    xs = [jnp.broadcast_to(land[m, c, pl.ds(n, 1), :], (8, TILE)) for c in range(3)]
    xs = [(v - w) * shrink for v, w in zip(xs, (centre_x, 0.5 * slab_width, 0.5 * slab_width))]
    p = jnp.where(comp == 0, xs[0], jnp.where(comp == 1, xs[1], xs[2]))
    norm = xs[0] * xs[0] + xs[1] * xs[1] + xs[2] * xs[2]
    if own:
        row = (t - tpc) * TILE + lax.broadcasted_iota(jnp.int32, (8, TILE), 1)
        far = jnp.where(row < count, norm, 4096.0)
    else:
        far = norm
    high, middle, low = split3(p)
    fh, fm, fl = split3(far)
    last, top = comp == 3, sub < 4
    a0 = jnp.where(last, jnp.where(top, fh, fm), high)
    a1 = jnp.where(last, jnp.where(top, fl, 1.0), middle)
    a2 = jnp.where(last, 1.0, jnp.where(top, low, high))
    left = jnp.concatenate([a0, a1, a2, jnp.zeros((8, TILE), F32)], axis=0)
    lefts[t] = left.astype(BF16)
    lefts_t[t] = left.T.astype(BF16)
    if own:
        nh, nm, nl = split3(norm + 1.0 / reach_sq)
        h2, m2, l2 = -2.0 * high, -2.0 * middle, -2.0 * low
        b0 = jnp.where(last, 1.0, jnp.where(top, h2, m2))
        b1 = jnp.where(last, jnp.where(top, 1.0, nh), jnp.where(top, h2, m2))
        b2 = jnp.where(last, jnp.where(top, nm, nl), jnp.where(top, h2, l2))
        right = jnp.concatenate([b0, b1, b2, jnp.zeros((8, TILE), F32)], axis=0)
        rights[t - tpc] = right.astype(BF16)
        places[t - tpc] = p


def prepare_chunk(m, own, *refs):
    tpc = refs[0].shape[2]
    for n in range(tpc):
        prepare_tile(m, n, own, *refs)


def quotients(i, buf, neighbours, lefts_t, rights):
    right = rights[i]
    for n in range(neighbours.shape[0]):
        buf[n * TILE : (n + 1) * TILE, :] = jnp.dot(
            lefts_t[neighbours[n, i]], right, preferred_element_type=F32
        )


def tile_force(i, buf, neighbours, lefts, places, force, count):
    tpc = force.shape[2]
    total = jnp.zeros((KROWS, TILE), F32)
    for n in range(0, neighbours.shape[0], 2):
        q = buf[n * TILE : (n + 2) * TILE, :]
        r = 1.0 / q
        r2 = r * r
        d = jnp.maximum(r2 - r, 0.0)
        f = ((d * d) * (r2 * r - 0.5 * reach_sq**3)).astype(BF16)
        x = jnp.concatenate([lefts[neighbours[n, i]], lefts[neighbours[n + 1, i]]], axis=1)
        total = total + jnp.dot(x, f, preferred_element_type=F32)
    moved = total[0:8] + total[8:16] + total[16:24]
    row = i * TILE + lax.broadcasted_iota(jnp.int32, (8, TILE), 1)
    beads = lax.axis_size("bead")
    scale = jnp.where(row < count, 48.0 / 256.0 / reach_sq**5 / shrink / beads, 0.0)
    result = (places[i] * total[15:16] - moved) * scale
    for c in range(3):
        force[i // tpc, c, pl.ds(i % tpc, 1), :] = result[c : c + 1]


def forces(neighbours, count, lefts, lefts_t, rights, places, even, odd, force):
    tiles = rights.shape[0]
    quotients(0, even, neighbours, lefts_t, rights)

    def pair(k, carry):
        i = 2 * k
        quotients(i + 1, odd, neighbours, lefts_t, rights)
        tile_force(i, even, neighbours, lefts, places, force, count)
        after = jnp.minimum(i + 2, tiles - 1)
        quotients(after, even, neighbours, lefts_t, rights)
        tile_force(i + 1, odd, neighbours, lefts, places, force, count)
        return carry

    lax.fori_loop(0, tiles // 2, pair, 0)


def leapfrog(section, momentum, full, new_section, new_momentum):
    level = level_rows(lax.axis_index("bead"))
    safe = jnp.maximum(level, 1.0)
    mass = jnp.where(level > 0, (level + 1.0) / safe, 1.0)
    spring = jnp.where(level > 0, omega_sq * mass, 0.0)
    step = time_step / 3.0
    push = 0.5 * step * spring
    drift = step / mass
    for z in range(NZ):
        p = momentum[:, z] + (0.5 * time_step) * full[z]
        u = section[:, z]
        for turn in range(3):
            p = p - push * u
            u = u + drift * p
            p = p - push * u
        new_section[:, z] = u
        new_momentum[:, z] = p


def kernel(
    counts, neighbours, border, section_in, momentum_in, section_out, momentum_out,
    section, momentum, result_u, result_p, land, edge, force, full,
    lefts, lefts_t, rights, places, even, odd,
    r1f, t2f, r2f, pxf, r1b, t2b, r2b, pxb,
    load_sem, store_sem, halo_send, halo_recv, *sems,
):
    slab, slabs = lax.axis_index("slab"), lax.axis_size("slab")
    loads = [
        pltpu.make_async_copy(section_in, section, load_sem.at[0]),
        pltpu.make_async_copy(momentum_in, momentum, load_sem.at[1]),
    ]
    for load in loads:
        load.start()
    barrier = pltpu.get_barrier_semaphore()
    greeted = partners()
    for device in greeted:
        pl.semaphore_signal(barrier, inc=1, device_id=device, device_id_type=MESH)
    pl.semaphore_wait(barrier, len(greeted))
    for load in loads:
        load.wait()
    started = forward_scan(section, r1f, t2f, r2f, pxf, land, sems[:6])
    gather_rows(land, border, edge)
    halos = halo_exchange(edge, land, halo_send, halo_recv)
    count = counts[0]
    box = slab_width * slabs
    centre = (slab.astype(F32) + 0.5) * slab_width
    refs = (land, places, lefts, lefts_t, rights)

    def own_chunk(m, carry):
        prepare_chunk(m, True, *refs, centre, count)
        return carry

    lax.fori_loop(1, NZ + 1, own_chunk, 0)
    for copy in halos:
        copy.wait_recv()
    prepare_chunk(0, False, *refs, centre + jnp.where(slab == 0, box, 0.0), count)
    prepare_chunk(NZ + 1, False, *refs, centre - jnp.where(slab == slabs - 1, box, 0.0), count)
    forces(neighbours, count, lefts, lefts_t, rights, places, even, odd, force)
    started += halos + backward_scan(force, r1b, t2b, r2b, pxb, full, sems[6:])
    leapfrog(section, momentum, full, result_u, result_p)
    stores = [
        pltpu.make_async_copy(result_u, section_out, store_sem.at[0]),
        pltpu.make_async_copy(result_p, momentum_out, store_sem.at[1]),
    ]
    for store in stores:
        store.start()
    for copy in started:
        copy.wait_send()
    for store in stores:
        store.wait()


def step(section, momentum, neighbours, border_rows, counts):
    shape = section.shape
    listed = neighbours.shape[2]
    tiles = shape[2] // TILE
    tpc = tiles // NZ
    dense = (3, NZ, tpc, TILE)
    ext_tiles = (NZ + 2) * tpc
    chunk = (3, tpc, TILE)
    anywhere = pl.BlockSpec(memory_space=pl.ANY)
    scan_buffers = [
        pltpu.VMEM((NZ * NY, *chunk), F32),
        pltpu.VMEM((2, *chunk), F32),
        pltpu.VMEM((NX, 2, *chunk), F32),
        pltpu.VMEM((NZ, *chunk), F32),
    ]
    scan_sems = [DMA((NZ * NY,))] * 2 + [DMA((NX,))] * 2 + [DMA((NZ,))] * 2
    like = jax.ShapeDtypeStruct(dense, F32)
    u, p = pl.pallas_call(
        kernel,
        out_shape=(like, like),
        in_specs=[
            pl.BlockSpec(memory_space=pltpu.SMEM),
            pl.BlockSpec(memory_space=pltpu.SMEM),
            pl.BlockSpec(memory_space=pltpu.VMEM),
            anywhere,
            anywhere,
        ],
        out_specs=(anywhere, anywhere),
        scratch_shapes=[pltpu.VMEM(dense, F32)] * 4
        + [
            pltpu.VMEM((NZ + 2, *chunk), F32),
            pltpu.VMEM((2, *chunk), F32),
            pltpu.VMEM((NZ, *chunk), F32),
            pltpu.VMEM((NZ, *chunk), F32),
            pltpu.VMEM((ext_tiles, KROWS, TILE), BF16),
            pltpu.VMEM((ext_tiles, TILE, KROWS), BF16),
            pltpu.VMEM((tiles, KROWS, TILE), BF16),
            pltpu.VMEM((tiles, 8, TILE), F32),
            pltpu.VMEM((listed * TILE, TILE), F32),
            pltpu.VMEM((listed * TILE, TILE), F32),
        ]
        + scan_buffers * 2
        + [DMA((2,))] * 4
        + scan_sems * 2,
        compiler_params=pltpu.CompilerParams(collective_id=0, has_side_effects=True),
        name="path_step",
    )(
        counts,
        neighbours.transpose(0, 2, 1).reshape(listed, tiles),
        border_rows.reshape(border_rows.shape[1:]),
        section.reshape(dense),
        momentum.reshape(dense),
    )
    return u.reshape(shape), p.reshape(shape)


def solution(mesh):
    return jax.shard_map(
        step,
        mesh=mesh,
        in_specs=(
            P("bead", None, "slab"),
            P("bead", None, "slab"),
            P("slab", None, None),
            P("slab", None, None),
            P("slab"),
        ),
        out_specs=(P("bead", None, "slab"), P("bead", None, "slab")),
        check_vma=False,
    )
```

```python
import functools
import math

import jax
import jax.numpy as jnp
from jax import lax
from jax.experimental import pallas as pl
from jax.experimental.pallas import tpu as pltpu
from jax.sharding import PartitionSpec as P

MESH = pl.DeviceIdType.MESH
time_step = 0.1
omega_sq = 4.0
slab_width = 3.0
reach_sq = 17.0
shrink = 1.0 / math.sqrt(reach_sq)
NX, NZ, NY = 4, 8, 2
TILE = 128
KROWS = 32
F32 = jnp.float32
BF16 = jnp.bfloat16
DMA = pltpu.SemaphoreType.DMA


def place():
    bead = lax.axis_index("bead")
    return bead // (NZ * NY), (bead // NY) % NZ, bead % NY


def bead_of(x, z, y):
    return (x * NZ + z) * NY + y


def to_bead(bead):
    return (bead, lax.axis_index("slab"))


def group_steps():
    return [(dz, dy) for dz in range(NZ) for dy in range(NY) if dz or dy]


def partners():
    x, z, y = place()
    slab, slabs = lax.axis_index("slab"), lax.axis_size("slab")
    found = [to_bead(bead_of(x, (z + dz) % NZ, (y + dy) % NY)) for dz, dy in group_steps()]
    found += [to_bead(bead_of((x + dx) % NX, z, y)) for dx in range(1, NX)]
    for ds in (1, slabs - 1):
        found += [(bead_of(x, (z + dz) % NZ, y), (slab + ds) % slabs) for dz in range(NZ)]
    return found


def send(src, dst, send_sem, recv_sem, device):
    copy = pltpu.make_async_remote_copy(
        src_ref=src,
        dst_ref=dst,
        send_sem=send_sem,
        recv_sem=recv_sem,
        device_id=device,
        device_id_type=MESH,
    )
    copy.start()
    return copy


def group_copy(src, r1, send_sem, recv_sem, dz, dy):
    x, z, y = place()
    slot = dz * NY + dy
    return pltpu.make_async_remote_copy(
        src_ref=src,
        dst_ref=r1.at[slot],
        send_sem=send_sem.at[slot],
        recv_sem=recv_sem.at[slot],
        device_id=to_bead(bead_of(x, (z + dz) % NZ, (y + dy) % NY)),
        device_id_type=MESH,
    )


def exchange_x(t2, r2, send_sem, recv_sem):
    x, z, y = place()
    return [
        send(t2, r2.at[dx], send_sem.at[dx], recv_sem.at[dx], to_bead(bead_of((x + dx) % NX, z, y)))
        for dx in range(1, NX)
    ]


def level_rows(bead):
    return jnp.full((1, TILE), bead.astype(F32), F32)


def slot_from(zs, ys):
    x, z, y = place()
    return ((z + (NZ - zs)) % NZ) * NY + (y + (NY - ys)) % NY


def near_first():
    return sorted(range(1, NZ), key=lambda dz: min(dz, NZ - dz))


def forward_scan(raw, r1, t2, r2, px, land, halo, sems):
    s1, q1, s2, q2, s3, q3, s4, q4 = sems
    x, z, y = place()
    slab, slabs = lax.axis_index("slab"), lax.axis_size("slab")
    sent = [group_copy(raw.at[(z + dz) % NZ], r1, s1, q1, dz, dy) for dz, dy in group_steps()]
    for copy in reversed(sent):
        copy.start()
    r1[0] = raw[z]
    for copy in sent:
        copy.wait_recv()
    total = jnp.zeros(r1.shape[1:], F32)
    for zs in reversed(range(NZ)):
        kept = None
        for ys in reversed(range(NY)):
            level = level_rows(bead_of(x, zs, ys))
            inverse = jnp.where(level > 0, 1.0 / jnp.maximum(level, 1.0), 0.0)
            total = total + r1[slot_from(zs, ys)] * inverse
            kept = total if kept is None else jnp.where(y == ys, total, kept)
        px[zs] = kept
    first = r1[slot_from(0, 0)]
    t2[0] = total
    t2[1] = first
    swapped = exchange_x(t2, r2, s2, q2)
    for copy in swapped:
        copy.wait_recv()
    base = jnp.zeros(r1.shape[1:], F32)
    for dx in range(1, NX):
        xs = (x + (NX - dx)) % NX
        base = base + jnp.where(xs > x, r2[dx, 0], 0.0)
        first = jnp.where(xs == 0, r2[dx, 1], first)
    beside = (slab + 1 + (slabs - 2) * (z // (NZ // 2))) % slabs
    returned, edges = [], []
    for dz in near_first()[::-1] + [0]:
        tz = (z + dz) % NZ
        bead = bead_of(x, tz, y)
        places = first + level_rows(bead) * (px[tz] + base)
        px[tz] = places
        edges.append(send(px.at[tz, 8:16], halo.at[z], s4.at[dz], q4.at[dz], (bead, beside)))
        if dz:
            returned.append(send(px.at[tz], land.at[z], s3.at[dz], q3.at[dz], to_bead(bead)))
        else:
            land[z] = places
    return sent + swapped, returned[::-1], edges[::-1]


def backward_scan(r1, t2, r2, px, full, arriving, sems):
    s2, q2, s3, q3 = sems
    x, z, y = place()
    for copy in arriving:
        copy.wait_recv()
    total = jnp.zeros(r1.shape[1:], F32)
    plain = jnp.zeros(r1.shape[1:], F32)
    for zs in range(NZ):
        kept = None
        for ys in range(NY):
            one = r1[slot_from(zs, ys)]
            plain = plain + one
            total = total + one * level_rows(bead_of(x, zs, ys))
            kept = total if kept is None else jnp.where(y == ys, total, kept)
        px[zs] = kept
    t2[0] = total
    t2[1] = plain
    swapped = exchange_x(t2, r2, s2, q2)
    for copy in swapped:
        copy.wait_recv()
    base = jnp.zeros(r1.shape[1:], F32)
    for dx in range(1, NX):
        xs = (x + (NX - dx)) % NX
        base = base + jnp.where(xs < x, r2[dx, 0], 0.0)
        plain = plain + r2[dx, 1]
    returned = []
    for dz in near_first()[::-1] + [0]:
        tz = (z + dz) % NZ
        bead = bead_of(x, tz, y)
        level = level_rows(bead)
        inverse = 1.0 / jnp.maximum(level, 1.0)
        result = jnp.where(level > 0, (px[tz] + base) * inverse, plain)
        if dz:
            px[tz] = result
            returned.append(send(px.at[tz], full.at[z], s3.at[dz], q3.at[dz], to_bead(bead)))
        else:
            full[z] = result
    return swapped, returned[::-1]


def pack_chunks(section, border, raw):
    tpc = section.shape[2]
    sub = lax.broadcasted_iota(jnp.int32, (8, TILE), 0)
    blocks = NZ // 2 * tpc // 8
    for z in range(NZ):
        for c in range(3):
            raw[z, c * tpc : (c + 1) * tpc, :] = section[c, z]
    pieces = []
    for c in range(3):
        for b in range(blocks):
            rows = [section[c, b * (8 // tpc) + m] for m in range(8 // tpc)]
            pieces.append(jnp.concatenate(rows, axis=0))
    half = NZ // 2
    for z in range(NZ):
        k, n = z // half, z % half
        index = jnp.broadcast_to(border[k : k + 1, n * TILE : (n + 1) * TILE], (8, TILE))
        lane, block = index % TILE, index // TILE
        rows = []
        for c in range(3):
            out = jnp.zeros((8, TILE), F32)
            for b in range(blocks):
                taken = jnp.take_along_axis(
                    pieces[c * blocks + b], lane, axis=1, mode="promise_in_bounds"
                )
                out = jnp.where(block == b * 8 + sub, taken, out)
            rows.append(jnp.sum(out, axis=0, keepdims=True))
        raw[z, 12:16, :] = jnp.concatenate(rows + [jnp.zeros((1, TILE), F32)], axis=0)


def split3(value):
    high = value.astype(BF16).astype(F32)
    rest = value - high
    middle = rest.astype(BF16).astype(F32)
    return high, middle, rest - middle


def prepare_tile(t, rows, shift, own, lefts, lefts_t, rights, places, row, count):
    sub = lax.broadcasted_iota(jnp.int32, (8, TILE), 0)
    comp = sub % 4
    xs = [jnp.broadcast_to(v, (8, TILE)) for v in rows]
    xs = [(v - w) * shrink for v, w in zip(xs, (shift, 0.5 * slab_width, 0.5 * slab_width))]
    p = jnp.where(comp == 0, xs[0], jnp.where(comp == 1, xs[1], xs[2]))
    norm = xs[0] * xs[0] + xs[1] * xs[1] + xs[2] * xs[2]
    far = norm
    if own is not None:
        place_in = row + lax.broadcasted_iota(jnp.int32, (8, TILE), 1)
        far = jnp.where(place_in < count, norm, 4096.0)
    high, middle, low = split3(p)
    fh, fm, fl = split3(far)
    last, top = comp == 3, sub < 4
    a0 = jnp.where(last, jnp.where(top, fh, fm), high)
    a1 = jnp.where(last, jnp.where(top, fl, 1.0), middle)
    a2 = jnp.where(last, 1.0, jnp.where(top, low, high))
    left = jnp.concatenate([a0, a1, a2, jnp.zeros((8, TILE), F32)], axis=0)
    lefts[t] = left.astype(BF16)
    lefts_t[t] = left.T.astype(BF16)
    if own is not None:
        nh, nm, nl = split3(norm + 1.0 / reach_sq)
        h2, m2, l2 = -2.0 * high, -2.0 * middle, -2.0 * low
        b0 = jnp.where(last, 1.0, jnp.where(top, h2, m2))
        b1 = jnp.where(last, jnp.where(top, 1.0, nh), jnp.where(top, h2, m2))
        b2 = jnp.where(last, jnp.where(top, nm, nl), jnp.where(top, h2, l2))
        right = jnp.concatenate([b0, b1, b2, jnp.zeros((8, TILE), F32)], axis=0)
        rights[own] = right.astype(BF16)
        places[own] = p


def prepare_own(z, land, centre, count, *refs):
    half, tpc = NZ // 2, refs[2].shape[0] // NZ
    for n in range(tpc):
        rows = [land[z, c * tpc + n : c * tpc + n + 1, :] for c in range(3)]
        i = z * tpc + n
        prepare_tile(half + i, rows, centre, i, *refs, i * TILE, count)


def prepare_halo(z, halo, shifts, *refs):
    half, tiles = NZ // 2, refs[2].shape[0]
    upper = z // half
    rows = [halo[z, 4 + c : 5 + c, :] for c in range(3)]
    shift = jnp.where(upper == 0, shifts[0], shifts[1])
    prepare_tile(z + upper * tiles, rows, shift, None, *refs, 0, 0)


def quotients(i, buf, neighbours, lefts_t, rights):
    right = rights[i]
    for n in range(neighbours.shape[0]):
        buf[n * TILE : (n + 1) * TILE, :] = jnp.dot(
            lefts_t[neighbours[n, i]], right, preferred_element_type=F32
        )


def tile_force(i, zc, n, buf, neighbours, lefts, places, force, count):
    total = jnp.zeros((KROWS, TILE), F32)
    for k in range(0, neighbours.shape[0], 2):
        q = buf[k * TILE : (k + 2) * TILE, :]
        r = 1.0 / q
        r2 = r * r
        d = jnp.maximum(r2 - r, 0.0)
        f = ((d * d) * (r2 * r - 0.5 * reach_sq**3)).astype(BF16)
        x = jnp.concatenate([lefts[neighbours[k, i]], lefts[neighbours[k + 1, i]]], axis=1)
        total = total + jnp.dot(x, f, preferred_element_type=F32)
    moved = total[0:8] + total[8:16] + total[16:24]
    row = i * TILE + lax.broadcasted_iota(jnp.int32, (8, TILE), 1)
    beads = lax.axis_size("bead")
    scale = jnp.where(row < count, 48.0 / 256.0 / reach_sq**5 / shrink / beads, 0.0)
    result = (places[i] * total[15:16] - moved) * scale
    for c in range(3):
        force[zc, 4 * c + n : 4 * c + n + 1, :] = result[c : c + 1]


def forces(neighbours, count, lefts, lefts_t, rights, places, even, odd, force, r1, send_sem, recv_sem):
    x, z, y = place()
    tpc = rights.shape[0] // NZ
    half = NZ // 2
    bufs = (even, odd)

    def offset(c):
        return half + (c // 2) * (1 - c % 2) - ((c + 1) // 2) * (c % 2)

    quotients(((z + half) % NZ) * tpc, even, neighbours, lefts_t, rights)

    def chunk(c, carry):
        dz = offset(c)
        zc = (z + dz) % NZ
        after = (z + offset(jnp.minimum(c + 1, NZ - 1))) % NZ
        for n in range(tpc):
            following = zc * tpc + n + 1 if n + 1 < tpc else after * tpc
            quotients(following, bufs[(n + 1) % 2], neighbours, lefts_t, rights)
            tile_force(zc * tpc + n, zc, n, bufs[n % 2], neighbours, lefts, places, force, count)
        group_copy(force.at[zc], r1, send_sem, recv_sem, dz, 1).start()

        @pl.when(c < NZ - 1)
        def _():
            group_copy(force.at[zc], r1, send_sem, recv_sem, dz, 0).start()

        return carry

    lax.fori_loop(0, NZ, chunk, 0)
    r1[0] = force[z]
    return [group_copy(force.at[(z + dz) % NZ], r1, send_sem, recv_sem, dz, dy) for dz, dy in group_steps()]


def kernel(
    counts, neighbours, border, section_in, out,
    section, result, raw, land, halo, force, full,
    lefts, lefts_t, rights, places, even, odd,
    r1f, t2f, r2f, pxf, r1b, t2b, r2b, pxb,
    load_sem, store_sem, *sems,
):
    x, z, y = place()
    slab, slabs = lax.axis_index("slab"), lax.axis_size("slab")
    load = pltpu.make_async_copy(section_in, section, load_sem.at[0])
    load.start()
    barrier = pltpu.get_barrier_semaphore()
    greeted = partners()
    for device in greeted:
        pl.semaphore_signal(barrier, inc=1, device_id=device, device_id_type=MESH)
    force[...] = jnp.zeros_like(force)
    load.wait()
    pack_chunks(section, border, raw)
    pl.semaphore_wait(barrier, len(greeted))
    started, returned, edges = forward_scan(raw, r1f, t2f, r2f, pxf, land, halo, sems[:8])
    count = counts[0]
    box = slab_width * slabs
    centre = (slab.astype(F32) + 0.5) * slab_width
    shifts = (
        centre + jnp.where(slab == 0, box, 0.0),
        centre - jnp.where(slab == slabs - 1, box, 0.0),
    )
    refs = (lefts, lefts_t, rights, places)
    prepare_own(z, land, centre, count, *refs)
    for copy, edge, dz in zip([None] + returned, edges, [0] + near_first()):
        source = (z + (NZ - dz)) % NZ
        if copy is not None:
            copy.wait_recv()
            prepare_own(source, land, centre, count, *refs)
        edge.wait_recv()
        prepare_halo(source, halo, shifts, *refs)
    arriving = forces(
        neighbours, count, lefts, lefts_t, rights, places, even, odd, force, r1b, *sems[8:10]
    )
    swapped, back = backward_scan(r1b, t2b, r2b, pxb, full, arriving, sems[10:])
    tpc = result.shape[2]
    for copy, dz in zip([None] + back, [0] + near_first()):
        source = (z + (NZ - dz)) % NZ
        if copy is not None:
            copy.wait_recv()
        for c in range(3):
            result[c, source] = full[source, c * tpc : (c + 1) * tpc, :]
    store = pltpu.make_async_copy(result, out, store_sem.at[0])
    store.start()
    for copy in started + returned + edges + arriving + swapped + back:
        copy.wait_send()
    store.wait()


def leapfrog(section, momentum, section_force):
    level = lax.axis_index("bead").astype(F32)
    safe = jnp.maximum(level, 1.0)
    mass = jnp.where(level > 0, (level + 1.0) / safe, 1.0)
    spring = jnp.where(level > 0, omega_sq * mass, 0.0)
    step = time_step / 3.0
    push = 0.5 * step * spring
    drift = step / mass
    p = momentum + (0.5 * time_step) * section_force
    u = section
    for turn in range(3):
        p = p - push * u
        u = u + drift * p
        p = p - push * u
    return u, p


def step(section, momentum, neighbours, border_rows, counts):
    shape = section.shape
    listed = neighbours.shape[2]
    tiles = shape[2] // TILE
    tpc = tiles // NZ
    dense = (3, NZ, tpc, TILE)
    ext_tiles = tiles + NZ
    chunk = (16, TILE)
    anywhere = pl.BlockSpec(memory_space=pl.ANY)
    vmem = lambda *dims: pltpu.VMEM(dims, F32)
    scan_buffers = [vmem(NZ * NY, *chunk), vmem(2, *chunk), vmem(NX, 2, *chunk), vmem(NZ, *chunk)]
    scan_sems = [DMA((NZ * NY,))] * 2 + [DMA((NX,))] * 2 + [DMA((NZ,))] * 2
    section, momentum = section.reshape(dense), momentum.reshape(dense)
    section_force = pl.pallas_call(
        kernel,
        out_shape=jax.ShapeDtypeStruct(dense, F32),
        in_specs=[
            pl.BlockSpec(memory_space=pltpu.SMEM),
            pl.BlockSpec(memory_space=pltpu.SMEM),
            pl.BlockSpec(memory_space=pltpu.VMEM),
            anywhere,
        ],
        out_specs=anywhere,
        scratch_shapes=[
            vmem(*dense),
            vmem(*dense),
            vmem(NZ, *chunk),
            vmem(NZ, *chunk),
            vmem(NZ, 8, TILE),
            vmem(NZ, *chunk),
            vmem(NZ, *chunk),
            pltpu.VMEM((ext_tiles, KROWS, TILE), BF16),
            pltpu.VMEM((ext_tiles, TILE, KROWS), BF16),
            pltpu.VMEM((tiles, KROWS, TILE), BF16),
            vmem(tiles, 8, TILE),
            vmem(listed * TILE, TILE),
            vmem(listed * TILE, TILE),
        ]
        + scan_buffers * 2
        + [DMA((1,))] * 2
        + scan_sems
        + [DMA((NZ,))] * 2
        + scan_sems,
        compiler_params=pltpu.CompilerParams(
            collective_id=0, has_side_effects=True, vmem_limit_bytes=24 * 2**20
        ),
        name="path_step",
    )(
        counts,
        neighbours.transpose(0, 2, 1).reshape(listed, tiles),
        border_rows.reshape(border_rows.shape[1:]),
        section,
    )
    u, p = leapfrog(section, momentum, section_force)
    return u.reshape(shape), p.reshape(shape)


def solution(mesh):
    return jax.shard_map(
        step,
        mesh=mesh,
        in_specs=(
            P("bead", None, "slab"),
            P("bead", None, "slab"),
            P("slab", None, None),
            P("slab", None, None),
            P("slab"),
        ),
        out_specs=(P("bead", None, "slab"), P("bead", None, "slab")),
        check_vma=False,
    )
```

```python
import functools
import math

import jax
import jax.numpy as jnp
from jax import lax
from jax.experimental import pallas as pl
from jax.experimental.pallas import tpu as pltpu
from jax.sharding import PartitionSpec as P

MESH = pl.DeviceIdType.MESH
time_step = 0.1
omega_sq = 4.0
slab_width = 3.0
reach_sq = 17.0
shrink = 1.0 / math.sqrt(reach_sq)
NX, NZ, NY = 4, 8, 2
TILE = 128
KROWS = 32
F32 = jnp.float32
BF16 = jnp.bfloat16
DMA = pltpu.SemaphoreType.DMA


def place():
    bead = lax.axis_index("bead")
    return bead // (NZ * NY), (bead // NY) % NZ, bead % NY


def bead_of(x, z, y):
    return (x * NZ + z) * NY + y


def to_bead(bead):
    return (bead, lax.axis_index("slab"))


def group_steps():
    return [(dz, dy) for dz in range(NZ) for dy in range(NY) if dz or dy]


def partners():
    x, z, y = place()
    slab, slabs = lax.axis_index("slab"), lax.axis_size("slab")
    found = [to_bead(bead_of(x, (z + dz) % NZ, (y + dy) % NY)) for dz, dy in group_steps()]
    found += [to_bead(bead_of((x + dx) % NX, z, y)) for dx in range(1, NX)]
    for ds in (1, slabs - 1):
        found += [(bead_of(x, (z + dz) % NZ, y), (slab + ds) % slabs) for dz in range(NZ)]
    return found


def send(src, dst, send_sem, recv_sem, device):
    copy = pltpu.make_async_remote_copy(
        src_ref=src,
        dst_ref=dst,
        send_sem=send_sem,
        recv_sem=recv_sem,
        device_id=device,
        device_id_type=MESH,
    )
    copy.start()
    return copy


def group_copy(src, r1, send_sem, recv_sem, dz, dy):
    x, z, y = place()
    slot = dz * NY + dy
    return pltpu.make_async_remote_copy(
        src_ref=src,
        dst_ref=r1.at[slot],
        send_sem=send_sem.at[slot],
        recv_sem=recv_sem.at[slot],
        device_id=to_bead(bead_of(x, (z + dz) % NZ, (y + dy) % NY)),
        device_id_type=MESH,
    )


def exchange_x(t2, r2, send_sem, recv_sem):
    x, z, y = place()
    return [
        send(t2, r2.at[dx], send_sem.at[dx], recv_sem.at[dx], to_bead(bead_of((x + dx) % NX, z, y)))
        for dx in range(1, NX)
    ]


def level_rows(bead):
    return jnp.full((1, TILE), bead.astype(F32), F32)


def slot_from(zs, ys):
    x, z, y = place()
    return ((z + (NZ - zs)) % NZ) * NY + (y + (NY - ys)) % NY


def near_first():
    return sorted(range(1, NZ), key=lambda dz: min(dz, NZ - dz))


def forward_scan(raw, r1, t2, r2, px, land, halo, sems):
    s1, q1, s2, q2, s3, q3, s4, q4 = sems
    x, z, y = place()
    slab, slabs = lax.axis_index("slab"), lax.axis_size("slab")
    sent = [group_copy(raw.at[(z + dz) % NZ], r1, s1, q1, dz, dy) for dz, dy in group_steps()]
    for copy in reversed(sent):
        copy.start()
    r1[0] = raw[z]
    for copy in sent:
        copy.wait_recv()
    total = jnp.zeros(r1.shape[1:], F32)
    for zs in reversed(range(NZ)):
        kept = None
        for ys in reversed(range(NY)):
            level = level_rows(bead_of(x, zs, ys))
            inverse = jnp.where(level > 0, 1.0 / jnp.maximum(level, 1.0), 0.0)
            total = total + r1[slot_from(zs, ys)] * inverse
            kept = total if kept is None else jnp.where(y == ys, total, kept)
        px[zs] = kept
    first = r1[slot_from(0, 0)]
    t2[0] = total
    t2[1] = first
    swapped = exchange_x(t2, r2, s2, q2)
    for copy in swapped:
        copy.wait_recv()
    base = jnp.zeros(r1.shape[1:], F32)
    for dx in range(1, NX):
        xs = (x + (NX - dx)) % NX
        base = base + jnp.where(xs > x, r2[dx, 0], 0.0)
        first = jnp.where(xs == 0, r2[dx, 1], first)
    beside = (slab + 1 + (slabs - 2) * (z // (NZ // 2))) % slabs
    returned, edges = [], []
    for dz in near_first()[::-1] + [0]:
        tz = (z + dz) % NZ
        bead = bead_of(x, tz, y)
        places = first + level_rows(bead) * (px[tz] + base)
        px[tz] = places
        edges.append(send(px.at[tz, 8:16], halo.at[z], s4.at[dz], q4.at[dz], (bead, beside)))
        if dz:
            returned.append(send(px.at[tz], land.at[z], s3.at[dz], q3.at[dz], to_bead(bead)))
        else:
            land[z] = places
    return sent + swapped, returned[::-1], edges[::-1]


def backward_scan(r1, t2, r2, px, full, arriving, sems):
    s2, q2, s3, q3 = sems
    x, z, y = place()
    for copy in arriving:
        copy.wait_recv()
    total = jnp.zeros(r1.shape[1:], F32)
    plain = jnp.zeros(r1.shape[1:], F32)
    for zs in range(NZ):
        kept = None
        for ys in range(NY):
            one = r1[slot_from(zs, ys)]
            plain = plain + one
            total = total + one * level_rows(bead_of(x, zs, ys))
            kept = total if kept is None else jnp.where(y == ys, total, kept)
        px[zs] = kept
    t2[0] = total
    t2[1] = plain
    swapped = exchange_x(t2, r2, s2, q2)
    for copy in swapped:
        copy.wait_recv()
    base = jnp.zeros(r1.shape[1:], F32)
    for dx in range(1, NX):
        xs = (x + (NX - dx)) % NX
        base = base + jnp.where(xs < x, r2[dx, 0], 0.0)
        plain = plain + r2[dx, 1]
    returned = []
    for dz in near_first()[::-1] + [0]:
        tz = (z + dz) % NZ
        bead = bead_of(x, tz, y)
        level = level_rows(bead)
        inverse = 1.0 / jnp.maximum(level, 1.0)
        result = jnp.where(level > 0, (px[tz] + base) * inverse, plain)
        if dz:
            px[tz] = result
            returned.append(send(px.at[tz], full.at[z], s3.at[dz], q3.at[dz], to_bead(bead)))
        else:
            full[z] = result
    return swapped, returned[::-1]


def pack_chunks(section, border, raw):
    tpc = section.shape[2]
    sub = lax.broadcasted_iota(jnp.int32, (8, TILE), 0)
    blocks = NZ // 2 * tpc // 8
    for z in range(NZ):
        for c in range(3):
            raw[z, c * tpc : (c + 1) * tpc, :] = section[c, z]
    pieces = []
    for c in range(3):
        for b in range(blocks):
            rows = [section[c, b * (8 // tpc) + m] for m in range(8 // tpc)]
            pieces.append(jnp.concatenate(rows, axis=0))
    half = NZ // 2
    for z in range(NZ):
        k, n = z // half, z % half
        index = jnp.broadcast_to(border[k : k + 1, n * TILE : (n + 1) * TILE], (8, TILE))
        lane, block = index % TILE, index // TILE
        rows = []
        for c in range(3):
            out = jnp.zeros((8, TILE), F32)
            for b in range(blocks):
                taken = jnp.take_along_axis(
                    pieces[c * blocks + b], lane, axis=1, mode="promise_in_bounds"
                )
                out = jnp.where(block == b * 8 + sub, taken, out)
            rows.append(jnp.sum(out, axis=0, keepdims=True))
        raw[z, 12:16, :] = jnp.concatenate(rows + [jnp.zeros((1, TILE), F32)], axis=0)


def split3(value):
    high = value.astype(BF16).astype(F32)
    rest = value - high
    middle = rest.astype(BF16).astype(F32)
    return high, middle, rest - middle


def prepare_tile(t, rows, shift, own, lefts, lefts_t, rights, places, row, count):
    sub = lax.broadcasted_iota(jnp.int32, (8, TILE), 0)
    comp = sub % 4
    xs = [jnp.broadcast_to(v, (8, TILE)) for v in rows]
    xs = [(v - w) * shrink for v, w in zip(xs, (shift, 0.5 * slab_width, 0.5 * slab_width))]
    p = jnp.where(comp == 0, xs[0], jnp.where(comp == 1, xs[1], xs[2]))
    norm = xs[0] * xs[0] + xs[1] * xs[1] + xs[2] * xs[2]
    far = norm
    if own is not None:
        place_in = row + lax.broadcasted_iota(jnp.int32, (8, TILE), 1)
        far = jnp.where(place_in < count, norm, 4096.0)
    high, middle, low = split3(p)
    fh, fm, fl = split3(far)
    last, top = comp == 3, sub < 4
    a0 = jnp.where(last, jnp.where(top, fh, fm), high)
    a1 = jnp.where(last, jnp.where(top, fl, 1.0), middle)
    a2 = jnp.where(last, 1.0, jnp.where(top, low, high))
    left = jnp.concatenate([a0, a1, a2, jnp.zeros((8, TILE), F32)], axis=0)
    lefts[t] = left.astype(BF16)
    lefts_t[t] = left.T.astype(BF16)
    if own is not None:
        nh, nm, nl = split3(norm + 1.0 / reach_sq)
        h2, m2, l2 = -2.0 * high, -2.0 * middle, -2.0 * low
        b0 = jnp.where(last, 1.0, jnp.where(top, h2, m2))
        b1 = jnp.where(last, jnp.where(top, 1.0, nh), jnp.where(top, h2, m2))
        b2 = jnp.where(last, jnp.where(top, nm, nl), jnp.where(top, h2, l2))
        right = jnp.concatenate([b0, b1, b2, jnp.zeros((8, TILE), F32)], axis=0)
        rights[own] = right.astype(BF16)
        places[own] = p


def prepare_own(z, land, centre, count, *refs):
    half, tpc = NZ // 2, refs[2].shape[0] // NZ
    for n in range(tpc):
        rows = [land[z, c * tpc + n : c * tpc + n + 1, :] for c in range(3)]
        i = z * tpc + n
        prepare_tile(half + i, rows, centre, i, *refs, i * TILE, count)


def prepare_halo(z, halo, shifts, *refs):
    half, tiles = NZ // 2, refs[2].shape[0]
    upper = z // half
    rows = [halo[z, 4 + c : 5 + c, :] for c in range(3)]
    shift = jnp.where(upper == 0, shifts[0], shifts[1])
    prepare_tile(z + upper * tiles, rows, shift, None, *refs, 0, 0)


def quotients(i, buf, neighbours, lefts_t, rights):
    right = rights[i]
    for n in range(neighbours.shape[0]):
        buf[n * TILE : (n + 1) * TILE, :] = jnp.dot(
            lefts_t[neighbours[n, i]], right, preferred_element_type=F32
        )


def tile_force(i, zc, n, buf, neighbours, lefts, places, force, count):
    total = jnp.zeros((KROWS, TILE), F32)
    for k in range(0, neighbours.shape[0], 2):
        q = buf[k * TILE : (k + 2) * TILE, :]
        r = 1.0 / q
        r2 = r * r
        d = jnp.maximum(r2 - r, 0.0)
        f = ((d * d) * (r2 * r - 0.5 * reach_sq**3)).astype(BF16)
        x = jnp.concatenate([lefts[neighbours[k, i]], lefts[neighbours[k + 1, i]]], axis=1)
        total = total + jnp.dot(x, f, preferred_element_type=F32)
    moved = total[0:8] + total[8:16] + total[16:24]
    row = i * TILE + lax.broadcasted_iota(jnp.int32, (8, TILE), 1)
    beads = lax.axis_size("bead")
    scale = jnp.where(row < count, 48.0 / 256.0 / reach_sq**5 / shrink / beads, 0.0)
    result = (places[i] * total[15:16] - moved) * scale
    for c in range(3):
        force[zc, 4 * c + n : 4 * c + n + 1, :] = result[c : c + 1]


def forces(neighbours, count, lefts, lefts_t, rights, places, even, odd, force, r1, send_sem, recv_sem):
    x, z, y = place()
    tpc = rights.shape[0] // NZ
    half = NZ // 2
    bufs = (even, odd)

    def offset(c):
        return half + (c // 2) * (1 - c % 2) - ((c + 1) // 2) * (c % 2)

    quotients(((z + half) % NZ) * tpc, even, neighbours, lefts_t, rights)

    def chunk(c, carry):
        dz = offset(c)
        zc = (z + dz) % NZ
        after = (z + offset(jnp.minimum(c + 1, NZ - 1))) % NZ
        for n in range(tpc):
            following = zc * tpc + n + 1 if n + 1 < tpc else after * tpc
            quotients(following, bufs[(n + 1) % 2], neighbours, lefts_t, rights)
            tile_force(zc * tpc + n, zc, n, bufs[n % 2], neighbours, lefts, places, force, count)
        group_copy(force.at[zc], r1, send_sem, recv_sem, dz, 1).start()

        @pl.when(c < NZ - 1)
        def _():
            group_copy(force.at[zc], r1, send_sem, recv_sem, dz, 0).start()

        return carry

    lax.fori_loop(0, NZ, chunk, 0)
    r1[0] = force[z]
    return [group_copy(force.at[(z + dz) % NZ], r1, send_sem, recv_sem, dz, dy) for dz, dy in group_steps()]


def kernel(
    counts, neighbours_in, border_in, section_in, out,
    neighbours, border, section, result, raw, land, halo, force, full,
    lefts, lefts_t, rights, places, even, odd,
    r1f, t2f, r2f, pxf, r1b, t2b, r2b, pxb,
    load_sem, store_sem, *sems,
):
    x, z, y = place()
    slab, slabs = lax.axis_index("slab"), lax.axis_size("slab")
    loads = [
        pltpu.make_async_copy(section_in, section, load_sem.at[0]),
        pltpu.make_async_copy(border_in, border, load_sem.at[1]),
        pltpu.make_async_copy(neighbours_in, neighbours, load_sem.at[2]),
    ]
    for load in loads:
        load.start()
    barrier = pltpu.get_barrier_semaphore()
    greeted = partners()
    for device in greeted:
        pl.semaphore_signal(barrier, inc=1, device_id=device, device_id_type=MESH)
    force[...] = jnp.zeros_like(force)
    for load in loads:
        load.wait()
    pack_chunks(section, border, raw)
    pl.semaphore_wait(barrier, len(greeted))
    started, returned, edges = forward_scan(raw, r1f, t2f, r2f, pxf, land, halo, sems[:8])
    count = counts[0]
    box = slab_width * slabs
    centre = (slab.astype(F32) + 0.5) * slab_width
    shifts = (
        centre + jnp.where(slab == 0, box, 0.0),
        centre - jnp.where(slab == slabs - 1, box, 0.0),
    )
    refs = (lefts, lefts_t, rights, places)
    prepare_own(z, land, centre, count, *refs)
    for copy, edge, dz in zip([None] + returned, edges, [0] + near_first()):
        source = (z + (NZ - dz)) % NZ
        if copy is not None:
            copy.wait_recv()
            prepare_own(source, land, centre, count, *refs)
        edge.wait_recv()
        prepare_halo(source, halo, shifts, *refs)
    arriving = forces(
        neighbours, count, lefts, lefts_t, rights, places, even, odd, force, r1b, *sems[8:10]
    )
    swapped, back = backward_scan(r1b, t2b, r2b, pxb, full, arriving, sems[10:])
    tpc = result.shape[2]
    stores = []
    for copy, dz in zip([None] + back, [0] + near_first()):
        source = (z + (NZ - dz)) % NZ
        if copy is not None:
            copy.wait_recv()
        for c in range(3):
            result[c, source] = full[source, c * tpc : (c + 1) * tpc, :]
        store = pltpu.make_async_copy(result.at[:, source], out.at[:, source], store_sem.at[dz])
        store.start()
        stores.append(store)
    for copy in started + returned + edges + arriving + swapped + back:
        copy.wait_send()
    for store in stores:
        store.wait()


def leapfrog(section, momentum, section_force):
    level = lax.axis_index("bead").astype(F32)
    safe = jnp.maximum(level, 1.0)
    mass = jnp.where(level > 0, (level + 1.0) / safe, 1.0)
    spring = jnp.where(level > 0, omega_sq * mass, 0.0)
    step = time_step / 3.0
    push = 0.5 * step * spring
    drift = step / mass
    p = momentum + (0.5 * time_step) * section_force
    u = section
    for turn in range(3):
        p = p - push * u
        u = u + drift * p
        p = p - push * u
    return u, p


def step(section, momentum, neighbours, border_rows, counts):
    shape = section.shape
    listed = neighbours.shape[2]
    tiles = shape[2] // TILE
    tpc = tiles // NZ
    dense = (3, NZ, tpc, TILE)
    ext_tiles = tiles + NZ
    chunk = (16, TILE)
    anywhere = pl.BlockSpec(memory_space=pl.ANY)
    in_hbm = pl.BlockSpec(memory_space=pltpu.HBM)
    hbm = lambda array: pltpu.with_memory_space_constraint(array, pltpu.HBM)
    vmem = lambda *dims: pltpu.VMEM(dims, F32)
    scan_buffers = [vmem(NZ * NY, *chunk), vmem(2, *chunk), vmem(NX, 2, *chunk), vmem(NZ, *chunk)]
    scan_sems = [DMA((NZ * NY,))] * 2 + [DMA((NX,))] * 2 + [DMA((NZ,))] * 2
    section, momentum = section.reshape(dense), momentum.reshape(dense)
    section_force = pl.pallas_call(
        kernel,
        out_shape=jax.ShapeDtypeStruct(dense, F32),
        in_specs=[
            pl.BlockSpec(memory_space=pltpu.SMEM),
            in_hbm,
            in_hbm,
            in_hbm,
        ],
        out_specs=anywhere,
        scratch_shapes=[
            pltpu.SMEM((listed, tiles), jnp.int32),
            pltpu.VMEM(border_rows.shape[1:], jnp.int32),
            vmem(*dense),
            vmem(*dense),
            vmem(NZ, *chunk),
            vmem(NZ, *chunk),
            vmem(NZ, 8, TILE),
            vmem(NZ, *chunk),
            vmem(NZ, *chunk),
            pltpu.VMEM((ext_tiles, KROWS, TILE), BF16),
            pltpu.VMEM((ext_tiles, TILE, KROWS), BF16),
            pltpu.VMEM((tiles, KROWS, TILE), BF16),
            vmem(tiles, 8, TILE),
            vmem(listed * TILE, TILE),
            vmem(listed * TILE, TILE),
        ]
        + scan_buffers * 2
        + [DMA((3,)), DMA((NZ,))]
        + scan_sems
        + [DMA((NZ,))] * 2
        + scan_sems,
        compiler_params=pltpu.CompilerParams(
            collective_id=0, has_side_effects=True, vmem_limit_bytes=24 * 2**20
        ),
        name="path_step",
    )(
        counts,
        hbm(neighbours.transpose(0, 2, 1).reshape(listed, tiles)),
        hbm(border_rows.reshape(border_rows.shape[1:])),
        hbm(section),
    )
    u, p = leapfrog(section, momentum, section_force)
    return u.reshape(shape), p.reshape(shape)


def solution(mesh):
    return jax.shard_map(
        step,
        mesh=mesh,
        in_specs=(
            P("bead", None, "slab"),
            P("bead", None, "slab"),
            P("slab", None, None),
            P("slab", None, None),
            P("slab"),
        ),
        out_specs=(P("bead", None, "slab"), P("bead", None, "slab")),
        check_vma=False,
    )
```

```python
import functools
import math

import jax
import jax.numpy as jnp
from jax import lax
from jax.experimental import pallas as pl
from jax.experimental.pallas import tpu as pltpu
from jax.sharding import PartitionSpec as P

MESH = pl.DeviceIdType.MESH
time_step = 0.1
omega_sq = 4.0
slab_width = 3.0
reach_sq = 17.0
shrink = 1.0 / math.sqrt(reach_sq)
NX, NZ, NY = 4, 8, 2
TILE = 128
KROWS = 32
F32 = jnp.float32
BF16 = jnp.bfloat16
DMA = pltpu.SemaphoreType.DMA


def rem(value, size):
    return lax.rem(value, jnp.int32(size))


def place():
    bead = lax.axis_index("bead")
    return lax.div(bead, jnp.int32(NZ * NY)), rem(lax.div(bead, jnp.int32(NY)), NZ), rem(bead, NY)


def bead_of(x, z, y):
    return (x * NZ + z) * NY + y


def to_bead(bead):
    return (bead, lax.axis_index("slab"))


def group_steps():
    return [(dz, dy) for dz in range(NZ) for dy in range(NY) if dz or dy]


def partners():
    x, z, y = place()
    slab, slabs = lax.axis_index("slab"), lax.axis_size("slab")
    found = [to_bead(bead_of(x, rem(z + dz, NZ), rem(y + dy, NY))) for dz, dy in group_steps()]
    found += [to_bead(bead_of(rem(x + dx, NX), z, y)) for dx in range(1, NX)]
    for ds in (1, slabs - 1):
        found += [(bead_of(x, rem(z + dz, NZ), y), rem(slab + ds, slabs)) for dz in range(NZ)]
    return found


def send(src, dst, send_sem, recv_sem, device):
    copy = pltpu.make_async_remote_copy(
        src_ref=src,
        dst_ref=dst,
        send_sem=send_sem,
        recv_sem=recv_sem,
        device_id=device,
        device_id_type=MESH,
    )
    copy.start()
    return copy


def group_copy(src, r1, send_sem, recv_sem, dz, dy):
    x, z, y = place()
    slot = dz * NY + dy
    return pltpu.make_async_remote_copy(
        src_ref=src,
        dst_ref=r1.at[slot],
        send_sem=send_sem.at[slot],
        recv_sem=recv_sem.at[slot],
        device_id=to_bead(bead_of(x, rem(z + dz, NZ), rem(y + dy, NY))),
        device_id_type=MESH,
    )


def exchange_x(t2, r2, send_sem, recv_sem):
    x, z, y = place()
    return [
        send(t2, r2.at[pl.ds(2 * dx, 2)], send_sem.at[dx], recv_sem.at[dx], to_bead(bead_of(rem(x + dx, NX), z, y)))
        for dx in range(1, NX)
    ]


def level_rows(bead):
    return jnp.full((1, 1, TILE), bead.astype(F32), F32)


def slot_from(zs, ys):
    x, z, y = place()
    return rem(z + (NZ - zs), NZ) * NY + rem(y + (NY - ys), NY)


def near_first():
    return sorted(range(1, NZ), key=lambda dz: min(dz, NZ - dz))


def forward_scan(raw, r1, t2, r2, px, land, halo, sems):
    s1, q1, s2, q2, s3, q3, s4, q4 = sems
    x, z, y = place()
    slab, slabs = lax.axis_index("slab"), lax.axis_size("slab")
    sent = [group_copy(raw.at[rem(z + dz, NZ)], r1, s1, q1, dz, dy) for dz, dy in group_steps()]
    for copy in reversed(sent):
        copy.start()
    r1[0] = raw[z]
    for copy in sent:
        copy.wait_recv()
    total = jnp.zeros(r1.shape[1:], F32)
    for zs in reversed(range(NZ)):
        kept = None
        for ys in reversed(range(NY)):
            one = r1[slot_from(zs, ys)]
            if zs == 0 and ys == 0:
                one = jnp.where(x == 0, 0.0, one)
            total = total + one
            kept = total if kept is None else jnp.where(y == ys, total, kept)
        px[zs] = kept
    first = r1[slot_from(0, 0)]
    t2[0] = total
    t2[1] = first
    swapped = exchange_x(t2, r2, s2, q2)
    for copy in swapped:
        copy.wait_recv()
    base = jnp.zeros(r1.shape[1:], F32)
    for dx in range(1, NX):
        xs = rem(x + (NX - dx), NX)
        base = base + jnp.where(xs > x, r2[2 * dx], 0.0)
        first = jnp.where(xs == 0, r2[2 * dx + 1], first)
    beside = rem(slab + 1 + (slabs - 2) * lax.div(z, jnp.int32(NZ // 2)), slabs)
    returned, edges = [], []
    for dz in near_first()[::-1] + [0]:
        tz = rem(z + dz, NZ)
        bead = bead_of(x, tz, y)
        places = first + level_rows(bead) * (px[tz] + base)
        px[tz] = places
        edges.append(send(px.at[tz, 3], halo.at[z], s4.at[dz], q4.at[dz], (bead, beside)))
        if dz:
            returned.append(send(px.at[tz, 0:3], land.at[z], s3.at[dz], q3.at[dz], to_bead(bead)))
        else:
            land[z] = places[0:3]
    return sent + swapped, returned[::-1], edges[::-1]


def backward_scan(r1, t2, r2, px, full, arriving, sems):
    s2, q2, s3, q3 = sems
    x, z, y = place()
    for copy in arriving:
        copy.wait_recv()
    total = jnp.zeros(r1.shape[1:], F32)
    plain = jnp.zeros(r1.shape[1:], F32)
    for zs in range(NZ):
        kept = None
        for ys in range(NY):
            one = r1[slot_from(zs, ys)]
            plain = plain + one
            total = total + one * level_rows(bead_of(x, zs, ys))
            kept = total if kept is None else jnp.where(y == ys, total, kept)
        px[zs] = kept
    t2[0] = total
    t2[1] = plain
    swapped = exchange_x(t2, r2, s2, q2)
    for copy in swapped:
        copy.wait_recv()
    base = jnp.zeros(r1.shape[1:], F32)
    for dx in range(1, NX):
        xs = rem(x + (NX - dx), NX)
        base = base + jnp.where(xs < x, r2[2 * dx], 0.0)
        plain = plain + r2[2 * dx + 1]
    returned = []
    for dz in near_first()[::-1] + [0]:
        tz = rem(z + dz, NZ)
        bead = bead_of(x, tz, y)
        result = jnp.where(bead > 0, px[tz] + base, plain)
        if dz:
            px[tz] = result
            returned.append(send(px.at[tz], full.at[z], s3.at[dz], q3.at[dz], to_bead(bead)))
        else:
            full[z] = result
    return swapped, returned[::-1]


def pack_chunks(section, border, raw):
    level = level_rows(lax.axis_index("bead"))
    inverse = 1.0 / jnp.maximum(level, 1.0)
    tpc = section.shape[2]
    sub = lax.broadcasted_iota(jnp.int32, (8, TILE), 0)
    blocks = NZ // 2 * tpc // 8
    for z in range(NZ):
        raw[z, 0:3] = section[:, z] * inverse
    pieces = []
    for c in range(3):
        for b in range(blocks):
            rows = [section[c, b * (8 // tpc) + m] for m in range(8 // tpc)]
            pieces.append(jnp.concatenate(rows, axis=0))
    half = NZ // 2
    for z in range(NZ):
        k, n = z // half, z % half
        index = jnp.broadcast_to(border[k : k + 1, n * TILE : (n + 1) * TILE], (8, TILE))
        lane, block = index % TILE, index // TILE
        rows = []
        for c in range(3):
            out = jnp.zeros((8, TILE), F32)
            for b in range(blocks):
                taken = jnp.take_along_axis(
                    pieces[c * blocks + b], lane, axis=1, mode="promise_in_bounds"
                )
                out = jnp.where(block == b * 8 + sub, taken, out)
            rows.append(jnp.sum(out, axis=0, keepdims=True))
        raw[z, 3] = jnp.concatenate(rows + [jnp.zeros((1, TILE), F32)], axis=0) * inverse[0]


def split3(value):
    high = value.astype(BF16).astype(F32)
    rest = value - high
    middle = rest.astype(BF16).astype(F32)
    return high, middle, rest - middle


def prepare_tile(t, rows, shift, own, lefts, lefts_t, rights, places, row, count):
    sub = lax.broadcasted_iota(jnp.int32, (8, TILE), 0)
    comp = sub % 4
    xs = [jnp.broadcast_to(v, (8, TILE)) for v in rows]
    xs = [(v - w) * shrink for v, w in zip(xs, (shift, 0.5 * slab_width, 0.5 * slab_width))]
    p = jnp.where(comp == 0, xs[0], jnp.where(comp == 1, xs[1], xs[2]))
    norm = xs[0] * xs[0] + xs[1] * xs[1] + xs[2] * xs[2]
    far = norm
    if own is not None:
        place_in = row + lax.broadcasted_iota(jnp.int32, (8, TILE), 1)
        far = jnp.where(place_in < count, norm, 4096.0)
    high, middle, low = split3(p)
    fh, fm, fl = split3(far)
    last, top = comp == 3, sub < 4
    a0 = jnp.where(last, jnp.where(top, fh, fm), high)
    a1 = jnp.where(last, jnp.where(top, fl, 1.0), middle)
    a2 = jnp.where(last, 1.0, jnp.where(top, low, high))
    left = jnp.concatenate([a0, a1, a2, jnp.zeros((8, TILE), F32)], axis=0)
    lefts[t] = left.astype(BF16)
    lefts_t[t] = left.T.astype(BF16)
    if own is not None:
        nh, nm, nl = split3(norm + 1.0 / reach_sq)
        h2, m2, l2 = -2.0 * high, -2.0 * middle, -2.0 * low
        b0 = jnp.where(last, 1.0, jnp.where(top, h2, m2))
        b1 = jnp.where(last, jnp.where(top, 1.0, nh), jnp.where(top, h2, m2))
        b2 = jnp.where(last, jnp.where(top, nm, nl), jnp.where(top, h2, l2))
        right = jnp.concatenate([b0, b1, b2, jnp.zeros((8, TILE), F32)], axis=0)
        rights[own] = right.astype(BF16)
        places[own] = p


def prepare_own(z, land, centre, count, *refs):
    half, tpc = NZ // 2, refs[2].shape[0] // NZ
    for n in range(tpc):
        rows = [land[z, c, n : n + 1, :] for c in range(3)]
        i = z * tpc + n
        prepare_tile(half + i, rows, centre, i, *refs, i * TILE, count)


def prepare_halo(z, halo, shifts, *refs):
    half, tiles = NZ // 2, refs[2].shape[0]
    upper = lax.div(z, jnp.int32(half))
    rows = [halo[z, c : c + 1, :] for c in range(3)]
    shift = jnp.where(upper == 0, shifts[0], shifts[1])
    prepare_tile(z + upper * tiles, rows, shift, None, *refs, 0, 0)


def quotients(i, buf, neighbours, lefts_t, rights):
    right = rights[i]
    for n in range(neighbours.shape[0]):
        buf[n * TILE : (n + 1) * TILE, :] = jnp.dot(
            lefts_t[neighbours[n, i]], right, preferred_element_type=F32
        )


def tile_force(i, zc, n, buf, neighbours, lefts, places, force, count):
    total = jnp.zeros((KROWS, TILE), F32)
    for k in range(0, neighbours.shape[0], 2):
        q = buf[k * TILE : (k + 2) * TILE, :]
        r = 1.0 / q
        r2 = r * r
        d = jnp.maximum(r2 - r, 0.0)
        f = ((d * d) * (r2 * r - 0.5 * reach_sq**3)).astype(BF16)
        x = jnp.concatenate([lefts[neighbours[k, i]], lefts[neighbours[k + 1, i]]], axis=1)
        total = total + jnp.dot(x, f, preferred_element_type=F32)
    moved = total[0:8] + total[8:16] + total[16:24]
    row = i * TILE + lax.broadcasted_iota(jnp.int32, (8, TILE), 1)
    beads = lax.axis_size("bead")
    scale = jnp.where(row < count, 48.0 / 256.0 / reach_sq**5 / shrink / beads, 0.0)
    result = (places[i] * total[15:16] - moved) * scale
    for c in range(3):
        force[zc, c, n : n + 1, :] = result[c : c + 1]


def forces(neighbours, count, lefts, lefts_t, rights, places, even, odd, force, r1, send_sem, recv_sem):
    x, z, y = place()
    tpc = rights.shape[0] // NZ
    half = NZ // 2
    bufs = (even, odd)

    def offset(c):
        return half + lax.div(c, jnp.int32(2)) * (1 - rem(c, 2)) - lax.div(c + 1, jnp.int32(2)) * rem(c, 2)

    quotients(rem(z + half, NZ) * tpc, even, neighbours, lefts_t, rights)

    def chunk(c, carry):
        dz = offset(c)
        zc = rem(z + dz, NZ)
        after = rem(z + offset(jnp.minimum(c + 1, NZ - 1)), NZ)
        for n in range(tpc):
            following = zc * tpc + n + 1 if n + 1 < tpc else after * tpc
            quotients(following, bufs[(n + 1) % 2], neighbours, lefts_t, rights)
            tile_force(zc * tpc + n, zc, n, bufs[n % 2], neighbours, lefts, places, force, count)
        group_copy(force.at[zc], r1, send_sem, recv_sem, dz, 1).start()

        @pl.when(c < NZ - 1)
        def _():
            group_copy(force.at[zc], r1, send_sem, recv_sem, dz, 0).start()

        return carry

    lax.fori_loop(0, NZ, chunk, 0)
    r1[0] = force[z]
    return [group_copy(force.at[rem(z + dz, NZ)], r1, send_sem, recv_sem, dz, dy) for dz, dy in group_steps()]


def kernel(
    counts, neighbours_in, border_in, section_in, out,
    neighbours, border, section, raw, land, halo, force, full,
    lefts, lefts_t, rights, places, even, odd,
    r1f, t2f, r2f, pxf, r1b, t2b, r2b, pxb,
    load_sem, store_sem, *sems,
):
    x, z, y = place()
    slab, slabs = lax.axis_index("slab"), lax.axis_size("slab")
    loads = [
        pltpu.make_async_copy(section_in, section, load_sem.at[0]),
        pltpu.make_async_copy(border_in, border, load_sem.at[1]),
        pltpu.make_async_copy(neighbours_in, neighbours, load_sem.at[2]),
    ]
    for load in loads:
        load.start()
    barrier = pltpu.get_barrier_semaphore()
    greeted = partners()
    for device in greeted:
        pl.semaphore_signal(barrier, inc=1, device_id=device, device_id_type=MESH)
    for load in loads:
        load.wait()
    pack_chunks(section, border, raw)
    pl.semaphore_wait(barrier, len(greeted))
    started, returned, edges = forward_scan(raw, r1f, t2f, r2f, pxf, land, halo, sems[:8])
    count = counts[0]
    box = slab_width * slabs
    centre = (slab.astype(F32) + 0.5) * slab_width
    shifts = (
        centre + jnp.where(slab == 0, box, 0.0),
        centre - jnp.where(slab == slabs - 1, box, 0.0),
    )
    refs = (lefts, lefts_t, rights, places)
    prepare_own(z, land, centre, count, *refs)
    for copy, edge, dz in zip([None] + returned, edges, [0] + near_first()):
        source = rem(z + (NZ - dz), NZ)
        if copy is not None:
            copy.wait_recv()
            prepare_own(source, land, centre, count, *refs)
        edge.wait_recv()
        prepare_halo(source, halo, shifts, *refs)
    arriving = forces(
        neighbours, count, lefts, lefts_t, rights, places, even, odd, force, r1b, *sems[8:10]
    )
    swapped, back = backward_scan(r1b, t2b, r2b, pxb, full, arriving, sems[10:])
    stores = []
    for copy, dz in zip([None] + back, [0] + near_first()):
        source = rem(z + (NZ - dz), NZ)
        if copy is not None:
            copy.wait_recv()
        store = pltpu.make_async_copy(full.at[source], out.at[:, source], store_sem.at[dz])
        store.start()
        stores.append(store)
    for copy in started + returned + edges + arriving + swapped + back:
        copy.wait_send()
    for store in stores:
        store.wait()


def leapfrog(section, momentum, section_force):
    level = lax.axis_index("bead").astype(F32)
    safe = jnp.maximum(level, 1.0)
    section_force = section_force / safe
    mass = jnp.where(level > 0, (level + 1.0) / safe, 1.0)
    spring = jnp.where(level > 0, omega_sq * mass, 0.0)
    step = time_step / 3.0
    push = 0.5 * step * spring
    drift = step / mass
    p = momentum + (0.5 * time_step) * section_force
    u = section
    for turn in range(3):
        p = p - push * u
        u = u + drift * p
        p = p - push * u
    return u, p


def step(section, momentum, neighbours, border_rows, counts):
    shape = section.shape
    listed = neighbours.shape[2]
    tiles = shape[2] // TILE
    tpc = tiles // NZ
    dense = (3, NZ, tpc, TILE)
    ext_tiles = tiles + NZ
    chunk, wide = (3, tpc, TILE), (4, tpc, TILE)
    anywhere = pl.BlockSpec(memory_space=pl.ANY)
    in_hbm = pl.BlockSpec(memory_space=pltpu.HBM)
    hbm = lambda array: pltpu.with_memory_space_constraint(array, pltpu.HBM)
    vmem = lambda *dims: pltpu.VMEM(dims, F32)
    scan_buffers = [
        vmem(count, *part)
        for part in (wide, chunk)
        for count in (NZ * NY, 2, NX * 2, NZ)
    ]
    scan_sems = [DMA((NZ * NY,))] * 2 + [DMA((NX,))] * 2 + [DMA((NZ,))] * 2
    section, momentum = section.reshape(dense), momentum.reshape(dense)
    section_force = pl.pallas_call(
        kernel,
        out_shape=jax.ShapeDtypeStruct(dense, F32),
        in_specs=[
            pl.BlockSpec(memory_space=pltpu.SMEM),
            in_hbm,
            in_hbm,
            in_hbm,
        ],
        out_specs=anywhere,
        scratch_shapes=[
            pltpu.SMEM((listed, tiles), jnp.int32),
            pltpu.VMEM(border_rows.shape[1:], jnp.int32),
            vmem(*dense),
            vmem(NZ, *wide),
            vmem(NZ, *chunk),
            vmem(NZ, 4, TILE),
            vmem(NZ, *chunk),
            vmem(NZ, *chunk),
            pltpu.VMEM((ext_tiles, KROWS, TILE), BF16),
            pltpu.VMEM((ext_tiles, TILE, KROWS), BF16),
            pltpu.VMEM((tiles, KROWS, TILE), BF16),
            vmem(tiles, 8, TILE),
            vmem(listed * TILE, TILE),
            vmem(listed * TILE, TILE),
        ]
        + scan_buffers
        + [DMA((3,)), DMA((NZ,))]
        + scan_sems
        + [DMA((NZ,))] * 2
        + scan_sems,
        compiler_params=pltpu.CompilerParams(
            collective_id=0, has_side_effects=True, vmem_limit_bytes=24 * 2**20
        ),
        name="path_step",
    )(
        counts,
        hbm(neighbours.transpose(0, 2, 1).reshape(listed, tiles)),
        hbm(border_rows.reshape(border_rows.shape[1:])),
        hbm(section),
    )
    u, p = leapfrog(section, momentum, section_force)
    return u.reshape(shape), p.reshape(shape)


def solution(mesh):
    return jax.shard_map(
        step,
        mesh=mesh,
        in_specs=(
            P("bead", None, "slab"),
            P("bead", None, "slab"),
            P("slab", None, None),
            P("slab", None, None),
            P("slab"),
        ),
        out_specs=(P("bead", None, "slab"), P("bead", None, "slab")),
        check_vma=False,
    )
```

```python
import functools
import math

import jax
import jax.numpy as jnp
from jax import lax
from jax.experimental import pallas as pl
from jax.experimental.pallas import tpu as pltpu
from jax.sharding import PartitionSpec as P

MESH = pl.DeviceIdType.MESH
time_step = 0.1
omega_sq = 4.0
slab_width = 3.0
reach_sq = 17.0
shrink = 1.0 / math.sqrt(reach_sq)
NX, NZ, NY = 4, 8, 2
TILE = 128
KROWS = 32
F32 = jnp.float32
BF16 = jnp.bfloat16
DMA = pltpu.SemaphoreType.DMA


def rem(value, size):
    return lax.rem(value, jnp.int32(size))


def place():
    bead = lax.axis_index("bead")
    return lax.div(bead, jnp.int32(NZ * NY)), rem(lax.div(bead, jnp.int32(NY)), NZ), rem(bead, NY)


def bead_of(x, z, y):
    return (x * NZ + z) * NY + y


def to_bead(bead):
    return (bead, lax.axis_index("slab"))


def group_steps():
    return [(dz, dy) for dz in range(NZ) for dy in range(NY) if dz or dy]


def reach(dz):
    return min(dz, NZ - dz)


def partners():
    x, z, y = place()
    slab, slabs = lax.axis_index("slab"), lax.axis_size("slab")
    found = []
    for dz in sorted(range(NZ), key=reach, reverse=True):
        tz = rem(z + dz, NZ)
        found += [to_bead(bead_of(x, tz, rem(y + dy, NY))) for dy in reversed(range(NY)) if dz or dy]
        found += [(bead_of(x, tz, y), rem(slab + ds, slabs)) for ds in (1, slabs - 1)]
    return found + [to_bead(bead_of(rem(x + dx, NX), z, y)) for dx in range(1, NX)]


def remote(src, dst, send_sem, recv_sem, device):
    return pltpu.make_async_remote_copy(
        src_ref=src,
        dst_ref=dst,
        send_sem=send_sem,
        recv_sem=recv_sem,
        device_id=device,
        device_id_type=MESH,
    )


def send(*args):
    copy = remote(*args)
    copy.start()
    return copy


def await_bytes(ref, sem):
    pltpu.make_async_copy(ref, ref, sem).wait()


def group_copy(src, r1, send_sem, recv_sem, dz, dy):
    x, z, y = place()
    device = to_bead(bead_of(x, rem(z + dz, NZ), rem(y + dy, NY)))
    return remote(src, r1.at[dz * NY + dy], send_sem.at[0], recv_sem.at[0], device)


def exchange_x(src, slots, send_sem, recv_sem):
    x, z, y = place()
    for dx in range(1, NX):
        device = to_bead(bead_of(rem(x + dx, NX), z, y))
        send(src, slots.at[dx], send_sem.at[0], recv_sem.at[0], device)


def level_rows(bead):
    return jnp.full((1, 1, TILE), bead.astype(F32), F32)


def slot_from(zs, ys):
    x, z, y = place()
    return rem(z + (NZ - zs), NZ) * NY + rem(y + (NY - ys), NY)


def near_first():
    return sorted(range(1, NZ), key=reach)


def forward_scan(raw, r1, t2, r2, first_in, px, land, halo, sems):
    s1, q1, s2, q2, sf, qf, s3, q3, s4, q4 = sems
    x, z, y = place()
    slab, slabs = lax.axis_index("slab"), lax.axis_size("slab")
    for dz, dy in reversed(group_steps()):
        group_copy(raw.at[rem(z + dz, NZ)], r1, s1, q1, dz, dy).start()
    r1[0] = raw[z]
    await_bytes(r1.at[1:], q1.at[0])

    @pl.when(x == 0)
    def _():
        for dx in range(1, NX):
            device = to_bead(bead_of(dx, z, y))
            send(r1.at[slot_from(0, 0)], first_in.at[0], sf.at[0], qf.at[0], device)
        first_in[0] = r1[slot_from(0, 0)]

    total = jnp.zeros(r1.shape[1:], F32)
    for zs in reversed(range(NZ)):
        kept = None
        for ys in reversed(range(NY)):
            one = r1[slot_from(zs, ys)]
            if zs == 0 and ys == 0:
                one = jnp.where(x == 0, 0.0, one)
            total = total + one
            kept = total if kept is None else jnp.where(y == ys, total, kept)
        px[zs] = kept
    t2[0] = total
    exchange_x(t2.at[0], r2, s2, q2)

    @pl.when(x != 0)
    def _():
        await_bytes(first_in.at[0], qf.at[0])

    await_bytes(r2.at[1:], q2.at[0])
    base = jnp.zeros(r1.shape[1:], F32)
    for dx in range(1, NX):
        xs = rem(x + (NX - dx), NX)
        base = base + jnp.where(xs > x, r2[dx], 0.0)
    first = first_in[0]
    beside = rem(slab + 1 + (slabs - 2) * lax.div(z, jnp.int32(NZ // 2)), slabs)
    for dz in near_first()[::-1] + [0]:
        tz = rem(z + dz, NZ)
        bead = bead_of(x, tz, y)
        places = first + level_rows(bead) * (px[tz] + base)
        px[tz] = places
        send(px.at[tz, 3], halo.at[z], s4.at[0], q4.at[dz], (bead, beside))
        if dz:
            send(px.at[tz, 0:3], land.at[z], s3.at[0], q3.at[dz], to_bead(bead))
        else:
            land[z] = places[0:3]

    def finish():
        await_bytes(r1.at[1:], s1.at[0])
        await_bytes(r2.at[1:], s2.at[0])
        await_bytes(land.at[1:], s3.at[0])
        await_bytes(halo, s4.at[0])

        @pl.when(x == 0)
        def _():
            await_bytes(r2.at[1:], sf.at[0])

    return finish


def backward_scan(r1, t2, r2, plain_in, px, out, sems):
    s1, q1, s2, q2, sf, qf, s3, q3, own_sem = sems
    x, z, y = place()
    await_bytes(r1.at[1:], q1.at[0])
    plain = jnp.zeros(r1.shape[1:], F32)
    total = jnp.zeros(r1.shape[1:], F32)
    for zs in range(NZ):
        kept = None
        for ys in range(NY):
            one = r1[slot_from(zs, ys)]
            plain = plain + one
            total = total + one * level_rows(bead_of(x, zs, ys))
            kept = total if kept is None else jnp.where(y == ys, total, kept)
        px[zs] = kept
    t2[0] = total
    t2[1] = plain
    exchange_x(t2.at[0], r2, s2, q2)

    @pl.when(x != 0)
    def _():
        send(t2.at[1], plain_in.at[x], sf.at[0], qf.at[0], to_bead(bead_of(0, z, y)))

    @pl.when(x == 0)
    def _():
        plain_in[0] = plain
        await_bytes(plain_in.at[1:], qf.at[0])

    await_bytes(r2.at[1:], q2.at[0])
    base = jnp.zeros(r1.shape[1:], F32)
    for dx in range(1, NX):
        xs = rem(x + (NX - dx), NX)
        base = base + jnp.where(xs < x, r2[dx], 0.0)
    for zs in range(NZ):
        px[zs] = px[zs] + base

    @pl.when((x == 0) & (y == 0))
    def _():
        everything = plain_in[0]
        for xs in range(1, NX):
            everything = everything + plain_in[xs]
        px[0] = everything

    for dz in near_first()[::-1] + [0]:
        tz = rem(z + dz, NZ)
        if dz:
            device = to_bead(bead_of(x, tz, y))
            send(px.at[tz], out.at[:, z], s3.at[0], q3.at[0], device)
        else:
            own = pltpu.make_async_copy(px.at[tz], out.at[:, z], own_sem.at[0])
            own.start()

    await_bytes(px.at[1:], q3.at[0])
    own.wait()
    await_bytes(r1.at[1:], s1.at[0])
    await_bytes(r2.at[1:], s2.at[0])
    await_bytes(px.at[1:], s3.at[0])

    @pl.when(x != 0)
    def _():
        await_bytes(t2.at[1], sf.at[0])


def pack_chunks(section, border, raw):
    level = level_rows(lax.axis_index("bead"))
    inverse = 1.0 / jnp.maximum(level, 1.0)
    tpc = section.shape[2]
    sub = lax.broadcasted_iota(jnp.int32, (8, TILE), 0)
    blocks = NZ // 2 * tpc // 8
    for z in range(NZ):
        raw[z, 0:3] = section[:, z] * inverse
    pieces = []
    for c in range(3):
        for b in range(blocks):
            rows = [section[c, b * (8 // tpc) + m] for m in range(8 // tpc)]
            pieces.append(jnp.concatenate(rows, axis=0))
    half = NZ // 2
    for z in range(NZ):
        k, n = z // half, z % half
        index = jnp.broadcast_to(border[k : k + 1, n * TILE : (n + 1) * TILE], (8, TILE))
        lane, block = index % TILE, index // TILE
        rows = []
        for c in range(3):
            out = jnp.zeros((8, TILE), F32)
            for b in range(blocks):
                taken = jnp.take_along_axis(
                    pieces[c * blocks + b], lane, axis=1, mode="promise_in_bounds"
                )
                out = jnp.where(block == b * 8 + sub, taken, out)
            rows.append(jnp.sum(out, axis=0, keepdims=True))
        raw[z, 3] = jnp.concatenate(rows + [jnp.zeros((1, TILE), F32)], axis=0) * inverse[0]


def split3(value):
    high = value.astype(BF16).astype(F32)
    rest = value - high
    middle = rest.astype(BF16).astype(F32)
    return high, middle, rest - middle


def prepare_tile(t, rows, shift, own, lefts, lefts_t, rights, places, row, count):
    sub = lax.broadcasted_iota(jnp.int32, (8, TILE), 0)
    comp = sub % 4
    xs = [jnp.broadcast_to(v, (8, TILE)) for v in rows]
    xs = [(v - w) * shrink for v, w in zip(xs, (shift, 0.5 * slab_width, 0.5 * slab_width))]
    p = jnp.where(comp == 0, xs[0], jnp.where(comp == 1, xs[1], xs[2]))
    norm = xs[0] * xs[0] + xs[1] * xs[1] + xs[2] * xs[2]
    far = norm
    if own is not None:
        place_in = row + lax.broadcasted_iota(jnp.int32, (8, TILE), 1)
        far = jnp.where(place_in < count, norm, 4096.0)
    high, middle, low = split3(p)
    fh, fm, fl = split3(far)
    last, top = comp == 3, sub < 4
    a0 = jnp.where(last, jnp.where(top, fh, fm), high)
    a1 = jnp.where(last, jnp.where(top, fl, 1.0), middle)
    a2 = jnp.where(last, 1.0, jnp.where(top, low, high))
    left = jnp.concatenate([a0, a1, a2, jnp.zeros((8, TILE), F32)], axis=0)
    lefts[t] = left.astype(BF16)
    lefts_t[t] = left.T.astype(BF16)
    if own is not None:
        nh, nm, nl = split3(norm + 1.0 / reach_sq)
        h2, m2, l2 = -2.0 * high, -2.0 * middle, -2.0 * low
        b0 = jnp.where(last, 1.0, jnp.where(top, h2, m2))
        b1 = jnp.where(last, jnp.where(top, 1.0, nh), jnp.where(top, h2, m2))
        b2 = jnp.where(last, jnp.where(top, nm, nl), jnp.where(top, h2, l2))
        right = jnp.concatenate([b0, b1, b2, jnp.zeros((8, TILE), F32)], axis=0)
        rights[own] = right.astype(BF16)
        places[own] = p


def prepare_own(z, land, centre, count, *refs):
    half, tpc = NZ // 2, refs[2].shape[0] // NZ
    for n in range(tpc):
        rows = [land[z, c, n : n + 1, :] for c in range(3)]
        i = z * tpc + n
        prepare_tile(half + i, rows, centre, i, *refs, i * TILE, count)


def prepare_halo(z, halo, shifts, *refs):
    half, tiles = NZ // 2, refs[2].shape[0]
    upper = lax.div(z, jnp.int32(half))
    rows = [halo[z, c : c + 1, :] for c in range(3)]
    shift = jnp.where(upper == 0, shifts[0], shifts[1])
    prepare_tile(z + upper * tiles, rows, shift, None, *refs, 0, 0)


def quotients(i, buf, neighbours, lefts_t, rights):
    right = rights[i]
    for n in range(neighbours.shape[0]):
        buf[n * TILE : (n + 1) * TILE, :] = jnp.dot(
            lefts_t[neighbours[n, i]], right, preferred_element_type=F32
        )


def tile_force(i, zc, n, buf, neighbours, lefts, places, force, count):
    total = jnp.zeros((KROWS, TILE), F32)
    for k in range(0, neighbours.shape[0], 2):
        q = buf[k * TILE : (k + 2) * TILE, :]
        r = 1.0 / q
        r2 = r * r
        d = jnp.maximum(r2 - r, 0.0)
        f = ((d * d) * (r2 * r - 0.5 * reach_sq**3)).astype(BF16)
        x = jnp.concatenate([lefts[neighbours[k, i]], lefts[neighbours[k + 1, i]]], axis=1)
        total = total + jnp.dot(x, f, preferred_element_type=F32)
    moved = total[0:8] + total[8:16] + total[16:24]
    row = i * TILE + lax.broadcasted_iota(jnp.int32, (8, TILE), 1)
    beads = lax.axis_size("bead")
    scale = jnp.where(row < count, 48.0 / 256.0 / reach_sq**5 / shrink / beads, 0.0)
    result = (places[i] * total[15:16] - moved) * scale
    for c in range(3):
        force[zc, c, n : n + 1, :] = result[c : c + 1]


def forces(neighbours, count, lefts, lefts_t, rights, places, even, odd, force, r1, send_sem, recv_sem):
    x, z, y = place()
    tpc = rights.shape[0] // NZ
    half = NZ // 2
    bufs = (even, odd)

    def offset(c):
        return half + lax.div(c, jnp.int32(2)) * (1 - rem(c, 2)) - lax.div(c + 1, jnp.int32(2)) * rem(c, 2)

    quotients(rem(z + half, NZ) * tpc, even, neighbours, lefts_t, rights)

    def chunk(c, carry):
        dz = offset(c)
        zc = rem(z + dz, NZ)
        after = rem(z + offset(jnp.minimum(c + 1, NZ - 1)), NZ)
        for n in range(tpc):
            following = zc * tpc + n + 1 if n + 1 < tpc else after * tpc
            quotients(following, bufs[(n + 1) % 2], neighbours, lefts_t, rights)
            tile_force(zc * tpc + n, zc, n, bufs[n % 2], neighbours, lefts, places, force, count)
        group_copy(force.at[zc], r1, send_sem, recv_sem, dz, 1).start()

        @pl.when(c < NZ - 1)
        def _():
            group_copy(force.at[zc], r1, send_sem, recv_sem, dz, 0).start()

        return carry

    lax.fori_loop(0, NZ, chunk, 0)
    r1[0] = force[z]


def kernel(
    counts, neighbours_in, border_in, section_in, out,
    neighbours, border, section, raw, land, halo, force,
    lefts, lefts_t, rights, places, even, odd,
    r1f, t2f, r2f, first_in, pxf, r1b, t2b, r2b, plain_in, pxb,
    load_sem, *sems,
):
    x, z, y = place()
    slab, slabs = lax.axis_index("slab"), lax.axis_size("slab")
    loads = [
        pltpu.make_async_copy(section_in, section, load_sem.at[0]),
        pltpu.make_async_copy(border_in, border, load_sem.at[1]),
        pltpu.make_async_copy(neighbours_in, neighbours, load_sem.at[2]),
    ]
    for load in loads:
        load.start()
    barrier = pltpu.get_barrier_semaphore()
    greeted = partners()
    for device in greeted:
        pl.semaphore_signal(barrier, inc=1, device_id=device, device_id_type=MESH)
    for load in loads:
        load.wait()
    pack_chunks(section, border, raw)
    pl.semaphore_wait(barrier, len(greeted))
    finish = forward_scan(raw, r1f, t2f, r2f, first_in, pxf, land, halo, sems[:10])
    q3, q4 = sems[7], sems[9]
    count = counts[0]
    box = slab_width * slabs
    centre = (slab.astype(F32) + 0.5) * slab_width
    shifts = (
        centre + jnp.where(slab == 0, box, 0.0),
        centre - jnp.where(slab == slabs - 1, box, 0.0),
    )
    refs = (lefts, lefts_t, rights, places)
    farthest = NZ // 2
    for distance in range(farthest + 1):
        chunks = [dz for dz in range(NZ) if reach(dz) == distance]
        tiles = [dz for dz in range(NZ) if reach(dz) == distance - 1]
        if distance == farthest:
            tiles += chunks
        for dz in chunks:
            if dz:
                await_bytes(land.at[0], q3.at[dz])
        for dz in tiles:
            await_bytes(halo.at[0], q4.at[dz])
        for dz in chunks:
            prepare_own(rem(z + (NZ - dz), NZ), land, centre, count, *refs)
        for dz in tiles:
            prepare_halo(rem(z + (NZ - dz), NZ), halo, shifts, *refs)
    forces(
        neighbours, count, lefts, lefts_t, rights, places, even, odd, force, r1b, sems[10], sems[11]
    )
    backward_scan(r1b, t2b, r2b, plain_in, pxb, out, sems[10:])
    finish()


def leapfrog(section, momentum, section_force):
    level = lax.axis_index("bead").astype(F32)
    safe = jnp.maximum(level, 1.0)
    section_force = section_force / safe
    mass = jnp.where(level > 0, (level + 1.0) / safe, 1.0)
    spring = jnp.where(level > 0, omega_sq * mass, 0.0)
    step = time_step / 3.0
    push = 0.5 * step * spring
    drift = step / mass
    p = momentum + (0.5 * time_step) * section_force
    u = section
    for turn in range(3):
        p = p - push * u
        u = u + drift * p
        p = p - push * u
    return u, p


def step(section, momentum, neighbours, border_rows, counts):
    shape = section.shape
    listed = neighbours.shape[2]
    tiles = shape[2] // TILE
    tpc = tiles // NZ
    dense = (3, NZ, tpc, TILE)
    ext_tiles = tiles + NZ
    chunk, wide = (3, tpc, TILE), (4, tpc, TILE)
    anywhere = pl.BlockSpec(memory_space=pl.ANY)
    in_hbm = pl.BlockSpec(memory_space=pltpu.HBM)
    hbm = lambda array: pltpu.with_memory_space_constraint(array, pltpu.HBM)
    vmem = lambda *dims: pltpu.VMEM(dims, F32)
    scan_buffers = [
        vmem(count, *part)
        for part in (wide, chunk)
        for count in (NZ * NY, 2, NX, NX, NZ)
    ]
    one, each = DMA((1,)), DMA((NZ,))
    section, momentum = section.reshape(dense), momentum.reshape(dense)
    section_force = pl.pallas_call(
        kernel,
        out_shape=jax.ShapeDtypeStruct(dense, F32),
        in_specs=[
            pl.BlockSpec(memory_space=pltpu.SMEM),
            in_hbm,
            in_hbm,
            in_hbm,
        ],
        out_specs=anywhere,
        scratch_shapes=[
            pltpu.SMEM((listed, tiles), jnp.int32),
            pltpu.VMEM(border_rows.shape[1:], jnp.int32),
            vmem(*dense),
            vmem(NZ, *wide),
            vmem(NZ, *chunk),
            vmem(NZ, 4, TILE),
            vmem(NZ, *chunk),
            pltpu.VMEM((ext_tiles, KROWS, TILE), BF16),
            pltpu.VMEM((ext_tiles, TILE, KROWS), BF16),
            pltpu.VMEM((tiles, KROWS, TILE), BF16),
            vmem(tiles, 8, TILE),
            vmem(listed * TILE, TILE),
            vmem(listed * TILE, TILE),
        ]
        + scan_buffers
        + [DMA((3,))]
        + [one] * 6
        + [one, each] * 2
        + [one] * 9,
        compiler_params=pltpu.CompilerParams(
            collective_id=0, has_side_effects=True, vmem_limit_bytes=24 * 2**20
        ),
        name="path_step",
    )(
        counts,
        hbm(neighbours.transpose(0, 2, 1).reshape(listed, tiles)),
        hbm(border_rows.reshape(border_rows.shape[1:])),
        hbm(section),
    )
    u, p = leapfrog(section, momentum, section_force)
    return u.reshape(shape), p.reshape(shape)


def solution(mesh):
    return jax.shard_map(
        step,
        mesh=mesh,
        in_specs=(
            P("bead", None, "slab"),
            P("bead", None, "slab"),
            P("slab", None, None),
            P("slab", None, None),
            P("slab"),
        ),
        out_specs=(P("bead", None, "slab"), P("bead", None, "slab")),
        check_vma=False,
    )
```

```python
import functools
import math

import jax
import jax.numpy as jnp
from jax import lax
from jax.experimental import pallas as pl
from jax.experimental.pallas import tpu as pltpu
from jax.sharding import PartitionSpec as P

MESH = pl.DeviceIdType.MESH
time_step = 0.1
omega_sq = 4.0
slab_width = 3.0
reach_sq = 17.0
shrink = 1.0 / math.sqrt(reach_sq)
NX, NZ, NY = 4, 8, 2
TILE = 128
KROWS = 32
F32 = jnp.float32
BF16 = jnp.bfloat16
DMA = pltpu.SemaphoreType.DMA


def rem(value, size):
    return lax.rem(value, jnp.int32(size))


def place():
    bead = lax.axis_index("bead")
    return lax.div(bead, jnp.int32(NZ * NY)), rem(lax.div(bead, jnp.int32(NY)), NZ), rem(bead, NY)


def bead_of(x, z, y):
    return (x * NZ + z) * NY + y


def to_bead(bead):
    return (bead, lax.axis_index("slab"))


def group_steps():
    return [(dz, dy) for dz in range(NZ) for dy in range(NY) if dz or dy]


def reach(dz):
    return min(dz, NZ - dz)


def partners():
    x, z, y = place()
    slab, slabs = lax.axis_index("slab"), lax.axis_size("slab")
    found = []
    for dz in sorted(range(NZ), key=reach, reverse=True):
        tz = rem(z + dz, NZ)
        found += [to_bead(bead_of(x, tz, rem(y + dy, NY))) for dy in reversed(range(NY)) if dz or dy]
        found += [(bead_of(x, tz, y), rem(slab + ds, slabs)) for ds in (1, slabs - 1)]
    return found + [to_bead(bead_of(rem(x + dx, NX), z, y)) for dx in range(1, NX)]


def remote(src, dst, send_sem, recv_sem, device):
    return pltpu.make_async_remote_copy(
        src_ref=src,
        dst_ref=dst,
        send_sem=send_sem,
        recv_sem=recv_sem,
        device_id=device,
        device_id_type=MESH,
    )


def send(*args):
    copy = remote(*args)
    copy.start()
    return copy


def await_bytes(ref, sem):
    pltpu.make_async_copy(ref, ref, sem).wait()


def group_copy(src, r1, send_sem, recv_sem, dz, dy, kind=0):
    x, z, y = place()
    device = to_bead(bead_of(x, rem(z + dz, NZ), rem(y + dy, NY)))
    return remote(src, r1.at[dz * NY + dy], send_sem.at[0], recv_sem.at[kind], device)


def near_offsets():
    return (1, NZ - 1, 0)


def near_slots():
    return [(dx, k, dy) for dx in range(1, NX) for k in range(len(near_offsets())) for dy in range(NY)]


def near_slot(dx, k, dy):
    return ((dx - 1) * len(near_offsets()) + k) * NY + dy


def exchange_x(src, slots, send_sem, recv_sem):
    x, z, y = place()
    for dx in range(1, NX):
        device = to_bead(bead_of(rem(x + dx, NX), z, y))
        send(src, slots.at[dx], send_sem.at[0], recv_sem.at[0], device)


def level_rows(bead):
    return jnp.full((1, 1, TILE), bead.astype(F32), F32)


def slot_from(zs, ys):
    x, z, y = place()
    return rem(z + (NZ - zs), NZ) * NY + rem(y + (NY - ys), NY)


def near_first():
    return sorted(range(1, NZ), key=reach)


def forward_scan(raw, r1, t2, r2, first_in, px, land, halo, sems):
    s1, q1, s2, q2, sf, qf, s3, q3, s4, q4 = sems
    x, z, y = place()
    slab, slabs = lax.axis_index("slab"), lax.axis_size("slab")
    for dz, dy in reversed(group_steps()):
        group_copy(raw.at[rem(z + dz, NZ)], r1, s1, q1, dz, dy).start()
    r1[0] = raw[z]
    await_bytes(r1.at[1:], q1.at[0])

    @pl.when(x == 0)
    def _():
        for dx in range(1, NX):
            device = to_bead(bead_of(dx, z, y))
            send(r1.at[slot_from(0, 0)], first_in.at[0], sf.at[0], qf.at[0], device)
        first_in[0] = r1[slot_from(0, 0)]

    total = jnp.zeros(r1.shape[1:], F32)
    for zs in reversed(range(NZ)):
        kept = None
        for ys in reversed(range(NY)):
            one = r1[slot_from(zs, ys)]
            if zs == 0 and ys == 0:
                one = jnp.where(x == 0, 0.0, one)
            total = total + one
            kept = total if kept is None else jnp.where(y == ys, total, kept)
        px[zs] = kept
    t2[0] = total
    exchange_x(t2.at[0], r2, s2, q2)

    @pl.when(x != 0)
    def _():
        await_bytes(first_in.at[0], qf.at[0])

    await_bytes(r2.at[1:], q2.at[0])
    base = jnp.zeros(r1.shape[1:], F32)
    for dx in range(1, NX):
        xs = rem(x + (NX - dx), NX)
        base = base + jnp.where(xs > x, r2[dx], 0.0)
    first = first_in[0]
    beside = rem(slab + 1 + (slabs - 2) * lax.div(z, jnp.int32(NZ // 2)), slabs)
    for dz in near_first()[::-1] + [0]:
        tz = rem(z + dz, NZ)
        bead = bead_of(x, tz, y)
        places = first + level_rows(bead) * (px[tz] + base)
        px[tz] = places
        send(px.at[tz, 3], halo.at[z], s4.at[0], q4.at[dz], (bead, beside))
        if dz:
            send(px.at[tz, 0:3], land.at[z], s3.at[0], q3.at[dz], to_bead(bead))
        else:
            land[z] = places[0:3]

    def finish():
        await_bytes(r1.at[1:], s1.at[0])
        await_bytes(r2.at[1:], s2.at[0])
        await_bytes(land.at[1:], s3.at[0])
        await_bytes(halo, s4.at[0])

        @pl.when(x == 0)
        def _():
            await_bytes(r2.at[1:], sf.at[0])

    return finish


def backward_scan(r1, near, t2, r2, plain_in, px, out, sems):
    s1, q1, sn, qn, s2, q2, sf, qf, s3, q3, own_sem = sems
    x, z, y = place()
    far = [(dz, dy) for dz in range(NZ) for dy in range(NY) if dz not in near_offsets()]
    await_bytes(r1.at[0 : len(far)], q1.at[0])
    total = jnp.zeros(r1.shape[1:], F32)
    plain = jnp.zeros(r1.shape[1:], F32)
    for dz, dy in far:
        one = r1[dz * NY + dy]
        plain = plain + one
        total = total + one * level_rows(bead_of(x, rem(z + (NZ - dz), NZ), rem(y + (NY - dy), NY)))
    t2[0] = total
    t2[1] = plain
    exchange_x(t2.at[0], r2, s2, q2)

    @pl.when(x != 0)
    def _():
        send(t2.at[1], plain_in.at[x], sf.at[0], qf.at[0], to_bead(bead_of(0, z, y)))

    await_bytes(r1.at[0 : len(group_steps()) - len(far)], q1.at[1])
    total = jnp.zeros(r1.shape[1:], F32)
    plain = jnp.zeros(r1.shape[1:], F32)
    for zs in range(NZ):
        kept = None
        for ys in range(NY):
            one = r1[slot_from(zs, ys)]
            plain = plain + one
            total = total + one * level_rows(bead_of(x, zs, ys))
            kept = total if kept is None else jnp.where(y == ys, total, kept)
        px[zs] = kept
    await_bytes(near, qn.at[0])
    base = jnp.zeros(r1.shape[1:], F32)
    for dx, k, dy in near_slots():
        xs = rem(x + (NX - dx), NX)
        source = bead_of(xs, rem(z + (NZ - near_offsets()[k]), NZ), rem(y + (NY - dy), NY))
        one = near[near_slot(dx, k, dy)]
        plain = plain + one
        base = base + jnp.where(xs < x, one * level_rows(source), 0.0)

    @pl.when(x == 0)
    def _():
        plain_in[0] = plain
        await_bytes(plain_in.at[1:], qf.at[0])

    await_bytes(r2.at[1:], q2.at[0])
    for dx in range(1, NX):
        xs = rem(x + (NX - dx), NX)
        base = base + jnp.where(xs < x, r2[dx], 0.0)
    for zs in range(NZ):
        px[zs] = px[zs] + base

    @pl.when((x == 0) & (y == 0))
    def _():
        everything = plain_in[0]
        for xs in range(1, NX):
            everything = everything + plain_in[xs]
        px[0] = everything

    for dz in near_first()[::-1] + [0]:
        tz = rem(z + dz, NZ)
        if dz:
            device = to_bead(bead_of(x, tz, y))
            send(px.at[tz], out.at[:, z], s3.at[0], q3.at[0], device)
        else:
            own = pltpu.make_async_copy(px.at[tz], out.at[:, z], own_sem.at[0])
            own.start()

    await_bytes(px.at[1:], q3.at[0])
    own.wait()
    await_bytes(r1.at[1:], s1.at[0])
    await_bytes(near, sn.at[0])
    await_bytes(r2.at[1:], s2.at[0])
    await_bytes(px.at[1:], s3.at[0])

    @pl.when(x != 0)
    def _():
        await_bytes(t2.at[1], sf.at[0])


def pack_chunks(section, border, raw):
    level = level_rows(lax.axis_index("bead"))
    inverse = 1.0 / jnp.maximum(level, 1.0)
    tpc = section.shape[2]
    sub = lax.broadcasted_iota(jnp.int32, (8, TILE), 0)
    blocks = NZ // 2 * tpc // 8
    for z in range(NZ):
        raw[z, 0:3] = section[:, z] * inverse
    pieces = []
    for c in range(3):
        for b in range(blocks):
            rows = [section[c, b * (8 // tpc) + m] for m in range(8 // tpc)]
            pieces.append(jnp.concatenate(rows, axis=0))
    half = NZ // 2
    for z in range(NZ):
        k, n = z // half, z % half
        index = jnp.broadcast_to(border[k : k + 1, n * TILE : (n + 1) * TILE], (8, TILE))
        lane, block = index % TILE, index // TILE
        rows = []
        for c in range(3):
            out = jnp.zeros((8, TILE), F32)
            for b in range(blocks):
                taken = jnp.take_along_axis(
                    pieces[c * blocks + b], lane, axis=1, mode="promise_in_bounds"
                )
                out = jnp.where(block == b * 8 + sub, taken, out)
            rows.append(jnp.sum(out, axis=0, keepdims=True))
        raw[z, 3] = jnp.concatenate(rows + [jnp.zeros((1, TILE), F32)], axis=0) * inverse[0]


def split3(value):
    high = value.astype(BF16).astype(F32)
    rest = value - high
    middle = rest.astype(BF16).astype(F32)
    return high, middle, rest - middle


def prepare_tile(t, rows, shift, own, lefts, lefts_t, rights, places, row, count):
    sub = lax.broadcasted_iota(jnp.int32, (8, TILE), 0)
    comp = sub % 4
    xs = [jnp.broadcast_to(v, (8, TILE)) for v in rows]
    xs = [(v - w) * shrink for v, w in zip(xs, (shift, 0.5 * slab_width, 0.5 * slab_width))]
    p = jnp.where(comp == 0, xs[0], jnp.where(comp == 1, xs[1], xs[2]))
    norm = xs[0] * xs[0] + xs[1] * xs[1] + xs[2] * xs[2]
    far = norm
    if own is not None:
        place_in = row + lax.broadcasted_iota(jnp.int32, (8, TILE), 1)
        far = jnp.where(place_in < count, norm, 4096.0)
    high, middle, low = split3(p)
    fh, fm, fl = split3(far)
    last, top = comp == 3, sub < 4
    a0 = jnp.where(last, jnp.where(top, fh, fm), high)
    a1 = jnp.where(last, jnp.where(top, fl, 1.0), middle)
    a2 = jnp.where(last, 1.0, jnp.where(top, low, high))
    left = jnp.concatenate([a0, a1, a2, jnp.zeros((8, TILE), F32)], axis=0)
    lefts[t] = left.astype(BF16)
    lefts_t[t] = left.T.astype(BF16)
    if own is not None:
        nh, nm, nl = split3(norm + 1.0 / reach_sq)
        h2, m2, l2 = -2.0 * high, -2.0 * middle, -2.0 * low
        b0 = jnp.where(last, 1.0, jnp.where(top, h2, m2))
        b1 = jnp.where(last, jnp.where(top, 1.0, nh), jnp.where(top, h2, m2))
        b2 = jnp.where(last, jnp.where(top, nm, nl), jnp.where(top, h2, l2))
        right = jnp.concatenate([b0, b1, b2, jnp.zeros((8, TILE), F32)], axis=0)
        rights[own] = right.astype(BF16)
        places[own] = p


def prepare_own(z, land, centre, count, *refs):
    half, tpc = NZ // 2, refs[2].shape[0] // NZ
    for n in range(tpc):
        rows = [land[z, c, n : n + 1, :] for c in range(3)]
        i = z * tpc + n
        prepare_tile(half + i, rows, centre, i, *refs, i * TILE, count)


def prepare_halo(z, halo, shifts, *refs):
    half, tiles = NZ // 2, refs[2].shape[0]
    upper = lax.div(z, jnp.int32(half))
    rows = [halo[z, c : c + 1, :] for c in range(3)]
    shift = jnp.where(upper == 0, shifts[0], shifts[1])
    prepare_tile(z + upper * tiles, rows, shift, None, *refs, 0, 0)


def quotients(i, buf, neighbours, lefts_t, rights):
    right = rights[i]
    for n in range(neighbours.shape[0]):
        buf[n * TILE : (n + 1) * TILE, :] = jnp.dot(
            lefts_t[neighbours[n, i]], right, preferred_element_type=F32
        )


def tile_force(i, zc, n, buf, neighbours, lefts, places, force, count):
    total = jnp.zeros((KROWS, TILE), F32)
    for k in range(0, neighbours.shape[0], 2):
        q = buf[k * TILE : (k + 2) * TILE, :]
        r = 1.0 / q
        r2 = r * r
        d = jnp.maximum(r2 - r, 0.0)
        f = ((d * d) * (r2 * r - 0.5 * reach_sq**3)).astype(BF16)
        x = jnp.concatenate([lefts[neighbours[k, i]], lefts[neighbours[k + 1, i]]], axis=1)
        total = total + jnp.dot(x, f, preferred_element_type=F32)
    moved = total[0:8] + total[8:16] + total[16:24]
    row = i * TILE + lax.broadcasted_iota(jnp.int32, (8, TILE), 1)
    beads = lax.axis_size("bead")
    scale = jnp.where(row < count, 48.0 / 256.0 / reach_sq**5 / shrink / beads, 0.0)
    result = (places[i] * total[15:16] - moved) * scale
    for c in range(3):
        force[zc, c, n : n + 1, :] = result[c : c + 1]


def forces(neighbours, count, lefts, lefts_t, rights, places, even, odd, force, r1, near, sems):
    x, z, y = place()
    tpc = rights.shape[0] // NZ
    half = NZ // 2
    bufs = (even, odd)
    send_sem, recv_sem, near_send, near_recv = sems

    def offset(c):
        return half + lax.div(c, jnp.int32(2)) * (1 - rem(c, 2)) - lax.div(c + 1, jnp.int32(2)) * rem(c, 2)

    quotients(rem(z + half, NZ) * tpc, even, neighbours, lefts_t, rights)

    def chunk(c, carry):
        dz = offset(c)
        zc = rem(z + dz, NZ)
        after = rem(z + offset(jnp.minimum(c + 1, NZ - 1)), NZ)
        for n in range(tpc):
            following = zc * tpc + n + 1 if n + 1 < tpc else after * tpc
            quotients(following, bufs[(n + 1) % 2], neighbours, lefts_t, rights)
            tile_force(zc * tpc + n, zc, n, bufs[n % 2], neighbours, lefts, places, force, count)
        first_near = NZ - len(near_offsets())
        kind = jnp.minimum(jnp.maximum(c - first_near + 1, 0), 1)
        group_copy(force.at[zc], r1, send_sem, recv_sem, dz, 1, kind).start()

        @pl.when(c < NZ - 1)
        def _():
            group_copy(force.at[zc], r1, send_sem, recv_sem, dz, 0, kind).start()

        @pl.when(c >= first_near)
        def _():
            for dx in range(1, NX):
                for dy in range(NY):
                    device = to_bead(bead_of(rem(x + dx, NX), zc, rem(y + dy, NY)))
                    slot = near_slot(dx, c - first_near, dy)
                    send(force.at[zc], near.at[slot], near_send.at[0], near_recv.at[0], device)

        return carry

    lax.fori_loop(0, NZ, chunk, 0)
    r1[0] = force[z]


def kernel(
    counts, neighbours_in, border_in, section_in, out,
    neighbours, border, section, raw, land, halo, force,
    lefts, lefts_t, rights, places, even, odd,
    r1f, t2f, r2f, first_in, pxf, r1b, t2b, r2b, plain_in, pxb, near,
    load_sem, *sems,
):
    x, z, y = place()
    slab, slabs = lax.axis_index("slab"), lax.axis_size("slab")
    loads = [
        pltpu.make_async_copy(section_in, section, load_sem.at[0]),
        pltpu.make_async_copy(border_in, border, load_sem.at[1]),
        pltpu.make_async_copy(neighbours_in, neighbours, load_sem.at[2]),
    ]
    for load in loads:
        load.start()
    barrier = pltpu.get_barrier_semaphore()
    greeted = partners()
    for device in greeted:
        pl.semaphore_signal(barrier, inc=1, device_id=device, device_id_type=MESH)
    for load in loads:
        load.wait()
    pack_chunks(section, border, raw)
    pl.semaphore_wait(barrier, len(greeted))
    finish = forward_scan(raw, r1f, t2f, r2f, first_in, pxf, land, halo, sems[:10])
    q3, q4 = sems[7], sems[9]
    count = counts[0]
    box = slab_width * slabs
    centre = (slab.astype(F32) + 0.5) * slab_width
    shifts = (
        centre + jnp.where(slab == 0, box, 0.0),
        centre - jnp.where(slab == slabs - 1, box, 0.0),
    )
    refs = (lefts, lefts_t, rights, places)
    farthest = NZ // 2
    for distance in range(farthest + 1):
        chunks = [dz for dz in range(NZ) if reach(dz) == distance]
        tiles = [dz for dz in range(NZ) if reach(dz) == distance - 1]
        if distance == farthest:
            tiles += chunks
        for dz in chunks:
            if dz:
                await_bytes(land.at[0], q3.at[dz])
        for dz in tiles:
            await_bytes(halo.at[0], q4.at[dz])
        for dz in chunks:
            prepare_own(rem(z + (NZ - dz), NZ), land, centre, count, *refs)
        for dz in tiles:
            prepare_halo(rem(z + (NZ - dz), NZ), halo, shifts, *refs)
    forces(
        neighbours, count, lefts, lefts_t, rights, places, even, odd, force, r1b, near, sems[10:14]
    )
    backward_scan(r1b, near, t2b, r2b, plain_in, pxb, out, sems[10:])
    finish()


def leapfrog(section, momentum, section_force):
    level = lax.axis_index("bead").astype(F32)
    safe = jnp.maximum(level, 1.0)
    section_force = section_force / safe
    mass = jnp.where(level > 0, (level + 1.0) / safe, 1.0)
    spring = jnp.where(level > 0, omega_sq * mass, 0.0)
    step = time_step / 3.0
    push = 0.5 * step * spring
    drift = step / mass
    p = momentum + (0.5 * time_step) * section_force
    u = section
    for turn in range(3):
        p = p - push * u
        u = u + drift * p
        p = p - push * u
    return u, p


def step(section, momentum, neighbours, border_rows, counts):
    shape = section.shape
    listed = neighbours.shape[2]
    tiles = shape[2] // TILE
    tpc = tiles // NZ
    dense = (3, NZ, tpc, TILE)
    ext_tiles = tiles + NZ
    chunk, wide = (3, tpc, TILE), (4, tpc, TILE)
    anywhere = pl.BlockSpec(memory_space=pl.ANY)
    in_hbm = pl.BlockSpec(memory_space=pltpu.HBM)
    hbm = lambda array: pltpu.with_memory_space_constraint(array, pltpu.HBM)
    vmem = lambda *dims: pltpu.VMEM(dims, F32)
    scan_buffers = [
        vmem(count, *part)
        for part in (wide, chunk)
        for count in (NZ * NY, 2, NX, NX, NZ)
    ]
    one, each = DMA((1,)), DMA((NZ,))
    section, momentum = section.reshape(dense), momentum.reshape(dense)
    section_force = pl.pallas_call(
        kernel,
        out_shape=jax.ShapeDtypeStruct(dense, F32),
        in_specs=[
            pl.BlockSpec(memory_space=pltpu.SMEM),
            in_hbm,
            in_hbm,
            in_hbm,
        ],
        out_specs=anywhere,
        scratch_shapes=[
            pltpu.SMEM((listed, tiles), jnp.int32),
            pltpu.VMEM(border_rows.shape[1:], jnp.int32),
            vmem(*dense),
            vmem(NZ, *wide),
            vmem(NZ, *chunk),
            vmem(NZ, 4, TILE),
            vmem(NZ, *chunk),
            pltpu.VMEM((ext_tiles, KROWS, TILE), BF16),
            pltpu.VMEM((ext_tiles, TILE, KROWS), BF16),
            pltpu.VMEM((tiles, KROWS, TILE), BF16),
            vmem(tiles, 8, TILE),
            vmem(listed * TILE, TILE),
            vmem(listed * TILE, TILE),
        ]
        + scan_buffers
        + [vmem(len(near_slots()), *chunk)]
        + [DMA((3,))]
        + [one] * 6
        + [one, each] * 2
        + [one, DMA((2,))]
        + [one] * 9,
        compiler_params=pltpu.CompilerParams(
            collective_id=0, has_side_effects=True, vmem_limit_bytes=24 * 2**20
        ),
        name="path_step",
    )(
        counts,
        hbm(neighbours.transpose(0, 2, 1).reshape(listed, tiles)),
        hbm(border_rows.reshape(border_rows.shape[1:])),
        hbm(section),
    )
    u, p = leapfrog(section, momentum, section_force)
    return u.reshape(shape), p.reshape(shape)


def solution(mesh):
    return jax.shard_map(
        step,
        mesh=mesh,
        in_specs=(
            P("bead", None, "slab"),
            P("bead", None, "slab"),
            P("slab", None, None),
            P("slab", None, None),
            P("slab"),
        ),
        out_specs=(P("bead", None, "slab"), P("bead", None, "slab")),
        check_vma=False,
    )
```

```python
import functools
import math

import jax
import jax.numpy as jnp
from jax import lax
from jax.experimental import pallas as pl
from jax.experimental.pallas import tpu as pltpu
from jax.sharding import PartitionSpec as P

MESH = pl.DeviceIdType.MESH
time_step = 0.1
omega_sq = 4.0
slab_width = 3.0
reach_sq = 17.0
shrink = 1.0 / math.sqrt(reach_sq)
NX, NZ, NY = 4, 8, 2
TILE = 128
KROWS = 32
F32 = jnp.float32
BF16 = jnp.bfloat16
DMA = pltpu.SemaphoreType.DMA


def rem(value, size):
    return lax.rem(value, jnp.int32(size))


def place():
    bead = lax.axis_index("bead")
    return lax.div(bead, jnp.int32(NZ * NY)), rem(lax.div(bead, jnp.int32(NY)), NZ), rem(bead, NY)


def bead_of(x, z, y):
    return (x * NZ + z) * NY + y


def to_bead(bead):
    return (bead, lax.axis_index("slab"))


def group_steps():
    return [(dz, dy) for dz in range(NZ) for dy in range(NY) if dz or dy]


def reach(dz):
    return min(dz, NZ - dz)


def partners():
    x, z, y = place()
    slab, slabs = lax.axis_index("slab"), lax.axis_size("slab")
    found = []
    for dz in sorted(range(NZ), key=reach, reverse=True):
        tz = rem(z + dz, NZ)
        found += [to_bead(bead_of(x, tz, rem(y + dy, NY))) for dy in reversed(range(NY)) if dz or dy]
        found += [(bead_of(x, tz, y), rem(slab + ds, slabs)) for ds in (1, slabs - 1)]
    return found + [to_bead(bead_of(rem(x + dx, NX), z, y)) for dx in range(1, NX)]


def remote(src, dst, send_sem, recv_sem, device):
    return pltpu.make_async_remote_copy(
        src_ref=src,
        dst_ref=dst,
        send_sem=send_sem,
        recv_sem=recv_sem,
        device_id=device,
        device_id_type=MESH,
    )


def send(*args):
    copy = remote(*args)
    copy.start()
    return copy


def await_bytes(ref, sem):
    pltpu.make_async_copy(ref, ref, sem).wait()


def group_copy(src, r1, send_sem, recv_sem, dz, dy, kind=0):
    x, z, y = place()
    device = to_bead(bead_of(x, rem(z + dz, NZ), rem(y + dy, NY)))
    return remote(src, r1.at[dz * NY + dy], send_sem.at[0], recv_sem.at[kind], device)


def near_offsets():
    return (NZ - 2, 1, NZ - 1, 0) if NZ > 4 else (1, NZ - 1, 0)


def near_slots():
    return [(dx, k, dy) for dx in range(1, NX) for k in range(len(near_offsets())) for dy in range(NY)]


def near_slot(dx, k, dy):
    return ((dx - 1) * len(near_offsets()) + k) * NY + dy


def exchange_x(src, slots, send_sem, recv_sem):
    x, z, y = place()
    for dx in range(1, NX):
        device = to_bead(bead_of(rem(x + dx, NX), z, y))
        send(src, slots.at[dx], send_sem.at[0], recv_sem.at[0], device)


def level_rows(bead):
    return jnp.full((1, 1, TILE), bead.astype(F32), F32)


def slot_from(zs, ys):
    x, z, y = place()
    return rem(z + (NZ - zs), NZ) * NY + rem(y + (NY - ys), NY)


def near_first():
    return sorted(range(1, NZ), key=reach)


def forward_scan(raw, r1, t2, r2, first_in, px, land, halo, sems):
    s1, q1, s2, q2, sf, qf, s3, q3, s4, q4 = sems
    x, z, y = place()
    slab, slabs = lax.axis_index("slab"), lax.axis_size("slab")
    for dz, dy in sorted(group_steps(), key=lambda step: -reach(step[0]) - step[1]):
        group_copy(raw.at[rem(z + dz, NZ)], r1, s1, q1, dz, dy).start()
    r1[0] = raw[z]
    await_bytes(r1.at[1:], q1.at[0])

    @pl.when(x == 0)
    def _():
        for dx in range(1, NX):
            device = to_bead(bead_of(dx, z, y))
            send(r1.at[slot_from(0, 0)], first_in.at[0], sf.at[0], qf.at[0], device)
        first_in[0] = r1[slot_from(0, 0)]

    total = jnp.zeros(r1.shape[1:], F32)
    for zs in reversed(range(NZ)):
        kept = None
        for ys in reversed(range(NY)):
            one = r1[slot_from(zs, ys)]
            if zs == 0 and ys == 0:
                one = jnp.where(x == 0, 0.0, one)
            total = total + one
            kept = total if kept is None else jnp.where(y == ys, total, kept)
        px[zs] = kept
    t2[0] = total
    exchange_x(t2.at[0], r2, s2, q2)

    @pl.when(x != 0)
    def _():
        await_bytes(first_in.at[0], qf.at[0])

    await_bytes(r2.at[1:], q2.at[0])
    base = jnp.zeros(r1.shape[1:], F32)
    for dx in range(1, NX):
        xs = rem(x + (NX - dx), NX)
        base = base + jnp.where(xs > x, r2[dx], 0.0)
    first = first_in[0]
    beside = rem(slab + 1 + (slabs - 2) * lax.div(z, jnp.int32(NZ // 2)), slabs)
    for dz in near_first()[::-1] + [0]:
        tz = rem(z + dz, NZ)
        bead = bead_of(x, tz, y)
        places = first + level_rows(bead) * (px[tz] + base)
        px[tz] = places
        send(px.at[tz, 3], halo.at[z], s4.at[0], q4.at[dz], (bead, beside))
        if dz:
            send(px.at[tz, 0:3], land.at[z], s3.at[0], q3.at[dz], to_bead(bead))
        else:
            land[z] = places[0:3]

    def finish():
        await_bytes(r1.at[1:], s1.at[0])
        await_bytes(r2.at[1:], s2.at[0])
        await_bytes(land.at[1:], s3.at[0])
        await_bytes(halo, s4.at[0])

        @pl.when(x == 0)
        def _():
            await_bytes(r2.at[1:], sf.at[0])

    return finish


def backward_scan(r1, near, t2, r2, plain_in, px, out, sems):
    s1, q1, sn, qn, s2, q2, sf, qf, s3, q3, own_sem = sems
    x, z, y = place()
    far = [(dz, dy) for dz in range(NZ) for dy in range(NY) if dz not in near_offsets()]
    await_bytes(r1.at[0 : len(far)], q1.at[0])
    total = jnp.zeros(r1.shape[1:], F32)
    plain = jnp.zeros(r1.shape[1:], F32)
    for dz, dy in far:
        one = r1[dz * NY + dy]
        plain = plain + one
        total = total + one * level_rows(bead_of(x, rem(z + (NZ - dz), NZ), rem(y + (NY - dy), NY)))
    t2[0] = total
    t2[1] = plain
    exchange_x(t2.at[0], r2, s2, q2)

    @pl.when(x != 0)
    def _():
        send(t2.at[1], plain_in.at[x], sf.at[0], qf.at[0], to_bead(bead_of(0, z, y)))

    await_bytes(r1.at[0 : len(group_steps()) - len(far)], q1.at[1])
    total = jnp.zeros(r1.shape[1:], F32)
    plain = jnp.zeros(r1.shape[1:], F32)
    for zs in range(NZ):
        kept = None
        for ys in range(NY):
            one = r1[slot_from(zs, ys)]
            plain = plain + one
            total = total + one * level_rows(bead_of(x, zs, ys))
            kept = total if kept is None else jnp.where(y == ys, total, kept)
        px[zs] = kept
    await_bytes(near, qn.at[0])
    base = jnp.zeros(r1.shape[1:], F32)
    for dx, k, dy in near_slots():
        xs = rem(x + (NX - dx), NX)
        source = bead_of(xs, rem(z + (NZ - near_offsets()[k]), NZ), rem(y + (NY - dy), NY))
        one = near[near_slot(dx, k, dy)]
        plain = plain + one
        base = base + jnp.where(xs < x, one * level_rows(source), 0.0)

    @pl.when(x == 0)
    def _():
        plain_in[0] = plain
        await_bytes(plain_in.at[1:], qf.at[0])

    await_bytes(r2.at[1:], q2.at[0])
    for dx in range(1, NX):
        xs = rem(x + (NX - dx), NX)
        base = base + jnp.where(xs < x, r2[dx], 0.0)
    for zs in range(NZ):
        px[zs] = px[zs] + base

    @pl.when((x == 0) & (y == 0))
    def _():
        everything = plain_in[0]
        for xs in range(1, NX):
            everything = everything + plain_in[xs]
        px[0] = everything

    for dz in near_first()[::-1] + [0]:
        tz = rem(z + dz, NZ)
        if dz:
            device = to_bead(bead_of(x, tz, y))
            send(px.at[tz], out.at[:, z], s3.at[0], q3.at[0], device)
        else:
            own = pltpu.make_async_copy(px.at[tz], out.at[:, z], own_sem.at[0])
            own.start()

    await_bytes(px.at[1:], q3.at[0])
    own.wait()
    await_bytes(r1.at[1:], s1.at[0])
    await_bytes(near, sn.at[0])
    await_bytes(r2.at[1:], s2.at[0])
    await_bytes(px.at[1:], s3.at[0])

    @pl.when(x != 0)
    def _():
        await_bytes(t2.at[1], sf.at[0])


def pack_chunks(section, border, raw):
    level = level_rows(lax.axis_index("bead"))
    inverse = 1.0 / jnp.maximum(level, 1.0)
    tpc = section.shape[2]
    sub = lax.broadcasted_iota(jnp.int32, (8, TILE), 0)
    blocks = NZ // 2 * tpc // 8
    for z in range(NZ):
        raw[z, 0:3] = section[:, z] * inverse
    pieces = []
    for c in range(3):
        for b in range(blocks):
            rows = [section[c, b * (8 // tpc) + m] for m in range(8 // tpc)]
            pieces.append(jnp.concatenate(rows, axis=0))
    half = NZ // 2
    for z in range(NZ):
        k, n = z // half, z % half
        index = jnp.broadcast_to(border[k : k + 1, n * TILE : (n + 1) * TILE], (8, TILE))
        lane, block = index % TILE, index // TILE
        rows = []
        for c in range(3):
            out = jnp.zeros((8, TILE), F32)
            for b in range(blocks):
                taken = jnp.take_along_axis(
                    pieces[c * blocks + b], lane, axis=1, mode="promise_in_bounds"
                )
                out = jnp.where(block == b * 8 + sub, taken, out)
            rows.append(jnp.sum(out, axis=0, keepdims=True))
        raw[z, 3] = jnp.concatenate(rows + [jnp.zeros((1, TILE), F32)], axis=0) * inverse[0]


def split3(value):
    high = value.astype(BF16).astype(F32)
    rest = value - high
    middle = rest.astype(BF16).astype(F32)
    return high, middle, rest - middle


def prepare_tile(t, rows, shift, own, lefts, lefts_t, rights, places, row, count):
    sub = lax.broadcasted_iota(jnp.int32, (8, TILE), 0)
    comp = sub % 4
    xs = [jnp.broadcast_to(v, (8, TILE)) for v in rows]
    xs = [(v - w) * shrink for v, w in zip(xs, (shift, 0.5 * slab_width, 0.5 * slab_width))]
    p = jnp.where(comp == 0, xs[0], jnp.where(comp == 1, xs[1], xs[2]))
    norm = xs[0] * xs[0] + xs[1] * xs[1] + xs[2] * xs[2]
    far = norm
    if own is not None:
        place_in = row + lax.broadcasted_iota(jnp.int32, (8, TILE), 1)
        far = jnp.where(place_in < count, norm, 4096.0)
    high, middle, low = split3(p)
    fh, fm, fl = split3(far)
    last, top = comp == 3, sub < 4
    a0 = jnp.where(last, jnp.where(top, fh, fm), high)
    a1 = jnp.where(last, jnp.where(top, fl, 1.0), middle)
    a2 = jnp.where(last, 1.0, jnp.where(top, low, high))
    left = jnp.concatenate([a0, a1, a2, jnp.zeros((8, TILE), F32)], axis=0)
    lefts[t] = left.astype(BF16)
    lefts_t[t] = left.T.astype(BF16)
    if own is not None:
        nh, nm, nl = split3(norm + 1.0 / reach_sq)
        h2, m2, l2 = -2.0 * high, -2.0 * middle, -2.0 * low
        b0 = jnp.where(last, 1.0, jnp.where(top, h2, m2))
        b1 = jnp.where(last, jnp.where(top, 1.0, nh), jnp.where(top, h2, m2))
        b2 = jnp.where(last, jnp.where(top, nm, nl), jnp.where(top, h2, l2))
        right = jnp.concatenate([b0, b1, b2, jnp.zeros((8, TILE), F32)], axis=0)
        rights[own] = right.astype(BF16)
        places[own] = p


def prepare_own(z, land, centre, count, *refs):
    half, tpc = NZ // 2, refs[2].shape[0] // NZ
    for n in range(tpc):
        rows = [land[z, c, n : n + 1, :] for c in range(3)]
        i = z * tpc + n
        prepare_tile(half + i, rows, centre, i, *refs, i * TILE, count)


def prepare_halo(z, halo, shifts, *refs):
    half, tiles = NZ // 2, refs[2].shape[0]
    upper = lax.div(z, jnp.int32(half))
    rows = [halo[z, c : c + 1, :] for c in range(3)]
    shift = jnp.where(upper == 0, shifts[0], shifts[1])
    prepare_tile(z + upper * tiles, rows, shift, None, *refs, 0, 0)


def quotients(i, buf, neighbours, lefts_t, rights):
    right = rights[i]
    for n in range(neighbours.shape[0]):
        buf[n * TILE : (n + 1) * TILE, :] = jnp.dot(
            lefts_t[neighbours[n, i]], right, preferred_element_type=F32
        )


def tile_force(i, zc, n, buf, neighbours, lefts, places, force, count):
    total = jnp.zeros((KROWS, TILE), F32)
    for k in range(0, neighbours.shape[0], 2):
        q = buf[k * TILE : (k + 2) * TILE, :]
        r = 1.0 / q
        r2 = r * r
        d = jnp.maximum(r2 - r, 0.0)
        f = ((d * d) * (r2 * r - 0.5 * reach_sq**3)).astype(BF16)
        x = jnp.concatenate([lefts[neighbours[k, i]], lefts[neighbours[k + 1, i]]], axis=1)
        total = total + jnp.dot(x, f, preferred_element_type=F32)
    moved = total[0:8] + total[8:16] + total[16:24]
    row = i * TILE + lax.broadcasted_iota(jnp.int32, (8, TILE), 1)
    beads = lax.axis_size("bead")
    scale = jnp.where(row < count, 48.0 / 256.0 / reach_sq**5 / shrink / beads, 0.0)
    result = (places[i] * total[15:16] - moved) * scale
    for c in range(3):
        force[zc, c, n : n + 1, :] = result[c : c + 1]


def forces(neighbours, count, lefts, lefts_t, rights, places, even, odd, force, r1, near, sems):
    x, z, y = place()
    tpc = rights.shape[0] // NZ
    half = NZ // 2
    bufs = (even, odd)
    send_sem, recv_sem, near_send, near_recv = sems

    def offset(c):
        return half + lax.div(c, jnp.int32(2)) * (1 - rem(c, 2)) - lax.div(c + 1, jnp.int32(2)) * rem(c, 2)

    quotients(rem(z + half, NZ) * tpc, even, neighbours, lefts_t, rights)

    def chunk(c, carry):
        dz = offset(c)
        zc = rem(z + dz, NZ)
        after = rem(z + offset(jnp.minimum(c + 1, NZ - 1)), NZ)
        for n in range(tpc):
            following = zc * tpc + n + 1 if n + 1 < tpc else after * tpc
            quotients(following, bufs[(n + 1) % 2], neighbours, lefts_t, rights)
            tile_force(zc * tpc + n, zc, n, bufs[n % 2], neighbours, lefts, places, force, count)
        first_near = NZ - len(near_offsets())
        kind = jnp.minimum(jnp.maximum(c - first_near + 1, 0), 1)
        group_copy(force.at[zc], r1, send_sem, recv_sem, dz, 1, kind).start()

        @pl.when(c < NZ - 1)
        def _():
            group_copy(force.at[zc], r1, send_sem, recv_sem, dz, 0, kind).start()

        @pl.when(c >= first_near)
        def _():
            for dx in range(1, NX):
                for dy in range(NY):
                    device = to_bead(bead_of(rem(x + dx, NX), zc, rem(y + dy, NY)))
                    slot = near_slot(dx, c - first_near, dy)
                    send(force.at[zc], near.at[slot], near_send.at[0], near_recv.at[0], device)

        return carry

    lax.fori_loop(0, NZ, chunk, 0)
    r1[0] = force[z]


def kernel(
    counts, neighbours_in, border_in, section_in, out,
    neighbours, border, section, raw, land, halo, force,
    lefts, lefts_t, rights, places, even, odd,
    r1f, t2f, r2f, first_in, pxf, r1b, t2b, r2b, plain_in, pxb, near,
    load_sem, *sems,
):
    x, z, y = place()
    slab, slabs = lax.axis_index("slab"), lax.axis_size("slab")
    loads = [
        pltpu.make_async_copy(section_in, section, load_sem.at[0]),
        pltpu.make_async_copy(border_in, border, load_sem.at[1]),
        pltpu.make_async_copy(neighbours_in, neighbours, load_sem.at[2]),
    ]
    barrier = pltpu.get_barrier_semaphore()
    greeted = partners()
    for device in greeted:
        pl.semaphore_signal(barrier, inc=1, device_id=device, device_id_type=MESH)
    for load in loads:
        load.start()
    for load in loads:
        load.wait()
    pack_chunks(section, border, raw)
    pl.semaphore_wait(barrier, len(greeted))
    finish = forward_scan(raw, r1f, t2f, r2f, first_in, pxf, land, halo, sems[:10])
    q3, q4 = sems[7], sems[9]
    count = counts[0]
    box = slab_width * slabs
    centre = (slab.astype(F32) + 0.5) * slab_width
    shifts = (
        centre + jnp.where(slab == 0, box, 0.0),
        centre - jnp.where(slab == slabs - 1, box, 0.0),
    )
    refs = (lefts, lefts_t, rights, places)
    farthest = NZ // 2
    for distance in range(farthest + 1):
        chunks = [dz for dz in range(NZ) if reach(dz) == distance]
        tiles = [dz for dz in range(NZ) if reach(dz) == distance - 1]
        if distance == farthest:
            tiles += chunks
        for dz in chunks:
            if dz:
                await_bytes(land.at[0], q3.at[dz])
        for dz in tiles:
            await_bytes(halo.at[0], q4.at[dz])
        for dz in chunks:
            prepare_own(rem(z + (NZ - dz), NZ), land, centre, count, *refs)
        for dz in tiles:
            prepare_halo(rem(z + (NZ - dz), NZ), halo, shifts, *refs)
    forces(
        neighbours, count, lefts, lefts_t, rights, places, even, odd, force, r1b, near, sems[10:14]
    )
    backward_scan(r1b, near, t2b, r2b, plain_in, pxb, out, sems[10:])
    finish()


def leapfrog(section, momentum, section_force):
    level = lax.axis_index("bead").astype(F32)
    safe = jnp.maximum(level, 1.0)
    section_force = section_force / safe
    mass = jnp.where(level > 0, (level + 1.0) / safe, 1.0)
    spring = jnp.where(level > 0, omega_sq * mass, 0.0)
    step = time_step / 3.0
    push = 0.5 * step * spring
    drift = step / mass
    p = momentum + (0.5 * time_step) * section_force
    u = section
    for turn in range(3):
        p = p - push * u
        u = u + drift * p
        p = p - push * u
    return u, p


def step(section, momentum, neighbours, border_rows, counts):
    shape = section.shape
    listed = neighbours.shape[2]
    tiles = shape[2] // TILE
    tpc = tiles // NZ
    dense = (3, NZ, tpc, TILE)
    ext_tiles = tiles + NZ
    chunk, wide = (3, tpc, TILE), (4, tpc, TILE)
    anywhere = pl.BlockSpec(memory_space=pl.ANY)
    in_hbm = pl.BlockSpec(memory_space=pltpu.HBM)
    hbm = lambda array: pltpu.with_memory_space_constraint(array, pltpu.HBM)
    vmem = lambda *dims: pltpu.VMEM(dims, F32)
    scan_buffers = [
        vmem(count, *part)
        for part in (wide, chunk)
        for count in (NZ * NY, 2, NX, NX, NZ)
    ]
    one, each = DMA((1,)), DMA((NZ,))
    section, momentum = section.reshape(dense), momentum.reshape(dense)
    section_force = pl.pallas_call(
        kernel,
        out_shape=jax.ShapeDtypeStruct(dense, F32),
        in_specs=[
            pl.BlockSpec(memory_space=pltpu.SMEM),
            in_hbm,
            in_hbm,
            in_hbm,
        ],
        out_specs=anywhere,
        scratch_shapes=[
            pltpu.SMEM((listed, tiles), jnp.int32),
            pltpu.VMEM(border_rows.shape[1:], jnp.int32),
            vmem(*dense),
            vmem(NZ, *wide),
            vmem(NZ, *chunk),
            vmem(NZ, 4, TILE),
            vmem(NZ, *chunk),
            pltpu.VMEM((ext_tiles, KROWS, TILE), BF16),
            pltpu.VMEM((ext_tiles, TILE, KROWS), BF16),
            pltpu.VMEM((tiles, KROWS, TILE), BF16),
            vmem(tiles, 8, TILE),
            vmem(listed * TILE, TILE),
            vmem(listed * TILE, TILE),
        ]
        + scan_buffers
        + [vmem(len(near_slots()), *chunk)]
        + [DMA((3,))]
        + [one] * 6
        + [one, each] * 2
        + [one, DMA((2,))]
        + [one] * 9,
        compiler_params=pltpu.CompilerParams(
            collective_id=0, has_side_effects=True, vmem_limit_bytes=24 * 2**20
        ),
        name="path_step",
    )(
        counts,
        hbm(neighbours.transpose(0, 2, 1).reshape(listed, tiles)),
        hbm(border_rows.reshape(border_rows.shape[1:])),
        hbm(section),
    )
    u, p = leapfrog(section, momentum, section_force)
    return u.reshape(shape), p.reshape(shape)


def solution(mesh):
    return jax.shard_map(
        step,
        mesh=mesh,
        in_specs=(
            P("bead", None, "slab"),
            P("bead", None, "slab"),
            P("slab", None, None),
            P("slab", None, None),
            P("slab"),
        ),
        out_specs=(P("bead", None, "slab"), P("bead", None, "slab")),
        check_vma=False,
    )
```

```python
import functools
import math

import jax
import jax.numpy as jnp
from jax import lax
from jax.experimental import pallas as pl
from jax.experimental.pallas import tpu as pltpu
from jax.sharding import PartitionSpec as P

MESH = pl.DeviceIdType.MESH
time_step = 0.1
omega_sq = 4.0
slab_width = 3.0
reach_sq = 17.0
shrink = 1.0 / math.sqrt(reach_sq)
NX, NZ, NY = 4, 8, 2
TILE = 128
KROWS = 32
F32 = jnp.float32
BF16 = jnp.bfloat16
DMA = pltpu.SemaphoreType.DMA


def rem(value, size):
    return lax.rem(value, jnp.int32(size))


def place():
    bead = lax.axis_index("bead")
    return lax.div(bead, jnp.int32(NZ * NY)), rem(lax.div(bead, jnp.int32(NY)), NZ), rem(bead, NY)


def bead_of(x, z, y):
    return (x * NZ + z) * NY + y


def to_bead(bead):
    return (bead, lax.axis_index("slab"))


def group_steps():
    return [(dz, dy) for dz in range(NZ) for dy in range(NY) if dz or dy]


def reach(dz):
    return min(dz, NZ - dz)


def partners():
    x, z, y = place()
    slab, slabs = lax.axis_index("slab"), lax.axis_size("slab")
    found = []
    for dz in sorted(range(NZ), key=reach, reverse=True):
        tz = rem(z + dz, NZ)
        found += [to_bead(bead_of(x, tz, rem(y + dy, NY))) for dy in reversed(range(NY)) if dz or dy]
        found += [(bead_of(x, tz, y), rem(slab + ds, slabs)) for ds in (1, slabs - 1)]
    return found + [to_bead(bead_of(rem(x + dx, NX), z, y)) for dx in range(1, NX)]


def remote(src, dst, send_sem, recv_sem, device):
    return pltpu.make_async_remote_copy(
        src_ref=src,
        dst_ref=dst,
        send_sem=send_sem,
        recv_sem=recv_sem,
        device_id=device,
        device_id_type=MESH,
    )


def send(*args):
    copy = remote(*args)
    copy.start()
    return copy


def await_bytes(ref, sem):
    pltpu.make_async_copy(ref, ref, sem).wait()


def group_copy(src, r1, send_sem, recv_sem, dz, dy, kind=0):
    x, z, y = place()
    device = to_bead(bead_of(x, rem(z + dz, NZ), rem(y + dy, NY)))
    return remote(src, r1.at[dz * NY + dy], send_sem.at[0], recv_sem.at[kind], device)


def near_offsets():
    return (NZ - 2, 1, NZ - 1, 0) if NZ > 4 else (1, NZ - 1, 0)


def near_slots():
    return [(dx, k, dy) for dx in range(1, NX) for k in range(len(near_offsets())) for dy in range(NY)]


def near_slot(dx, k, dy):
    return ((dx - 1) * len(near_offsets()) + k) * NY + dy


def exchange_x(src, slots, send_sem, recv_sem):
    x, z, y = place()
    for dx in range(1, NX):
        device = to_bead(bead_of(rem(x + dx, NX), z, y))
        send(src, slots.at[dx], send_sem.at[0], recv_sem.at[0], device)


def level_rows(bead):
    return jnp.full((1, 1, TILE), bead.astype(F32), F32)


def slot_from(zs, ys):
    x, z, y = place()
    return rem(z + (NZ - zs), NZ) * NY + rem(y + (NY - ys), NY)


def near_first():
    return sorted(range(1, NZ), key=reach)


def forward_scan(raw, r1, t2, r2, first_in, px, land, halo, sems):
    s1, q1, s2, q2, sf, qf, s3, q3, s4, q4 = sems
    x, z, y = place()
    slab, slabs = lax.axis_index("slab"), lax.axis_size("slab")
    for dz, dy in sorted(group_steps(), key=lambda step: -reach(step[0]) - step[1]):
        group_copy(raw.at[rem(z + dz, NZ)], r1, s1, q1, dz, dy).start()
    r1[0] = raw[z]
    await_bytes(r1.at[1:], q1.at[0])

    @pl.when(x == 0)
    def _():
        for dx in range(1, NX):
            device = to_bead(bead_of(dx, z, y))
            send(r1.at[slot_from(0, 0)], first_in.at[0], sf.at[0], qf.at[0], device)
        first_in[0] = r1[slot_from(0, 0)]

    total = jnp.zeros(r1.shape[1:], F32)
    for zs in reversed(range(NZ)):
        kept = None
        for ys in reversed(range(NY)):
            one = r1[slot_from(zs, ys)]
            if zs == 0 and ys == 0:
                one = jnp.where(x == 0, 0.0, one)
            total = total + one
            kept = total if kept is None else jnp.where(y == ys, total, kept)
        px[zs] = kept
    t2[0] = total
    exchange_x(t2.at[0], r2, s2, q2)

    @pl.when(x != 0)
    def _():
        await_bytes(first_in.at[0], qf.at[0])

    await_bytes(r2.at[1:], q2.at[0])
    base = jnp.zeros(r1.shape[1:], F32)
    for dx in range(1, NX):
        xs = rem(x + (NX - dx), NX)
        base = base + jnp.where(xs > x, r2[dx], 0.0)
    first = first_in[0]
    beside = rem(slab + 1 + (slabs - 2) * lax.div(z, jnp.int32(NZ // 2)), slabs)
    for dz in near_first()[::-1] + [0]:
        tz = rem(z + dz, NZ)
        bead = bead_of(x, tz, y)
        places = first + level_rows(bead) * (px[tz] + base)
        px[tz] = places
        send(px.at[tz, 3], halo.at[z], s4.at[0], q4.at[dz], (bead, beside))
        if dz:
            send(px.at[tz, 0:3], land.at[z], s3.at[0], q3.at[dz], to_bead(bead))
        else:
            land[z] = places[0:3]

    def finish():
        await_bytes(r1.at[1:], s1.at[0])
        await_bytes(r2.at[1:], s2.at[0])
        await_bytes(land.at[1:], s3.at[0])
        await_bytes(halo, s4.at[0])

        @pl.when(x == 0)
        def _():
            await_bytes(r2.at[1:], sf.at[0])

    return finish


def backward_scan(r1, near, t2, r2, plain_in, px, out, sems):
    s1, q1, sn, qn, s2, q2, sf, qf, s3, q3, own_sem = sems
    x, z, y = place()
    far = [(dz, dy) for dz in range(NZ) for dy in range(NY) if dz not in near_offsets()]
    await_bytes(r1.at[0 : len(far)], q1.at[0])
    total = jnp.zeros(r1.shape[1:], F32)
    plain = jnp.zeros(r1.shape[1:], F32)
    for dz, dy in far:
        one = r1[dz * NY + dy]
        plain = plain + one
        total = total + one * level_rows(bead_of(x, rem(z + (NZ - dz), NZ), rem(y + (NY - dy), NY)))
    t2[0] = total
    t2[1] = plain
    exchange_x(t2.at[0], r2, s2, q2)

    @pl.when(x != 0)
    def _():
        send(t2.at[1], plain_in.at[x], sf.at[0], qf.at[0], to_bead(bead_of(0, z, y)))

    await_bytes(r1.at[0 : len(group_steps()) - len(far)], q1.at[1])
    total = jnp.zeros(r1.shape[1:], F32)
    plain = jnp.zeros(r1.shape[1:], F32)
    for zs in range(NZ):
        kept = None
        for ys in range(NY):
            one = r1[slot_from(zs, ys)]
            plain = plain + one
            total = total + one * level_rows(bead_of(x, zs, ys))
            kept = total if kept is None else jnp.where(y == ys, total, kept)
        px[zs] = kept
    await_bytes(near, qn.at[0])
    base = jnp.zeros(r1.shape[1:], F32)
    for dx, k, dy in near_slots():
        xs = rem(x + (NX - dx), NX)
        source = bead_of(xs, rem(z + (NZ - near_offsets()[k]), NZ), rem(y + (NY - dy), NY))
        one = near[near_slot(dx, k, dy)]
        plain = plain + one
        base = base + jnp.where(xs < x, one * level_rows(source), 0.0)

    @pl.when(x == 0)
    def _():
        plain_in[0] = plain
        await_bytes(plain_in.at[1:], qf.at[0])

    await_bytes(r2.at[1:], q2.at[0])
    for dx in range(1, NX):
        xs = rem(x + (NX - dx), NX)
        base = base + jnp.where(xs < x, r2[dx], 0.0)
    for zs in range(NZ):
        px[zs] = px[zs] + base

    @pl.when((x == 0) & (y == 0))
    def _():
        everything = plain_in[0]
        for xs in range(1, NX):
            everything = everything + plain_in[xs]
        px[0] = everything

    for dz in near_first()[::-1] + [0]:
        tz = rem(z + dz, NZ)
        if dz:
            device = to_bead(bead_of(x, tz, y))
            send(px.at[tz], out.at[:, z], s3.at[0], q3.at[0], device)
        else:
            own = pltpu.make_async_copy(px.at[tz], out.at[:, z], own_sem.at[0])
            own.start()

    await_bytes(px.at[1:], q3.at[0])
    own.wait()
    await_bytes(r1.at[1:], s1.at[0])
    await_bytes(near, sn.at[0])
    await_bytes(r2.at[1:], s2.at[0])
    await_bytes(px.at[1:], s3.at[0])

    @pl.when(x != 0)
    def _():
        await_bytes(t2.at[1], sf.at[0])


def pack_chunks(section, border, raw):
    level = level_rows(lax.axis_index("bead"))
    inverse = 1.0 / jnp.maximum(level, 1.0)
    tpc = section.shape[2]
    sub = lax.broadcasted_iota(jnp.int32, (8, TILE), 0)
    blocks = NZ // 2 * tpc // 8
    for z in range(NZ):
        raw[z, 0:3] = section[:, z] * inverse
    pieces = []
    for c in range(3):
        for b in range(blocks):
            rows = [section[c, b * (8 // tpc) + m] for m in range(8 // tpc)]
            pieces.append(jnp.concatenate(rows, axis=0))
    half = NZ // 2
    for z in range(NZ):
        k, n = z // half, z % half
        index = jnp.broadcast_to(border[k : k + 1, n * TILE : (n + 1) * TILE], (8, TILE))
        lane, block = index % TILE, index // TILE
        rows = []
        for c in range(3):
            out = jnp.zeros((8, TILE), F32)
            for b in range(blocks):
                taken = jnp.take_along_axis(
                    pieces[c * blocks + b], lane, axis=1, mode="promise_in_bounds"
                )
                out = jnp.where(block == b * 8 + sub, taken, out)
            rows.append(jnp.sum(out, axis=0, keepdims=True))
        raw[z, 3] = jnp.concatenate(rows + [jnp.zeros((1, TILE), F32)], axis=0) * inverse[0]


def split3(value):
    high = value.astype(BF16).astype(F32)
    rest = value - high
    middle = rest.astype(BF16).astype(F32)
    return high, middle, rest - middle


def prepare_tile(t, rows, shift, own, lefts, lefts_t, rights, places, row, count):
    sub = lax.broadcasted_iota(jnp.int32, (8, TILE), 0)
    comp = sub % 4
    xs = [jnp.broadcast_to(v, (8, TILE)) for v in rows]
    xs = [(v - w) * shrink for v, w in zip(xs, (shift, 0.5 * slab_width, 0.5 * slab_width))]
    p = jnp.where(comp == 0, xs[0], jnp.where(comp == 1, xs[1], xs[2]))
    norm = xs[0] * xs[0] + xs[1] * xs[1] + xs[2] * xs[2]
    far = norm
    if own is not None:
        place_in = row + lax.broadcasted_iota(jnp.int32, (8, TILE), 1)
        far = jnp.where(place_in < count, norm, 4096.0)
    high, middle, low = split3(p)
    fh, fm, fl = split3(far)
    last, top = comp == 3, sub < 4
    a0 = jnp.where(last, jnp.where(top, fh, fm), high)
    a1 = jnp.where(last, jnp.where(top, fl, 1.0), middle)
    a2 = jnp.where(last, 1.0, jnp.where(top, low, high))
    left = jnp.concatenate([a0, a1, a2, jnp.zeros((8, TILE), F32)], axis=0)
    lefts[t] = left.astype(BF16)
    lefts_t[t] = left.T.astype(BF16)
    if own is not None:
        nh, nm, nl = split3(norm + 1.0 / reach_sq)
        h2, m2, l2 = -2.0 * high, -2.0 * middle, -2.0 * low
        b0 = jnp.where(last, 1.0, jnp.where(top, h2, m2))
        b1 = jnp.where(last, jnp.where(top, 1.0, nh), jnp.where(top, h2, m2))
        b2 = jnp.where(last, jnp.where(top, nm, nl), jnp.where(top, h2, l2))
        right = jnp.concatenate([b0, b1, b2, jnp.zeros((8, TILE), F32)], axis=0)
        rights[own] = right.astype(BF16)
        places[own] = p


def prepare_own(z, land, centre, count, *refs):
    half, tpc = NZ // 2, refs[2].shape[0] // NZ
    for n in range(tpc):
        rows = [land[z, c, n : n + 1, :] for c in range(3)]
        i = z * tpc + n
        prepare_tile(half + i, rows, centre, i, *refs, i * TILE, count)


def prepare_halo(z, halo, shifts, *refs):
    half, tiles = NZ // 2, refs[2].shape[0]
    upper = lax.div(z, jnp.int32(half))
    rows = [halo[z, c : c + 1, :] for c in range(3)]
    shift = jnp.where(upper == 0, shifts[0], shifts[1])
    prepare_tile(z + upper * tiles, rows, shift, None, *refs, 0, 0)


def quotients(i, buf, neighbours, lefts_t, rights):
    right = rights[i]
    for n in range(neighbours.shape[0]):
        buf[n * TILE : (n + 1) * TILE, :] = jnp.dot(
            lefts_t[neighbours[n, i]], right, preferred_element_type=F32
        )


def tile_force(i, zc, n, buf, neighbours, lefts, places, force, count):
    total = jnp.zeros((KROWS, TILE), F32)
    for k in range(0, neighbours.shape[0], 2):
        q = buf[k * TILE : (k + 2) * TILE, :]
        r = 1.0 / q
        r2 = r * r
        d = jnp.maximum((r2 - r).astype(BF16), jnp.zeros(q.shape, BF16))
        f = (d * d) * (r2 * r - 0.5 * reach_sq**3).astype(BF16)
        x = jnp.concatenate([lefts[neighbours[k, i]], lefts[neighbours[k + 1, i]]], axis=1)
        total = total + jnp.dot(x, f, preferred_element_type=F32)
    moved = total[0:8] + total[8:16] + total[16:24]
    row = i * TILE + lax.broadcasted_iota(jnp.int32, (8, TILE), 1)
    beads = lax.axis_size("bead")
    scale = jnp.where(row < count, 48.0 / 256.0 / reach_sq**5 / shrink / beads, 0.0)
    result = (places[i] * total[15:16] - moved) * scale
    for c in range(3):
        force[zc, c, n : n + 1, :] = result[c : c + 1]


def forces(neighbours, count, lefts, lefts_t, rights, places, even, odd, force, r1, near, sems):
    x, z, y = place()
    tpc = rights.shape[0] // NZ
    half = NZ // 2
    bufs = (even, odd)
    send_sem, recv_sem, near_send, near_recv = sems

    def offset(c):
        return half + lax.div(c, jnp.int32(2)) * (1 - rem(c, 2)) - lax.div(c + 1, jnp.int32(2)) * rem(c, 2)

    quotients(rem(z + half, NZ) * tpc, even, neighbours, lefts_t, rights)

    first_near = NZ - len(near_offsets())

    def compute(c):
        zc = rem(z + offset(c), NZ)
        after = rem(z + offset(jnp.minimum(c + 1, NZ - 1)), NZ)
        for n in range(tpc):
            following = zc * tpc + n + 1 if n + 1 < tpc else after * tpc
            quotients(following, bufs[(n + 1) % 2], neighbours, lefts_t, rights)
            tile_force(zc * tpc + n, zc, n, bufs[n % 2], neighbours, lefts, places, force, count)

    def leave(c, kind, dy):
        dz = offset(c)
        group_copy(force.at[rem(z + dz, NZ)], r1, send_sem, recv_sem, dz, dy, kind).start()

    def pair(g, carry):
        for m in range(2):
            compute(2 * g + m)
        for m in range(2):
            for dy in range(NY):
                leave(2 * g + m, 0, dy)
        return carry

    def chunk(c, carry):
        compute(c)
        kind = jnp.minimum(jnp.maximum(c - first_near + 1, 0), 1)
        leave(c, kind, 1)

        @pl.when(c < NZ - 1)
        def _():
            leave(c, kind, 0)

        @pl.when(c >= first_near)
        def _():
            zc = rem(z + offset(c), NZ)
            for dx in range(1, NX):
                for dy in range(NY):
                    device = to_bead(bead_of(rem(x + dx, NX), zc, rem(y + dy, NY)))
                    slot = near_slot(dx, c - first_near, dy)
                    send(force.at[zc], near.at[slot], near_send.at[0], near_recv.at[0], device)

        return carry

    pairs = (first_near - 1) // 2
    lax.fori_loop(0, pairs, pair, 0)
    lax.fori_loop(2 * pairs, NZ, chunk, 0)
    r1[0] = force[z]


def kernel(
    counts, neighbours_in, border_in, section_in, out,
    neighbours, border, section, raw, land, halo, force,
    lefts, lefts_t, rights, places, even, odd,
    r1f, t2f, r2f, first_in, pxf, r1b, t2b, r2b, plain_in, pxb, near,
    load_sem, *sems,
):
    x, z, y = place()
    slab, slabs = lax.axis_index("slab"), lax.axis_size("slab")
    loads = [
        pltpu.make_async_copy(section_in, section, load_sem.at[0]),
        pltpu.make_async_copy(border_in, border, load_sem.at[1]),
        pltpu.make_async_copy(neighbours_in, neighbours, load_sem.at[2]),
    ]
    barrier = pltpu.get_barrier_semaphore()
    greeted = partners()
    for device in greeted:
        pl.semaphore_signal(barrier, inc=1, device_id=device, device_id_type=MESH)
    for load in loads:
        load.start()
    for load in loads:
        load.wait()
    pack_chunks(section, border, raw)
    pl.semaphore_wait(barrier, len(greeted))
    finish = forward_scan(raw, r1f, t2f, r2f, first_in, pxf, land, halo, sems[:10])
    q3, q4 = sems[7], sems[9]
    count = counts[0]
    box = slab_width * slabs
    centre = (slab.astype(F32) + 0.5) * slab_width
    shifts = (
        centre + jnp.where(slab == 0, box, 0.0),
        centre - jnp.where(slab == slabs - 1, box, 0.0),
    )
    refs = (lefts, lefts_t, rights, places)
    farthest = NZ // 2
    for distance in range(farthest + 1):
        chunks = [dz for dz in range(NZ) if reach(dz) == distance]
        tiles = [dz for dz in range(NZ) if reach(dz) == distance - 1]
        if distance == farthest:
            tiles += chunks
        for dz in chunks:
            if dz:
                await_bytes(land.at[0], q3.at[dz])
        for dz in tiles:
            await_bytes(halo.at[0], q4.at[dz])
        for dz in chunks:
            prepare_own(rem(z + (NZ - dz), NZ), land, centre, count, *refs)
        for dz in tiles:
            prepare_halo(rem(z + (NZ - dz), NZ), halo, shifts, *refs)
    forces(
        neighbours, count, lefts, lefts_t, rights, places, even, odd, force, r1b, near, sems[10:14]
    )
    backward_scan(r1b, near, t2b, r2b, plain_in, pxb, out, sems[10:])
    finish()


def leapfrog(section, momentum, section_force):
    level = lax.axis_index("bead").astype(F32)
    safe = jnp.maximum(level, 1.0)
    section_force = section_force / safe
    mass = jnp.where(level > 0, (level + 1.0) / safe, 1.0)
    spring = jnp.where(level > 0, omega_sq * mass, 0.0)
    step = time_step / 3.0
    push = 0.5 * step * spring
    drift = step / mass
    p = momentum + (0.5 * time_step) * section_force
    u = section
    for turn in range(3):
        p = p - push * u
        u = u + drift * p
        p = p - push * u
    return u, p


def step(section, momentum, neighbours, border_rows, counts):
    shape = section.shape
    listed = neighbours.shape[2]
    tiles = shape[2] // TILE
    tpc = tiles // NZ
    dense = (3, NZ, tpc, TILE)
    ext_tiles = tiles + NZ
    chunk, wide = (3, tpc, TILE), (4, tpc, TILE)
    anywhere = pl.BlockSpec(memory_space=pl.ANY)
    in_hbm = pl.BlockSpec(memory_space=pltpu.HBM)
    hbm = lambda array: pltpu.with_memory_space_constraint(array, pltpu.HBM)
    vmem = lambda *dims: pltpu.VMEM(dims, F32)
    scan_buffers = [
        vmem(count, *part)
        for part in (wide, chunk)
        for count in (NZ * NY, 2, NX, NX, NZ)
    ]
    one, each = DMA((1,)), DMA((NZ,))
    section, momentum = section.reshape(dense), momentum.reshape(dense)
    section_force = pl.pallas_call(
        kernel,
        out_shape=jax.ShapeDtypeStruct(dense, F32),
        in_specs=[
            pl.BlockSpec(memory_space=pltpu.SMEM),
            in_hbm,
            in_hbm,
            in_hbm,
        ],
        out_specs=anywhere,
        scratch_shapes=[
            pltpu.SMEM((listed, tiles), jnp.int32),
            pltpu.VMEM(border_rows.shape[1:], jnp.int32),
            vmem(*dense),
            vmem(NZ, *wide),
            vmem(NZ, *chunk),
            vmem(NZ, 4, TILE),
            vmem(NZ, *chunk),
            pltpu.VMEM((ext_tiles, KROWS, TILE), BF16),
            pltpu.VMEM((ext_tiles, TILE, KROWS), BF16),
            pltpu.VMEM((tiles, KROWS, TILE), BF16),
            vmem(tiles, 8, TILE),
            vmem(listed * TILE, TILE),
            vmem(listed * TILE, TILE),
        ]
        + scan_buffers
        + [vmem(len(near_slots()), *chunk)]
        + [DMA((3,))]
        + [one] * 6
        + [one, each] * 2
        + [one, DMA((2,))]
        + [one] * 9,
        compiler_params=pltpu.CompilerParams(
            collective_id=0, has_side_effects=True, vmem_limit_bytes=24 * 2**20
        ),
        name="path_step",
    )(
        counts,
        hbm(neighbours.transpose(0, 2, 1).reshape(listed, tiles)),
        hbm(border_rows.reshape(border_rows.shape[1:])),
        hbm(section),
    )
    u, p = leapfrog(section, momentum, section_force)
    return u.reshape(shape), p.reshape(shape)


def solution(mesh):
    return jax.shard_map(
        step,
        mesh=mesh,
        in_specs=(
            P("bead", None, "slab"),
            P("bead", None, "slab"),
            P("slab", None, None),
            P("slab", None, None),
            P("slab"),
        ),
        out_specs=(P("bead", None, "slab"), P("bead", None, "slab")),
        check_vma=False,
    )
```

```python
import functools
import math

import jax
import jax.numpy as jnp
from jax import lax
from jax.experimental import pallas as pl
from jax.experimental.pallas import tpu as pltpu
from jax.sharding import PartitionSpec as P

MESH = pl.DeviceIdType.MESH
time_step = 0.1
omega_sq = 4.0
slab_width = 3.0
reach_sq = 17.0
shrink = 1.0 / math.sqrt(reach_sq)
NX, NZ, NY = 4, 8, 2
TILE = 128
KROWS = 32
F32 = jnp.float32
BF16 = jnp.bfloat16
DMA = pltpu.SemaphoreType.DMA


def rem(value, size):
    return lax.rem(value, jnp.int32(size))


def place():
    bead = lax.axis_index("bead")
    return lax.div(bead, jnp.int32(NZ * NY)), rem(lax.div(bead, jnp.int32(NY)), NZ), rem(bead, NY)


def bead_of(x, z, y):
    return (x * NZ + z) * NY + y


def to_bead(bead):
    return (bead, lax.axis_index("slab"))


def group_steps():
    return [(dz, dy) for dz in range(NZ) for dy in range(NY) if dz or dy]


def reach(dz):
    return min(dz, NZ - dz)


def partners():
    x, z, y = place()
    slab, slabs = lax.axis_index("slab"), lax.axis_size("slab")
    found = []
    for dz in sorted(range(NZ), key=reach, reverse=True):
        tz = rem(z + dz, NZ)
        found += [to_bead(bead_of(x, tz, rem(y + dy, NY))) for dy in reversed(range(NY)) if dz or dy]
        found += [(bead_of(x, tz, y), rem(slab + ds, slabs)) for ds in (1, slabs - 1)]
    return found + [to_bead(bead_of(rem(x + dx, NX), z, y)) for dx in range(1, NX)]


def remote(src, dst, send_sem, recv_sem, device):
    return pltpu.make_async_remote_copy(
        src_ref=src,
        dst_ref=dst,
        send_sem=send_sem,
        recv_sem=recv_sem,
        device_id=device,
        device_id_type=MESH,
    )


def send(*args):
    copy = remote(*args)
    copy.start()
    return copy


def await_bytes(ref, sem):
    pltpu.make_async_copy(ref, ref, sem).wait()


def group_copy(src, r1, send_sem, recv_sem, dz, dy, kind=0):
    x, z, y = place()
    device = to_bead(bead_of(x, rem(z + dz, NZ), rem(y + dy, NY)))
    return remote(src, r1.at[dz * NY + dy], send_sem.at[0], recv_sem.at[kind], device)


def near_offsets():
    return (NZ - 2, 1, NZ - 1, 0) if NZ > 4 else (1, NZ - 1, 0)


def near_slots():
    return [(dx, k, dy) for dx in range(1, NX) for k in range(len(near_offsets())) for dy in range(NY)]


def near_slot(dx, k, dy):
    return ((dx - 1) * len(near_offsets()) + k) * NY + dy


def exchange_x(src, slots, send_sem, recv_sem):
    x, z, y = place()
    for dx in range(1, NX):
        device = to_bead(bead_of(rem(x + dx, NX), z, y))
        send(src, slots.at[dx], send_sem.at[0], recv_sem.at[0], device)


def level_rows(bead):
    return jnp.full((1, 1, TILE), bead.astype(F32), F32)


def slot_from(zs, ys):
    x, z, y = place()
    return rem(z + (NZ - zs), NZ) * NY + rem(y + (NY - ys), NY)


def near_first():
    return sorted(range(1, NZ), key=reach)


def forward_scan(raw, r1, t2, r2, first_in, px, land, halo, sems):
    s1, q1, s2, q2, sf, qf, s3, q3, s4, q4 = sems
    x, z, y = place()
    slab, slabs = lax.axis_index("slab"), lax.axis_size("slab")
    for dz, dy in sorted(group_steps(), key=lambda step: -reach(step[0]) - step[1]):
        group_copy(raw.at[rem(z + dz, NZ)], r1, s1, q1, dz, dy).start()
    r1[0] = raw[z]
    await_bytes(r1.at[1:], q1.at[0])

    @pl.when(x == 0)
    def _():
        for dx in range(1, NX):
            device = to_bead(bead_of(dx, z, y))
            send(r1.at[slot_from(0, 0)], first_in.at[0], sf.at[0], qf.at[0], device)
        first_in[0] = r1[slot_from(0, 0)]

    total = jnp.zeros(r1.shape[1:], F32)
    for zs in reversed(range(NZ)):
        kept = None
        for ys in reversed(range(NY)):
            one = r1[slot_from(zs, ys)]
            if zs == 0 and ys == 0:
                one = jnp.where(x == 0, 0.0, one)
            total = total + one
            kept = total if kept is None else jnp.where(y == ys, total, kept)
        px[zs] = kept
    t2[0] = total
    exchange_x(t2.at[0], r2, s2, q2)

    @pl.when(x != 0)
    def _():
        await_bytes(first_in.at[0], qf.at[0])

    await_bytes(r2.at[1:], q2.at[0])
    base = jnp.zeros(r1.shape[1:], F32)
    for dx in range(1, NX):
        xs = rem(x + (NX - dx), NX)
        base = base + jnp.where(xs > x, r2[dx], 0.0)
    first = first_in[0]
    beside = rem(slab + 1 + (slabs - 2) * lax.div(z, jnp.int32(NZ // 2)), slabs)
    for dz in near_first()[::-1] + [0]:
        tz = rem(z + dz, NZ)
        bead = bead_of(x, tz, y)
        places = first + level_rows(bead) * (px[tz] + base)
        px[tz] = places
        send(px.at[tz, 3], halo.at[z], s4.at[0], q4.at[dz], (bead, beside))
        if dz:
            send(px.at[tz, 0:3], land.at[z], s3.at[0], q3.at[dz], to_bead(bead))
        else:
            land[z] = places[0:3]

    def finish():
        await_bytes(r1.at[1:], s1.at[0])
        await_bytes(r2.at[1:], s2.at[0])
        await_bytes(land.at[1:], s3.at[0])
        await_bytes(halo, s4.at[0])

        @pl.when(x == 0)
        def _():
            await_bytes(r2.at[1:], sf.at[0])

    return finish


def backward_scan(r1, near, t2, r2, plain_in, px, out, sems):
    s1, q1, sn, qn, s2, q2, sf, qf, s3, q3, own_sem = sems
    x, z, y = place()
    far = [(dz, dy) for dz in range(NZ) for dy in range(NY) if dz not in near_offsets()]
    await_bytes(r1.at[0 : len(far)], q1.at[0])
    total = jnp.zeros(r1.shape[1:], F32)
    plain = jnp.zeros(r1.shape[1:], F32)
    for dz, dy in far:
        one = r1[dz * NY + dy]
        plain = plain + one
        total = total + one * level_rows(bead_of(x, rem(z + (NZ - dz), NZ), rem(y + (NY - dy), NY)))
    t2[0] = total
    t2[1] = plain
    exchange_x(t2.at[0], r2, s2, q2)

    @pl.when(x != 0)
    def _():
        send(t2.at[1], plain_in.at[x], sf.at[0], qf.at[0], to_bead(bead_of(0, z, y)))

    def gather_near(k, base, plain):
        await_bytes(near.at[0 : (NX - 1) * NY], qn.at[k])
        for dx in range(1, NX):
            for dy in range(NY):
                xs = rem(x + (NX - dx), NX)
                source = bead_of(xs, rem(z + (NZ - near_offsets()[k]), NZ), rem(y + (NY - dy), NY))
                one = near[near_slot(dx, k, dy)]
                plain = plain + one
                base = base + jnp.where(xs < x, one * level_rows(source), 0.0)
        return base, plain

    base = jnp.zeros(r1.shape[1:], F32)
    plain = jnp.zeros(r1.shape[1:], F32)
    last = len(near_offsets()) - 1
    for k in range(last):
        base, plain = gather_near(k, base, plain)
    await_bytes(r1.at[0 : len(group_steps()) - len(far)], q1.at[1])
    total = jnp.zeros(r1.shape[1:], F32)
    for zs in range(NZ):
        kept = None
        for ys in range(NY):
            one = r1[slot_from(zs, ys)]
            plain = plain + one
            total = total + one * level_rows(bead_of(x, zs, ys))
            kept = total if kept is None else jnp.where(y == ys, total, kept)
        px[zs] = kept
    base, plain = gather_near(last, base, plain)

    @pl.when(x == 0)
    def _():
        plain_in[0] = plain
        await_bytes(plain_in.at[1:], qf.at[0])

    await_bytes(r2.at[1:], q2.at[0])
    for dx in range(1, NX):
        xs = rem(x + (NX - dx), NX)
        base = base + jnp.where(xs < x, r2[dx], 0.0)
    for zs in range(NZ):
        px[zs] = px[zs] + base

    @pl.when((x == 0) & (y == 0))
    def _():
        everything = plain_in[0]
        for xs in range(1, NX):
            everything = everything + plain_in[xs]
        px[0] = everything

    for dz in near_first()[::-1] + [0]:
        tz = rem(z + dz, NZ)
        if dz:
            device = to_bead(bead_of(x, tz, y))
            send(px.at[tz], out.at[:, z], s3.at[0], q3.at[0], device)
        else:
            own = pltpu.make_async_copy(px.at[tz], out.at[:, z], own_sem.at[0])
            own.start()

    await_bytes(px.at[1:], q3.at[0])
    own.wait()
    await_bytes(r1.at[1:], s1.at[0])
    await_bytes(near, sn.at[0])
    await_bytes(r2.at[1:], s2.at[0])
    await_bytes(px.at[1:], s3.at[0])

    @pl.when(x != 0)
    def _():
        await_bytes(t2.at[1], sf.at[0])


def pack_chunks(section, border, raw):
    level = level_rows(lax.axis_index("bead"))
    inverse = 1.0 / jnp.maximum(level, 1.0)
    tpc = section.shape[2]
    sub = lax.broadcasted_iota(jnp.int32, (8, TILE), 0)
    blocks = NZ // 2 * tpc // 8
    for z in range(NZ):
        raw[z, 0:3] = section[:, z] * inverse
    pieces = []
    for c in range(3):
        for b in range(blocks):
            rows = [section[c, b * (8 // tpc) + m] for m in range(8 // tpc)]
            pieces.append(jnp.concatenate(rows, axis=0))
    half = NZ // 2
    for z in range(NZ):
        k, n = z // half, z % half
        index = jnp.broadcast_to(border[k : k + 1, n * TILE : (n + 1) * TILE], (8, TILE))
        lane, block = index % TILE, index // TILE
        rows = []
        for c in range(3):
            out = jnp.zeros((8, TILE), F32)
            for b in range(blocks):
                taken = jnp.take_along_axis(
                    pieces[c * blocks + b], lane, axis=1, mode="promise_in_bounds"
                )
                out = jnp.where(block == b * 8 + sub, taken, out)
            rows.append(jnp.sum(out, axis=0, keepdims=True))
        raw[z, 3] = jnp.concatenate(rows + [jnp.zeros((1, TILE), F32)], axis=0) * inverse[0]


def split3(value):
    high = value.astype(BF16).astype(F32)
    rest = value - high
    middle = rest.astype(BF16).astype(F32)
    return high, middle, rest - middle


def prepare_tile(t, rows, shift, own, lefts, lefts_t, rights, places, row, count):
    sub = lax.broadcasted_iota(jnp.int32, (8, TILE), 0)
    comp = sub % 4
    xs = [jnp.broadcast_to(v, (8, TILE)) for v in rows]
    xs = [(v - w) * shrink for v, w in zip(xs, (shift, 0.5 * slab_width, 0.5 * slab_width))]
    p = jnp.where(comp == 0, xs[0], jnp.where(comp == 1, xs[1], xs[2]))
    norm = xs[0] * xs[0] + xs[1] * xs[1] + xs[2] * xs[2]
    far = norm
    if own is not None:
        place_in = row + lax.broadcasted_iota(jnp.int32, (8, TILE), 1)
        far = jnp.where(place_in < count, norm, 4096.0)
    high, middle, low = split3(p)
    fh, fm, fl = split3(far)
    last, top = comp == 3, sub < 4
    a0 = jnp.where(last, jnp.where(top, fh, fm), high)
    a1 = jnp.where(last, jnp.where(top, fl, 1.0), middle)
    a2 = jnp.where(last, 1.0, jnp.where(top, low, high))
    left = jnp.concatenate([a0, a1, a2, jnp.zeros((8, TILE), F32)], axis=0)
    lefts[t] = left.astype(BF16)
    lefts_t[t] = left.T.astype(BF16)
    if own is not None:
        nh, nm, nl = split3(norm + 1.0 / reach_sq)
        h2, m2, l2 = -2.0 * high, -2.0 * middle, -2.0 * low
        b0 = jnp.where(last, 1.0, jnp.where(top, h2, m2))
        b1 = jnp.where(last, jnp.where(top, 1.0, nh), jnp.where(top, h2, m2))
        b2 = jnp.where(last, jnp.where(top, nm, nl), jnp.where(top, h2, l2))
        right = jnp.concatenate([b0, b1, b2, jnp.zeros((8, TILE), F32)], axis=0)
        rights[own] = right.astype(BF16)
        places[own] = p


def prepare_own(z, land, centre, count, *refs):
    half, tpc = NZ // 2, refs[2].shape[0] // NZ
    for n in range(tpc):
        rows = [land[z, c, n : n + 1, :] for c in range(3)]
        i = z * tpc + n
        prepare_tile(half + i, rows, centre, i, *refs, i * TILE, count)


def prepare_halo(z, halo, shifts, *refs):
    half, tiles = NZ // 2, refs[2].shape[0]
    upper = lax.div(z, jnp.int32(half))
    rows = [halo[z, c : c + 1, :] for c in range(3)]
    shift = jnp.where(upper == 0, shifts[0], shifts[1])
    prepare_tile(z + upper * tiles, rows, shift, None, *refs, 0, 0)


def quotients(i, buf, neighbours, lefts_t, rights):
    right = rights[i]
    for n in range(neighbours.shape[0]):
        buf[n * TILE : (n + 1) * TILE, :] = jnp.dot(
            lefts_t[neighbours[n, i]], right, preferred_element_type=F32
        )


def tile_force(i, zc, n, buf, neighbours, lefts, places, force, count):
    total = jnp.zeros((KROWS, TILE), F32)
    for k in range(0, neighbours.shape[0], 2):
        q = buf[k * TILE : (k + 2) * TILE, :]
        r = 1.0 / q
        r2 = r * r
        d = jnp.maximum((r2 - r).astype(BF16), jnp.zeros(q.shape, BF16))
        f = (d * d) * (r2 * r - 0.5 * reach_sq**3).astype(BF16)
        x = jnp.concatenate([lefts[neighbours[k, i]], lefts[neighbours[k + 1, i]]], axis=1)
        total = total + jnp.dot(x, f, preferred_element_type=F32)
    moved = total[0:8] + total[8:16] + total[16:24]
    row = i * TILE + lax.broadcasted_iota(jnp.int32, (8, TILE), 1)
    beads = lax.axis_size("bead")
    scale = jnp.where(row < count, 48.0 / 256.0 / reach_sq**5 / shrink / beads, 0.0)
    result = (places[i] * total[15:16] - moved) * scale
    for c in range(3):
        force[zc, c, n : n + 1, :] = result[c : c + 1]


def forces(neighbours, count, lefts, lefts_t, rights, places, even, odd, force, r1, near, sems):
    x, z, y = place()
    tpc = rights.shape[0] // NZ
    half = NZ // 2
    bufs = (even, odd)
    send_sem, recv_sem, near_send, near_recv = sems

    def offset(c):
        return half + lax.div(c, jnp.int32(2)) * (1 - rem(c, 2)) - lax.div(c + 1, jnp.int32(2)) * rem(c, 2)

    quotients(rem(z + half, NZ) * tpc, even, neighbours, lefts_t, rights)

    first_near = NZ - len(near_offsets())

    def compute(c):
        zc = rem(z + offset(c), NZ)
        after = rem(z + offset(jnp.minimum(c + 1, NZ - 1)), NZ)
        for n in range(tpc):
            following = zc * tpc + n + 1 if n + 1 < tpc else after * tpc
            quotients(following, bufs[(n + 1) % 2], neighbours, lefts_t, rights)
            tile_force(zc * tpc + n, zc, n, bufs[n % 2], neighbours, lefts, places, force, count)

    def leave(c, kind, dy):
        dz = offset(c)
        group_copy(force.at[rem(z + dz, NZ)], r1, send_sem, recv_sem, dz, dy, kind).start()

    def pair(g, carry):
        for m in range(2):
            compute(2 * g + m)
        for m in range(2):
            for dy in range(NY):
                leave(2 * g + m, 0, dy)
        return carry

    def chunk(c, carry):
        compute(c)
        @pl.when(c >= first_near)
        def _():
            zc = rem(z + offset(c), NZ)
            for dx in sorted(range(1, NX), key=lambda step: -min(step, NX - step)):
                for dy in reversed(range(NY)):
                    device = to_bead(bead_of(rem(x + dx, NX), zc, rem(y + dy, NY)))
                    slot = near_slot(dx, c - first_near, dy)
                    send(force.at[zc], near.at[slot], near_send.at[0], near_recv.at[c - first_near], device)

        kind = jnp.minimum(jnp.maximum(c - first_near + 1, 0), 1)
        leave(c, kind, 1)

        @pl.when(c < NZ - 1)
        def _():
            leave(c, kind, 0)

        return carry

    pairs = (first_near - 1) // 2
    lax.fori_loop(0, pairs, pair, 0)
    lax.fori_loop(2 * pairs, NZ, chunk, 0)
    r1[0] = force[z]


def kernel(
    counts, neighbours_in, border_in, section_in, out,
    neighbours, border, section, raw, land, halo, force,
    lefts, lefts_t, rights, places, even, odd,
    r1f, t2f, r2f, first_in, pxf, r1b, t2b, r2b, plain_in, pxb, near,
    load_sem, *sems,
):
    x, z, y = place()
    slab, slabs = lax.axis_index("slab"), lax.axis_size("slab")
    loads = [
        pltpu.make_async_copy(section_in, section, load_sem.at[0]),
        pltpu.make_async_copy(border_in, border, load_sem.at[1]),
        pltpu.make_async_copy(neighbours_in, neighbours, load_sem.at[2]),
    ]
    barrier = pltpu.get_barrier_semaphore()
    greeted = partners()
    for device in greeted:
        pl.semaphore_signal(barrier, inc=1, device_id=device, device_id_type=MESH)
    for load in loads:
        load.start()
    for load in loads:
        load.wait()
    pack_chunks(section, border, raw)
    pl.semaphore_wait(barrier, len(greeted))
    finish = forward_scan(raw, r1f, t2f, r2f, first_in, pxf, land, halo, sems[:10])
    q3, q4 = sems[7], sems[9]
    count = counts[0]
    box = slab_width * slabs
    centre = (slab.astype(F32) + 0.5) * slab_width
    shifts = (
        centre + jnp.where(slab == 0, box, 0.0),
        centre - jnp.where(slab == slabs - 1, box, 0.0),
    )
    refs = (lefts, lefts_t, rights, places)
    farthest = NZ // 2
    for distance in range(farthest + 1):
        chunks = [dz for dz in range(NZ) if reach(dz) == distance]
        tiles = [dz for dz in range(NZ) if reach(dz) == distance - 1]
        if distance == farthest:
            tiles += chunks
        for dz in chunks:
            if dz:
                await_bytes(land.at[0], q3.at[dz])
        for dz in tiles:
            await_bytes(halo.at[0], q4.at[dz])
        for dz in chunks:
            prepare_own(rem(z + (NZ - dz), NZ), land, centre, count, *refs)
        for dz in tiles:
            prepare_halo(rem(z + (NZ - dz), NZ), halo, shifts, *refs)
    forces(
        neighbours, count, lefts, lefts_t, rights, places, even, odd, force, r1b, near, sems[10:14]
    )
    backward_scan(r1b, near, t2b, r2b, plain_in, pxb, out, sems[10:])
    finish()


def leapfrog(section, momentum, section_force):
    level = lax.axis_index("bead").astype(F32)
    safe = jnp.maximum(level, 1.0)
    section_force = section_force / safe
    mass = jnp.where(level > 0, (level + 1.0) / safe, 1.0)
    spring = jnp.where(level > 0, omega_sq * mass, 0.0)
    step = time_step / 3.0
    push = 0.5 * step * spring
    drift = step / mass
    p = momentum + (0.5 * time_step) * section_force
    u = section
    for turn in range(3):
        p = p - push * u
        u = u + drift * p
        p = p - push * u
    return u, p


def step(section, momentum, neighbours, border_rows, counts):
    shape = section.shape
    listed = neighbours.shape[2]
    tiles = shape[2] // TILE
    tpc = tiles // NZ
    dense = (3, NZ, tpc, TILE)
    ext_tiles = tiles + NZ
    chunk, wide = (3, tpc, TILE), (4, tpc, TILE)
    anywhere = pl.BlockSpec(memory_space=pl.ANY)
    in_hbm = pl.BlockSpec(memory_space=pltpu.HBM)
    hbm = lambda array: pltpu.with_memory_space_constraint(array, pltpu.HBM)
    vmem = lambda *dims: pltpu.VMEM(dims, F32)
    scan_buffers = [
        vmem(count, *part)
        for part in (wide, chunk)
        for count in (NZ * NY, 2, NX, NX, NZ)
    ]
    one, each = DMA((1,)), DMA((NZ,))
    section, momentum = section.reshape(dense), momentum.reshape(dense)
    section_force = pl.pallas_call(
        kernel,
        out_shape=jax.ShapeDtypeStruct(dense, F32),
        in_specs=[
            pl.BlockSpec(memory_space=pltpu.SMEM),
            in_hbm,
            in_hbm,
            in_hbm,
        ],
        out_specs=anywhere,
        scratch_shapes=[
            pltpu.SMEM((listed, tiles), jnp.int32),
            pltpu.VMEM(border_rows.shape[1:], jnp.int32),
            vmem(*dense),
            vmem(NZ, *wide),
            vmem(NZ, *chunk),
            vmem(NZ, 4, TILE),
            vmem(NZ, *chunk),
            pltpu.VMEM((ext_tiles, KROWS, TILE), BF16),
            pltpu.VMEM((ext_tiles, TILE, KROWS), BF16),
            pltpu.VMEM((tiles, KROWS, TILE), BF16),
            vmem(tiles, 8, TILE),
            vmem(listed * TILE, TILE),
            vmem(listed * TILE, TILE),
        ]
        + scan_buffers
        + [vmem(len(near_slots()), *chunk)]
        + [DMA((3,))]
        + [one] * 6
        + [one, each] * 2
        + [one, DMA((2,)), one, DMA((len(near_offsets()),))]
        + [one] * 7,
        compiler_params=pltpu.CompilerParams(
            collective_id=0, has_side_effects=True, vmem_limit_bytes=24 * 2**20
        ),
        name="path_step",
    )(
        counts,
        hbm(neighbours.transpose(0, 2, 1).reshape(listed, tiles)),
        hbm(border_rows.reshape(border_rows.shape[1:])),
        hbm(section),
    )
    u, p = leapfrog(section, momentum, section_force)
    return u.reshape(shape), p.reshape(shape)


def solution(mesh):
    return jax.shard_map(
        step,
        mesh=mesh,
        in_specs=(
            P("bead", None, "slab"),
            P("bead", None, "slab"),
            P("slab", None, None),
            P("slab", None, None),
            P("slab"),
        ),
        out_specs=(P("bead", None, "slab"), P("bead", None, "slab")),
        check_vma=False,
    )
```

```python
import functools
import math

import jax
import jax.numpy as jnp
from jax import lax
from jax.experimental import pallas as pl
from jax.experimental.pallas import tpu as pltpu
from jax.sharding import PartitionSpec as P

MESH = pl.DeviceIdType.MESH
time_step = 0.1
omega_sq = 4.0
slab_width = 3.0
reach_sq = 17.0
shrink = 1.0 / math.sqrt(reach_sq)
NX, NZ, NY = 4, 8, 2
TILE = 128
KROWS = 32
F32 = jnp.float32
BF16 = jnp.bfloat16
DMA = pltpu.SemaphoreType.DMA


def rem(value, size):
    return lax.rem(value, jnp.int32(size))


def place():
    bead = lax.axis_index("bead")
    return lax.div(bead, jnp.int32(NZ * NY)), rem(lax.div(bead, jnp.int32(NY)), NZ), rem(bead, NY)


def bead_of(x, z, y):
    return (x * NZ + z) * NY + y


def to_bead(bead):
    return (bead, lax.axis_index("slab"))


def group_steps():
    return [(dz, dy) for dz in range(NZ) for dy in range(NY) if dz or dy]


def reach(dz):
    return min(dz, NZ - dz)


def partners():
    x, z, y = place()
    slab, slabs = lax.axis_index("slab"), lax.axis_size("slab")
    found = []
    for dz in sorted(range(NZ), key=reach, reverse=True):
        tz = rem(z + dz, NZ)
        found += [to_bead(bead_of(x, tz, rem(y + dy, NY))) for dy in reversed(range(NY)) if dz or dy]
        found += [(bead_of(x, tz, y), rem(slab + ds, slabs)) for ds in (1, slabs - 1)]
    return found + [to_bead(bead_of(rem(x + dx, NX), z, y)) for dx in range(1, NX)]


def remote(src, dst, send_sem, recv_sem, device):
    return pltpu.make_async_remote_copy(
        src_ref=src,
        dst_ref=dst,
        send_sem=send_sem,
        recv_sem=recv_sem,
        device_id=device,
        device_id_type=MESH,
    )


def send(*args):
    copy = remote(*args)
    copy.start()
    return copy


def await_bytes(ref, sem):
    pltpu.make_async_copy(ref, ref, sem).wait()


def group_copy(src, r1, send_sem, recv_sem, dz, dy, kind=0):
    x, z, y = place()
    device = to_bead(bead_of(x, rem(z + dz, NZ), rem(y + dy, NY)))
    return remote(src, r1.at[dz * NY + dy], send_sem.at[0], recv_sem.at[kind], device)


def near_offsets():
    return (NZ - 2, 1, NZ - 1, 0) if NZ > 4 else (1, NZ - 1, 0)


def near_slots():
    return [(dx, k, dy) for dx in range(1, NX) for k in range(len(near_offsets())) for dy in range(NY)]


def near_slot(dx, k, dy):
    return ((dx - 1) * len(near_offsets()) + k) * NY + dy


def exchange_x(src, slots, send_sem, recv_sem):
    x, z, y = place()
    for dx in range(1, NX):
        device = to_bead(bead_of(rem(x + dx, NX), z, y))
        send(src, slots.at[dx], send_sem.at[0], recv_sem.at[0], device)


def level_rows(bead):
    return jnp.full((1, 1, TILE), bead.astype(F32), F32)


def slot_from(zs, ys):
    x, z, y = place()
    return rem(z + (NZ - zs), NZ) * NY + rem(y + (NY - ys), NY)


def near_first():
    return sorted(range(1, NZ), key=reach)


def forward_scan(raw, r1, t2, r2, first_in, px, land, halo, sems):
    s1, q1, s2, q2, sf, qf, s3, q3, s4, q4 = sems
    x, z, y = place()
    slab, slabs = lax.axis_index("slab"), lax.axis_size("slab")
    steps = sorted(group_steps(), key=lambda step: -reach(step[0]) - step[1])
    for dz, dy in steps:
        group_copy(raw.at[rem(z + dz, NZ)], r1, s1, q1, dz, dy, reach(dz)).start()
    r1[0] = raw[z]
    total = jnp.where(bead_of(x, z, y) == 0, 0.0, raw[z])
    for distance in range(NZ // 2 + 1):
        group = [step for step in steps if reach(step[0]) == distance]
        await_bytes(r1.at[0 : len(group)], q1.at[distance])
        for dz, dy in group:
            source = bead_of(x, rem(z + (NZ - dz), NZ), rem(y + (NY - dy), NY))
            total = total + jnp.where(source == 0, 0.0, r1[dz * NY + dy])
    t2[0] = total
    exchange_x(t2.at[0], r2, s2, q2)

    @pl.when(x == 0)
    def _():
        for dx in range(1, NX):
            device = to_bead(bead_of(dx, z, y))
            send(r1.at[slot_from(0, 0)], first_in.at[0], sf.at[0], qf.at[0], device)
        first_in[0] = r1[slot_from(0, 0)]

    total = jnp.zeros(r1.shape[1:], F32)
    for zs in reversed(range(NZ)):
        kept = None
        for ys in reversed(range(NY)):
            one = r1[slot_from(zs, ys)]
            if zs == 0 and ys == 0:
                one = jnp.where(x == 0, 0.0, one)
            total = total + one
            kept = total if kept is None else jnp.where(y == ys, total, kept)
        px[zs] = kept

    @pl.when(x != 0)
    def _():
        await_bytes(first_in.at[0], qf.at[0])

    await_bytes(r2.at[1:], q2.at[0])
    base = jnp.zeros(r1.shape[1:], F32)
    for dx in range(1, NX):
        xs = rem(x + (NX - dx), NX)
        base = base + jnp.where(xs > x, r2[dx], 0.0)
    first = first_in[0]
    beside = rem(slab + 1 + (slabs - 2) * lax.div(z, jnp.int32(NZ // 2)), slabs)
    for dz in near_first()[::-1] + [0]:
        tz = rem(z + dz, NZ)
        bead = bead_of(x, tz, y)
        places = first + level_rows(bead) * (px[tz] + base)
        px[tz] = places
        send(px.at[tz, 3], halo.at[z], s4.at[0], q4.at[dz], (bead, beside))
        if dz:
            send(px.at[tz, 0:3], land.at[z], s3.at[0], q3.at[dz], to_bead(bead))
        else:
            land[z] = places[0:3]

    def finish():
        await_bytes(r1.at[1:], s1.at[0])
        await_bytes(r2.at[1:], s2.at[0])
        await_bytes(land.at[1:], s3.at[0])
        await_bytes(halo, s4.at[0])

        @pl.when(x == 0)
        def _():
            await_bytes(r2.at[1:], sf.at[0])

    return finish


def backward_scan(r1, near, t2, r2, plain_in, px, out, sems):
    s1, q1, sn, qn, s2, q2, sf, qf, s3, q3, own_sem = sems
    x, z, y = place()
    far = [(dz, dy) for dz in range(NZ) for dy in range(NY) if dz not in near_offsets()]
    await_bytes(r1.at[0 : len(far)], q1.at[0])
    total = jnp.zeros(r1.shape[1:], F32)
    plain = jnp.zeros(r1.shape[1:], F32)
    for dz, dy in far:
        one = r1[dz * NY + dy]
        plain = plain + one
        total = total + one * level_rows(bead_of(x, rem(z + (NZ - dz), NZ), rem(y + (NY - dy), NY)))
    t2[0] = total
    t2[1] = plain
    exchange_x(t2.at[0], r2, s2, q2)

    @pl.when(x != 0)
    def _():
        send(t2.at[1], plain_in.at[x], sf.at[0], qf.at[0], to_bead(bead_of(0, z, y)))

    def gather_near(k, base, plain):
        await_bytes(near.at[0 : (NX - 1) * NY], qn.at[k])
        for dx in range(1, NX):
            for dy in range(NY):
                xs = rem(x + (NX - dx), NX)
                source = bead_of(xs, rem(z + (NZ - near_offsets()[k]), NZ), rem(y + (NY - dy), NY))
                one = near[near_slot(dx, k, dy)]
                plain = plain + one
                base = base + jnp.where(xs < x, one * level_rows(source), 0.0)
        return base, plain

    base = jnp.zeros(r1.shape[1:], F32)
    plain = jnp.zeros(r1.shape[1:], F32)
    last = len(near_offsets()) - 1
    for k in range(last):
        base, plain = gather_near(k, base, plain)
    await_bytes(r1.at[0 : len(group_steps()) - len(far)], q1.at[1])
    total = jnp.zeros(r1.shape[1:], F32)
    for zs in range(NZ):
        kept = None
        for ys in range(NY):
            one = r1[slot_from(zs, ys)]
            plain = plain + one
            total = total + one * level_rows(bead_of(x, zs, ys))
            kept = total if kept is None else jnp.where(y == ys, total, kept)
        px[zs] = kept
    base, plain = gather_near(last, base, plain)

    @pl.when(x == 0)
    def _():
        plain_in[0] = plain
        await_bytes(plain_in.at[1:], qf.at[0])

    await_bytes(r2.at[1:], q2.at[0])
    for dx in range(1, NX):
        xs = rem(x + (NX - dx), NX)
        base = base + jnp.where(xs < x, r2[dx], 0.0)
    for zs in range(NZ):
        px[zs] = px[zs] + base

    @pl.when((x == 0) & (y == 0))
    def _():
        everything = plain_in[0]
        for xs in range(1, NX):
            everything = everything + plain_in[xs]
        px[0] = everything

    for dz in near_first()[::-1] + [0]:
        tz = rem(z + dz, NZ)
        if dz:
            device = to_bead(bead_of(x, tz, y))
            send(px.at[tz], out.at[:, z], s3.at[0], q3.at[0], device)
        else:
            own = pltpu.make_async_copy(px.at[tz], out.at[:, z], own_sem.at[0])
            own.start()

    await_bytes(px.at[1:], q3.at[0])
    own.wait()
    await_bytes(r1.at[1:], s1.at[0])
    await_bytes(near, sn.at[0])
    await_bytes(r2.at[1:], s2.at[0])
    await_bytes(px.at[1:], s3.at[0])

    @pl.when(x != 0)
    def _():
        await_bytes(t2.at[1], sf.at[0])


def pack_chunks(section, border, raw):
    level = level_rows(lax.axis_index("bead"))
    inverse = 1.0 / jnp.maximum(level, 1.0)
    tpc = section.shape[2]
    sub = lax.broadcasted_iota(jnp.int32, (8, TILE), 0)
    blocks = NZ // 2 * tpc // 8
    for z in range(NZ):
        raw[z, 0:3] = section[:, z] * inverse
    pieces = []
    for c in range(3):
        for b in range(blocks):
            rows = [section[c, b * (8 // tpc) + m] for m in range(8 // tpc)]
            pieces.append(jnp.concatenate(rows, axis=0))
    half = NZ // 2
    for z in range(NZ):
        k, n = z // half, z % half
        index = jnp.broadcast_to(border[k : k + 1, n * TILE : (n + 1) * TILE], (8, TILE))
        lane, block = index % TILE, index // TILE
        rows = []
        for c in range(3):
            out = jnp.zeros((8, TILE), F32)
            for b in range(blocks):
                taken = jnp.take_along_axis(
                    pieces[c * blocks + b], lane, axis=1, mode="promise_in_bounds"
                )
                out = jnp.where(block == b * 8 + sub, taken, out)
            rows.append(jnp.sum(out, axis=0, keepdims=True))
        raw[z, 3] = jnp.concatenate(rows + [jnp.zeros((1, TILE), F32)], axis=0) * inverse[0]


def split3(value):
    high = value.astype(BF16).astype(F32)
    rest = value - high
    middle = rest.astype(BF16).astype(F32)
    return high, middle, rest - middle


def prepare_tile(t, rows, shift, own, lefts, lefts_t, rights, places, row, count):
    sub = lax.broadcasted_iota(jnp.int32, (8, TILE), 0)
    comp = sub % 4
    xs = [jnp.broadcast_to(v, (8, TILE)) for v in rows]
    xs = [(v - w) * shrink for v, w in zip(xs, (shift, 0.5 * slab_width, 0.5 * slab_width))]
    p = jnp.where(comp == 0, xs[0], jnp.where(comp == 1, xs[1], xs[2]))
    norm = xs[0] * xs[0] + xs[1] * xs[1] + xs[2] * xs[2]
    far = norm
    if own is not None:
        place_in = row + lax.broadcasted_iota(jnp.int32, (8, TILE), 1)
        far = jnp.where(place_in < count, norm, 4096.0)
    high, middle, low = split3(p)
    fh, fm, fl = split3(far)
    last, top = comp == 3, sub < 4
    a0 = jnp.where(last, jnp.where(top, fh, fm), high)
    a1 = jnp.where(last, jnp.where(top, fl, 1.0), middle)
    a2 = jnp.where(last, 1.0, jnp.where(top, low, high))
    left = jnp.concatenate([a0, a1, a2, jnp.zeros((8, TILE), F32)], axis=0)
    lefts[t] = left.astype(BF16)
    lefts_t[t] = left.T.astype(BF16)
    if own is not None:
        nh, nm, nl = split3(norm + 1.0 / reach_sq)
        h2, m2, l2 = -2.0 * high, -2.0 * middle, -2.0 * low
        b0 = jnp.where(last, 1.0, jnp.where(top, h2, m2))
        b1 = jnp.where(last, jnp.where(top, 1.0, nh), jnp.where(top, h2, m2))
        b2 = jnp.where(last, jnp.where(top, nm, nl), jnp.where(top, h2, l2))
        right = jnp.concatenate([b0, b1, b2, jnp.zeros((8, TILE), F32)], axis=0)
        rights[own] = right.astype(BF16)
        places[own] = p


def prepare_own(z, land, centre, count, *refs):
    half, tpc = NZ // 2, refs[2].shape[0] // NZ
    for n in range(tpc):
        rows = [land[z, c, n : n + 1, :] for c in range(3)]
        i = z * tpc + n
        prepare_tile(half + i, rows, centre, i, *refs, i * TILE, count)


def prepare_halo(z, halo, shifts, *refs):
    half, tiles = NZ // 2, refs[2].shape[0]
    upper = lax.div(z, jnp.int32(half))
    rows = [halo[z, c : c + 1, :] for c in range(3)]
    shift = jnp.where(upper == 0, shifts[0], shifts[1])
    prepare_tile(z + upper * tiles, rows, shift, None, *refs, 0, 0)


def quotients(i, buf, neighbours, lefts_t, rights):
    right = rights[i]
    for n in range(neighbours.shape[0]):
        buf[n * TILE : (n + 1) * TILE, :] = jnp.dot(
            lefts_t[neighbours[n, i]], right, preferred_element_type=F32
        )


def tile_force(i, zc, n, buf, neighbours, lefts, places, force, count):
    total = jnp.zeros((KROWS, TILE), F32)
    for k in range(0, neighbours.shape[0], 2):
        q = buf[k * TILE : (k + 2) * TILE, :]
        r = 1.0 / q
        r2 = r * r
        d = jnp.maximum((r2 - r).astype(BF16), jnp.zeros(q.shape, BF16))
        f = (d * d) * (r2 * r - 0.5 * reach_sq**3).astype(BF16)
        x = jnp.concatenate([lefts[neighbours[k, i]], lefts[neighbours[k + 1, i]]], axis=1)
        total = total + jnp.dot(x, f, preferred_element_type=F32)
    moved = total[0:8] + total[8:16] + total[16:24]
    row = i * TILE + lax.broadcasted_iota(jnp.int32, (8, TILE), 1)
    beads = lax.axis_size("bead")
    scale = jnp.where(row < count, 48.0 / 256.0 / reach_sq**5 / shrink / beads, 0.0)
    result = (places[i] * total[15:16] - moved) * scale
    for c in range(3):
        force[zc, c, n : n + 1, :] = result[c : c + 1]


def forces(neighbours, count, lefts, lefts_t, rights, places, even, odd, force, r1, near, sems):
    x, z, y = place()
    tpc = rights.shape[0] // NZ
    half = NZ // 2
    bufs = (even, odd)
    send_sem, recv_sem, near_send, near_recv = sems

    def offset(c):
        return half + lax.div(c, jnp.int32(2)) * (1 - rem(c, 2)) - lax.div(c + 1, jnp.int32(2)) * rem(c, 2)

    quotients(rem(z + half, NZ) * tpc, even, neighbours, lefts_t, rights)

    first_near = NZ - len(near_offsets())

    def compute(c):
        zc = rem(z + offset(c), NZ)
        after = rem(z + offset(jnp.minimum(c + 1, NZ - 1)), NZ)
        for n in range(tpc):
            following = zc * tpc + n + 1 if n + 1 < tpc else after * tpc
            quotients(following, bufs[(n + 1) % 2], neighbours, lefts_t, rights)
            tile_force(zc * tpc + n, zc, n, bufs[n % 2], neighbours, lefts, places, force, count)

    def leave(c, kind, dy):
        dz = offset(c)
        group_copy(force.at[rem(z + dz, NZ)], r1, send_sem, recv_sem, dz, dy, kind).start()

    def pair(g, carry):
        for m in range(2):
            compute(2 * g + m)
        for m in range(2):
            for dy in range(NY):
                leave(2 * g + m, 0, dy)
        return carry

    def chunk(c, carry):
        compute(c)
        @pl.when(c >= first_near)
        def _():
            zc = rem(z + offset(c), NZ)
            for dx in sorted(range(1, NX), key=lambda step: -min(step, NX - step)):
                for dy in reversed(range(NY)):
                    device = to_bead(bead_of(rem(x + dx, NX), zc, rem(y + dy, NY)))
                    slot = near_slot(dx, c - first_near, dy)
                    send(force.at[zc], near.at[slot], near_send.at[0], near_recv.at[c - first_near], device)

        kind = jnp.minimum(jnp.maximum(c - first_near + 1, 0), 1)
        leave(c, kind, 1)

        @pl.when(c < NZ - 1)
        def _():
            leave(c, kind, 0)

        return carry

    pairs = (first_near - 1) // 2
    lax.fori_loop(0, pairs, pair, 0)
    lax.fori_loop(2 * pairs, NZ, chunk, 0)
    r1[0] = force[z]


def kernel(
    counts, neighbours_in, border_in, section_in, out,
    neighbours, border, section, raw, land, halo, force,
    lefts, lefts_t, rights, places, even, odd,
    r1f, t2f, r2f, first_in, pxf, r1b, t2b, r2b, plain_in, pxb, near,
    load_sem, *sems,
):
    x, z, y = place()
    slab, slabs = lax.axis_index("slab"), lax.axis_size("slab")
    loads = [
        pltpu.make_async_copy(section_in, section, load_sem.at[0]),
        pltpu.make_async_copy(border_in, border, load_sem.at[1]),
        pltpu.make_async_copy(neighbours_in, neighbours, load_sem.at[2]),
    ]
    barrier = pltpu.get_barrier_semaphore()
    greeted = partners()
    for device in greeted:
        pl.semaphore_signal(barrier, inc=1, device_id=device, device_id_type=MESH)
    for load in loads:
        load.start()
    for load in loads:
        load.wait()
    pack_chunks(section, border, raw)
    pl.semaphore_wait(barrier, len(greeted))
    finish = forward_scan(raw, r1f, t2f, r2f, first_in, pxf, land, halo, sems[:10])
    q3, q4 = sems[7], sems[9]
    count = counts[0]
    box = slab_width * slabs
    centre = (slab.astype(F32) + 0.5) * slab_width
    shifts = (
        centre + jnp.where(slab == 0, box, 0.0),
        centre - jnp.where(slab == slabs - 1, box, 0.0),
    )
    refs = (lefts, lefts_t, rights, places)
    farthest = NZ // 2
    for distance in range(farthest + 1):
        chunks = [dz for dz in range(NZ) if reach(dz) == distance]
        tiles = [dz for dz in range(NZ) if reach(dz) == distance - 1]
        if distance == farthest:
            tiles += chunks
        for dz in chunks:
            if dz:
                await_bytes(land.at[0], q3.at[dz])
        for dz in tiles:
            await_bytes(halo.at[0], q4.at[dz])
        for dz in chunks:
            prepare_own(rem(z + (NZ - dz), NZ), land, centre, count, *refs)
        for dz in tiles:
            prepare_halo(rem(z + (NZ - dz), NZ), halo, shifts, *refs)
    forces(
        neighbours, count, lefts, lefts_t, rights, places, even, odd, force, r1b, near, sems[10:14]
    )
    backward_scan(r1b, near, t2b, r2b, plain_in, pxb, out, sems[10:])
    finish()


def leapfrog(section, momentum, section_force):
    level = lax.axis_index("bead").astype(F32)
    safe = jnp.maximum(level, 1.0)
    section_force = section_force / safe
    mass = jnp.where(level > 0, (level + 1.0) / safe, 1.0)
    spring = jnp.where(level > 0, omega_sq * mass, 0.0)
    step = time_step / 3.0
    push = 0.5 * step * spring
    drift = step / mass
    p = momentum + (0.5 * time_step) * section_force
    u = section
    for turn in range(3):
        p = p - push * u
        u = u + drift * p
        p = p - push * u
    return u, p


def step(section, momentum, neighbours, border_rows, counts):
    shape = section.shape
    listed = neighbours.shape[2]
    tiles = shape[2] // TILE
    tpc = tiles // NZ
    dense = (3, NZ, tpc, TILE)
    ext_tiles = tiles + NZ
    chunk, wide = (3, tpc, TILE), (4, tpc, TILE)
    anywhere = pl.BlockSpec(memory_space=pl.ANY)
    in_hbm = pl.BlockSpec(memory_space=pltpu.HBM)
    hbm = lambda array: pltpu.with_memory_space_constraint(array, pltpu.HBM)
    vmem = lambda *dims: pltpu.VMEM(dims, F32)
    scan_buffers = [
        vmem(count, *part)
        for part in (wide, chunk)
        for count in (NZ * NY, 2, NX, NX, NZ)
    ]
    one, each = DMA((1,)), DMA((NZ,))
    section, momentum = section.reshape(dense), momentum.reshape(dense)
    section_force = pl.pallas_call(
        kernel,
        out_shape=jax.ShapeDtypeStruct(dense, F32),
        in_specs=[
            pl.BlockSpec(memory_space=pltpu.SMEM),
            in_hbm,
            in_hbm,
            in_hbm,
        ],
        out_specs=anywhere,
        scratch_shapes=[
            pltpu.SMEM((listed, tiles), jnp.int32),
            pltpu.VMEM(border_rows.shape[1:], jnp.int32),
            vmem(*dense),
            vmem(NZ, *wide),
            vmem(NZ, *chunk),
            vmem(NZ, 4, TILE),
            vmem(NZ, *chunk),
            pltpu.VMEM((ext_tiles, KROWS, TILE), BF16),
            pltpu.VMEM((ext_tiles, TILE, KROWS), BF16),
            pltpu.VMEM((tiles, KROWS, TILE), BF16),
            vmem(tiles, 8, TILE),
            vmem(listed * TILE, TILE),
            vmem(listed * TILE, TILE),
        ]
        + scan_buffers
        + [vmem(len(near_slots()), *chunk)]
        + [DMA((3,))]
        + [one, DMA((NZ // 2 + 1,))]
        + [one] * 4
        + [one, each] * 2
        + [one, DMA((2,)), one, DMA((len(near_offsets()),))]
        + [one] * 7,
        compiler_params=pltpu.CompilerParams(
            collective_id=0, has_side_effects=True, vmem_limit_bytes=24 * 2**20
        ),
        name="path_step",
    )(
        counts,
        hbm(neighbours.transpose(0, 2, 1).reshape(listed, tiles)),
        hbm(border_rows.reshape(border_rows.shape[1:])),
        hbm(section),
    )
    u, p = leapfrog(section, momentum, section_force)
    return u.reshape(shape), p.reshape(shape)


def solution(mesh):
    return jax.shard_map(
        step,
        mesh=mesh,
        in_specs=(
            P("bead", None, "slab"),
            P("bead", None, "slab"),
            P("slab", None, None),
            P("slab", None, None),
            P("slab"),
        ),
        out_specs=(P("bead", None, "slab"), P("bead", None, "slab")),
        check_vma=False,
    )
```

```python
import functools
import math

import jax
import jax.numpy as jnp
from jax import lax
from jax.experimental import pallas as pl
from jax.experimental.pallas import tpu as pltpu
from jax.sharding import PartitionSpec as P

MESH = pl.DeviceIdType.MESH
time_step = 0.1
omega_sq = 4.0
slab_width = 3.0
reach_sq = 17.0
shrink = 1.0 / math.sqrt(reach_sq)
NX, NZ, NY = 4, 8, 2
TILE = 128
KROWS = 32
F32 = jnp.float32
BF16 = jnp.bfloat16
DMA = pltpu.SemaphoreType.DMA


def rem(value, size):
    return lax.rem(value, jnp.int32(size))


def place():
    bead = lax.axis_index("bead")
    return lax.div(bead, jnp.int32(NZ * NY)), rem(lax.div(bead, jnp.int32(NY)), NZ), rem(bead, NY)


def bead_of(x, z, y):
    return (x * NZ + z) * NY + y


def to_bead(bead):
    return (bead, lax.axis_index("slab"))


def group_steps():
    return [(dz, dy) for dz in range(NZ) for dy in range(NY) if dz or dy]


def reach(dz):
    return min(dz, NZ - dz)


def partners():
    x, z, y = place()
    slab, slabs = lax.axis_index("slab"), lax.axis_size("slab")
    found = []
    for dz in sorted(range(NZ), key=reach, reverse=True):
        tz = rem(z + dz, NZ)
        found += [to_bead(bead_of(x, tz, rem(y + dy, NY))) for dy in reversed(range(NY)) if dz or dy]
        found += [(bead_of(x, tz, y), rem(slab + ds, slabs)) for ds in (1, slabs - 1)]
    return found + [to_bead(bead_of(rem(x + dx, NX), z, y)) for dx in range(1, NX)]


def remote(src, dst, send_sem, recv_sem, device):
    return pltpu.make_async_remote_copy(
        src_ref=src,
        dst_ref=dst,
        send_sem=send_sem,
        recv_sem=recv_sem,
        device_id=device,
        device_id_type=MESH,
    )


def send(*args):
    copy = remote(*args)
    copy.start()
    return copy


def await_bytes(ref, sem):
    pltpu.make_async_copy(ref, ref, sem).wait()


def group_copy(src, r1, send_sem, recv_sem, dz, dy, kind=0):
    x, z, y = place()
    device = to_bead(bead_of(x, rem(z + dz, NZ), rem(y + dy, NY)))
    return remote(src, r1.at[dz * NY + dy], send_sem.at[0], recv_sem.at[kind], device)


def near_offsets():
    return (NZ - 2, 1, NZ - 1, 0) if NZ > 4 else (1, NZ - 1, 0)


def near_slots():
    return [(dx, k, dy) for dx in range(1, NX) for k in range(len(near_offsets())) for dy in range(NY)]


def near_slot(dx, k, dy):
    return ((dx - 1) * len(near_offsets()) + k) * NY + dy


def exchange_x(src, slots, send_sem, recv_sem):
    x, z, y = place()
    for dx in range(1, NX):
        device = to_bead(bead_of(rem(x + dx, NX), z, y))
        send(src, slots.at[dx], send_sem.at[0], recv_sem.at[0], device)


def level_rows(bead):
    return jnp.full((1, 1, TILE), bead.astype(F32), F32)


def slot_from(zs, ys):
    x, z, y = place()
    return rem(z + (NZ - zs), NZ) * NY + rem(y + (NY - ys), NY)


def near_first():
    return sorted(range(1, NZ), key=reach)


def forward_scan(raw, r1, t2, r2, first_in, px, land, halo, sems):
    s1, q1, s2, q2, sf, qf, s3, q3, s4, q4 = sems
    x, z, y = place()
    slab, slabs = lax.axis_index("slab"), lax.axis_size("slab")
    for dz, dy in sorted(group_steps(), key=lambda step: -reach(step[0]) - step[1]):
        group_copy(raw.at[rem(z + dz, NZ)], r1, s1, q1, dz, dy).start()
    r1[0] = raw[z]
    await_bytes(r1.at[1:], q1.at[0])

    @pl.when(x == 0)
    def _():
        for dx in range(1, NX):
            device = to_bead(bead_of(dx, z, y))
            send(r1.at[slot_from(0, 0)], first_in.at[0], sf.at[0], qf.at[0], device)
        first_in[0] = r1[slot_from(0, 0)]

    total = jnp.zeros(r1.shape[1:], F32)
    for zs in reversed(range(NZ)):
        kept = None
        for ys in reversed(range(NY)):
            one = r1[slot_from(zs, ys)]
            if zs == 0 and ys == 0:
                one = jnp.where(x == 0, 0.0, one)
            total = total + one
            kept = total if kept is None else jnp.where(y == ys, total, kept)
        px[zs] = kept
    t2[0] = total
    exchange_x(t2.at[0], r2, s2, q2)

    @pl.when(x != 0)
    def _():
        await_bytes(first_in.at[0], qf.at[0])

    await_bytes(r2.at[1:], q2.at[0])
    base = jnp.zeros(r1.shape[1:], F32)
    for dx in range(1, NX):
        xs = rem(x + (NX - dx), NX)
        base = base + jnp.where(xs > x, r2[dx], 0.0)
    first = first_in[0]
    beside = rem(slab + 1 + (slabs - 2) * lax.div(z, jnp.int32(NZ // 2)), slabs)
    for dz in near_first()[::-1] + [0]:
        tz = rem(z + dz, NZ)
        bead = bead_of(x, tz, y)
        places = first + level_rows(bead) * (px[tz] + base)
        px[tz] = places
        send(px.at[tz, 3], halo.at[z], s4.at[0], q4.at[dz], (bead, beside))
        if dz:
            send(px.at[tz, 0:3], land.at[z], s3.at[0], q3.at[dz], to_bead(bead))
        else:
            land[z] = places[0:3]

    def finish():
        await_bytes(r1.at[1:], s1.at[0])
        await_bytes(r2.at[1:], s2.at[0])
        await_bytes(land.at[1:], s3.at[0])
        await_bytes(halo, s4.at[0])

        @pl.when(x == 0)
        def _():
            await_bytes(r2.at[1:], sf.at[0])

    return finish


def backward_scan(r1, near, t2, r2, plain_in, px, out, sems):
    s1, q1, sn, qn, s2, q2, sf, qf, s3, q3, own_sem = sems
    x, z, y = place()
    far = [(dz, dy) for dz in range(NZ) for dy in range(NY) if dz not in near_offsets()]
    await_bytes(r1.at[0 : len(far)], q1.at[0])
    total = jnp.zeros(r1.shape[1:], F32)
    plain = jnp.zeros(r1.shape[1:], F32)
    for dz, dy in far:
        one = r1[dz * NY + dy]
        plain = plain + one
        total = total + one * level_rows(bead_of(x, rem(z + (NZ - dz), NZ), rem(y + (NY - dy), NY)))
    t2[0] = total
    t2[1] = plain
    exchange_x(t2.at[0], r2, s2, q2)

    @pl.when(x != 0)
    def _():
        send(t2.at[1], plain_in.at[x], sf.at[0], qf.at[0], to_bead(bead_of(0, z, y)))

    def gather_near(k, base, plain):
        await_bytes(near.at[0 : (NX - 1) * NY], qn.at[k])
        for dx in range(1, NX):
            for dy in range(NY):
                xs = rem(x + (NX - dx), NX)
                source = bead_of(xs, rem(z + (NZ - near_offsets()[k]), NZ), rem(y + (NY - dy), NY))
                one = near[near_slot(dx, k, dy)]
                plain = plain + one
                base = base + jnp.where(xs < x, one * level_rows(source), 0.0)
        return base, plain

    base = jnp.zeros(r1.shape[1:], F32)
    plain = jnp.zeros(r1.shape[1:], F32)
    last = len(near_offsets()) - 1
    for k in range(last):
        base, plain = gather_near(k, base, plain)
    await_bytes(r1.at[0 : len(group_steps()) - len(far)], q1.at[1])
    total = jnp.zeros(r1.shape[1:], F32)
    for zs in range(NZ):
        kept = None
        for ys in range(NY):
            one = r1[slot_from(zs, ys)]
            plain = plain + one
            total = total + one * level_rows(bead_of(x, zs, ys))
            kept = total if kept is None else jnp.where(y == ys, total, kept)
        px[zs] = kept
    base, plain = gather_near(last, base, plain)

    @pl.when(x == 0)
    def _():
        plain_in[0] = plain
        await_bytes(plain_in.at[1:], qf.at[0])

    await_bytes(r2.at[1:], q2.at[0])
    for dx in range(1, NX):
        xs = rem(x + (NX - dx), NX)
        base = base + jnp.where(xs < x, r2[dx], 0.0)
    @pl.when((x == 0) & (y == 0))
    def _():
        everything = plain_in[0]
        for xs in range(1, NX):
            everything = everything + plain_in[xs]
        px[0] = everything

    for dz in near_first()[::-1] + [0]:
        tz = rem(z + dz, NZ)
        px[tz] = px[tz] + jnp.where(bead_of(x, tz, y) == 0, 0.0, base)
        if dz:
            device = to_bead(bead_of(x, tz, y))
            send(px.at[tz], out.at[:, z], s3.at[0], q3.at[0], device)
        else:
            own = pltpu.make_async_copy(px.at[tz], out.at[:, z], own_sem.at[0])
            own.start()

    await_bytes(px.at[1:], q3.at[0])
    own.wait()
    await_bytes(r1.at[1:], s1.at[0])
    await_bytes(near, sn.at[0])
    await_bytes(r2.at[1:], s2.at[0])
    await_bytes(px.at[1:], s3.at[0])

    @pl.when(x != 0)
    def _():
        await_bytes(t2.at[1], sf.at[0])


def pack_chunks(section, border, raw):
    level = level_rows(lax.axis_index("bead"))
    inverse = 1.0 / jnp.maximum(level, 1.0)
    tpc = section.shape[2]
    sub = lax.broadcasted_iota(jnp.int32, (8, TILE), 0)
    blocks = NZ // 2 * tpc // 8
    for z in range(NZ):
        raw[z, 0:3] = section[:, z] * inverse
    pieces = []
    for c in range(3):
        for b in range(blocks):
            rows = [section[c, b * (8 // tpc) + m] for m in range(8 // tpc)]
            pieces.append(jnp.concatenate(rows, axis=0))
    half = NZ // 2
    for z in range(NZ):
        k, n = z // half, z % half
        index = jnp.broadcast_to(border[k : k + 1, n * TILE : (n + 1) * TILE], (8, TILE))
        lane, block = index % TILE, index // TILE
        rows = []
        for c in range(3):
            out = jnp.zeros((8, TILE), F32)
            for b in range(blocks):
                taken = jnp.take_along_axis(
                    pieces[c * blocks + b], lane, axis=1, mode="promise_in_bounds"
                )
                out = jnp.where(block == b * 8 + sub, taken, out)
            rows.append(jnp.sum(out, axis=0, keepdims=True))
        raw[z, 3] = jnp.concatenate(rows + [jnp.zeros((1, TILE), F32)], axis=0) * inverse[0]


def split3(value):
    high = value.astype(BF16).astype(F32)
    rest = value - high
    middle = rest.astype(BF16).astype(F32)
    return high, middle, rest - middle


def prepare_tile(t, rows, shift, own, lefts, lefts_t, rights, places, row, count):
    sub = lax.broadcasted_iota(jnp.int32, (8, TILE), 0)
    comp = sub % 4
    xs = [jnp.broadcast_to(v, (8, TILE)) for v in rows]
    xs = [(v - w) * shrink for v, w in zip(xs, (shift, 0.5 * slab_width, 0.5 * slab_width))]
    p = jnp.where(comp == 0, xs[0], jnp.where(comp == 1, xs[1], xs[2]))
    norm = xs[0] * xs[0] + xs[1] * xs[1] + xs[2] * xs[2]
    far = norm
    if own is not None:
        place_in = row + lax.broadcasted_iota(jnp.int32, (8, TILE), 1)
        far = jnp.where(place_in < count, norm, 4096.0)
    high, middle, low = split3(p)
    fh, fm, fl = split3(far)
    last, top = comp == 3, sub < 4
    a0 = jnp.where(last, jnp.where(top, fh, fm), high)
    a1 = jnp.where(last, jnp.where(top, fl, 1.0), middle)
    a2 = jnp.where(last, 1.0, jnp.where(top, low, high))
    left = jnp.concatenate([a0, a1, a2, jnp.zeros((8, TILE), F32)], axis=0)
    lefts[t] = left.astype(BF16)
    lefts_t[t] = left.T.astype(BF16)
    if own is not None:
        nh, nm, nl = split3(norm + 1.0 / reach_sq)
        h2, m2, l2 = -2.0 * high, -2.0 * middle, -2.0 * low
        b0 = jnp.where(last, 1.0, jnp.where(top, h2, m2))
        b1 = jnp.where(last, jnp.where(top, 1.0, nh), jnp.where(top, h2, m2))
        b2 = jnp.where(last, jnp.where(top, nm, nl), jnp.where(top, h2, l2))
        right = jnp.concatenate([b0, b1, b2, jnp.zeros((8, TILE), F32)], axis=0)
        rights[own] = right.astype(BF16)
        places[own] = p


def prepare_own(z, land, centre, count, *refs):
    half, tpc = NZ // 2, refs[2].shape[0] // NZ
    for n in range(tpc):
        rows = [land[z, c, n : n + 1, :] for c in range(3)]
        i = z * tpc + n
        prepare_tile(half + i, rows, centre, i, *refs, i * TILE, count)


def prepare_halo(z, halo, shifts, *refs):
    half, tiles = NZ // 2, refs[2].shape[0]
    upper = lax.div(z, jnp.int32(half))
    rows = [halo[z, c : c + 1, :] for c in range(3)]
    shift = jnp.where(upper == 0, shifts[0], shifts[1])
    prepare_tile(z + upper * tiles, rows, shift, None, *refs, 0, 0)


def quotients(i, buf, neighbours, lefts_t, rights):
    right = rights[i]
    for n in range(neighbours.shape[0]):
        buf[n * TILE : (n + 1) * TILE, :] = jnp.dot(
            lefts_t[neighbours[n, i]], right, preferred_element_type=F32
        )


def tile_force(i, zc, n, buf, neighbours, lefts, places, force, count):
    total = jnp.zeros((KROWS, TILE), F32)
    for k in range(0, neighbours.shape[0], 2):
        q = buf[k * TILE : (k + 2) * TILE, :]
        r = 1.0 / q
        r2 = r * r
        d = jnp.maximum((r2 - r).astype(BF16), jnp.zeros(q.shape, BF16))
        f = (d * d) * (r2 * r - 0.5 * reach_sq**3).astype(BF16)
        x = jnp.concatenate([lefts[neighbours[k, i]], lefts[neighbours[k + 1, i]]], axis=1)
        total = total + jnp.dot(x, f, preferred_element_type=F32)
    moved = total[0:8] + total[8:16] + total[16:24]
    row = i * TILE + lax.broadcasted_iota(jnp.int32, (8, TILE), 1)
    beads = lax.axis_size("bead")
    scale = jnp.where(row < count, 48.0 / 256.0 / reach_sq**5 / shrink / beads, 0.0)
    result = (places[i] * total[15:16] - moved) * scale
    for c in range(3):
        force[zc, c, n : n + 1, :] = result[c : c + 1]


def forces(neighbours, count, lefts, lefts_t, rights, places, even, odd, force, r1, near, sems):
    x, z, y = place()
    tpc = rights.shape[0] // NZ
    half = NZ // 2
    bufs = (even, odd)
    send_sem, recv_sem, near_send, near_recv = sems

    def offset(c):
        return half + lax.div(c, jnp.int32(2)) * (1 - rem(c, 2)) - lax.div(c + 1, jnp.int32(2)) * rem(c, 2)

    quotients(rem(z + half, NZ) * tpc, even, neighbours, lefts_t, rights)

    first_near = NZ - len(near_offsets())

    def compute(c):
        zc = rem(z + offset(c), NZ)
        after = rem(z + offset(jnp.minimum(c + 1, NZ - 1)), NZ)
        for n in range(tpc):
            following = zc * tpc + n + 1 if n + 1 < tpc else after * tpc
            quotients(following, bufs[(n + 1) % 2], neighbours, lefts_t, rights)
            tile_force(zc * tpc + n, zc, n, bufs[n % 2], neighbours, lefts, places, force, count)

    def leave(c, kind, dy):
        dz = offset(c)
        group_copy(force.at[rem(z + dz, NZ)], r1, send_sem, recv_sem, dz, dy, kind).start()

    def pair(g, carry):
        for m in range(2):
            compute(2 * g + m)
        for m in range(2):
            for dy in range(NY):
                leave(2 * g + m, 0, dy)
        return carry

    def chunk(c, carry):
        compute(c)
        @pl.when(c >= first_near)
        def _():
            zc = rem(z + offset(c), NZ)
            for dx in sorted(range(1, NX), key=lambda step: -min(step, NX - step)):
                for dy in reversed(range(NY)):
                    device = to_bead(bead_of(rem(x + dx, NX), zc, rem(y + dy, NY)))
                    slot = near_slot(dx, c - first_near, dy)
                    send(force.at[zc], near.at[slot], near_send.at[0], near_recv.at[c - first_near], device)

        kind = jnp.minimum(jnp.maximum(c - first_near + 1, 0), 1)
        leave(c, kind, 1)

        @pl.when(c < NZ - 1)
        def _():
            leave(c, kind, 0)

        return carry

    pairs = (first_near - 1) // 2
    lax.fori_loop(0, pairs, pair, 0)
    lax.fori_loop(2 * pairs, NZ, chunk, 0)
    r1[0] = force[z]


def kernel(
    counts, neighbours_in, border_in, section_in, out,
    neighbours, border, section, raw, land, halo, force,
    lefts, lefts_t, rights, places, even, odd,
    r1f, t2f, r2f, first_in, pxf, r1b, t2b, r2b, plain_in, pxb, near,
    load_sem, *sems,
):
    x, z, y = place()
    slab, slabs = lax.axis_index("slab"), lax.axis_size("slab")
    loads = [
        pltpu.make_async_copy(section_in, section, load_sem.at[0]),
        pltpu.make_async_copy(border_in, border, load_sem.at[1]),
        pltpu.make_async_copy(neighbours_in, neighbours, load_sem.at[2]),
    ]
    barrier = pltpu.get_barrier_semaphore()
    greeted = partners()
    for device in greeted:
        pl.semaphore_signal(barrier, inc=1, device_id=device, device_id_type=MESH)
    for load in loads:
        load.start()
    for load in loads:
        load.wait()
    pack_chunks(section, border, raw)
    pl.semaphore_wait(barrier, len(greeted))
    finish = forward_scan(raw, r1f, t2f, r2f, first_in, pxf, land, halo, sems[:10])
    q3, q4 = sems[7], sems[9]
    count = counts[0]
    box = slab_width * slabs
    centre = (slab.astype(F32) + 0.5) * slab_width
    shifts = (
        centre + jnp.where(slab == 0, box, 0.0),
        centre - jnp.where(slab == slabs - 1, box, 0.0),
    )
    refs = (lefts, lefts_t, rights, places)
    farthest = NZ // 2
    for distance in range(farthest + 1):
        chunks = [dz for dz in range(NZ) if reach(dz) == distance]
        tiles = [dz for dz in range(NZ) if reach(dz) == distance - 1]
        if distance == farthest:
            tiles += chunks
        for dz in chunks:
            if dz:
                await_bytes(land.at[0], q3.at[dz])
        for dz in tiles:
            await_bytes(halo.at[0], q4.at[dz])
        for dz in chunks:
            prepare_own(rem(z + (NZ - dz), NZ), land, centre, count, *refs)
        for dz in tiles:
            prepare_halo(rem(z + (NZ - dz), NZ), halo, shifts, *refs)
    forces(
        neighbours, count, lefts, lefts_t, rights, places, even, odd, force, r1b, near, sems[10:14]
    )
    backward_scan(r1b, near, t2b, r2b, plain_in, pxb, out, sems[10:])
    finish()


def leapfrog(section, momentum, section_force):
    level = lax.axis_index("bead").astype(F32)
    safe = jnp.maximum(level, 1.0)
    section_force = section_force / safe
    mass = jnp.where(level > 0, (level + 1.0) / safe, 1.0)
    spring = jnp.where(level > 0, omega_sq * mass, 0.0)
    step = time_step / 3.0
    push = 0.5 * step * spring
    drift = step / mass
    p = momentum + (0.5 * time_step) * section_force
    u = section
    for turn in range(3):
        p = p - push * u
        u = u + drift * p
        p = p - push * u
    return u, p


def step(section, momentum, neighbours, border_rows, counts):
    shape = section.shape
    listed = neighbours.shape[2]
    tiles = shape[2] // TILE
    tpc = tiles // NZ
    dense = (3, NZ, tpc, TILE)
    ext_tiles = tiles + NZ
    chunk, wide = (3, tpc, TILE), (4, tpc, TILE)
    anywhere = pl.BlockSpec(memory_space=pl.ANY)
    in_hbm = pl.BlockSpec(memory_space=pltpu.HBM)
    hbm = lambda array: pltpu.with_memory_space_constraint(array, pltpu.HBM)
    vmem = lambda *dims: pltpu.VMEM(dims, F32)
    scan_buffers = [
        vmem(count, *part)
        for part in (wide, chunk)
        for count in (NZ * NY, 2, NX, NX, NZ)
    ]
    one, each = DMA((1,)), DMA((NZ,))
    section, momentum = section.reshape(dense), momentum.reshape(dense)
    section_force = pl.pallas_call(
        kernel,
        out_shape=jax.ShapeDtypeStruct(dense, F32),
        in_specs=[
            pl.BlockSpec(memory_space=pltpu.SMEM),
            in_hbm,
            in_hbm,
            in_hbm,
        ],
        out_specs=anywhere,
        scratch_shapes=[
            pltpu.SMEM((listed, tiles), jnp.int32),
            pltpu.VMEM(border_rows.shape[1:], jnp.int32),
            vmem(*dense),
            vmem(NZ, *wide),
            vmem(NZ, *chunk),
            vmem(NZ, 4, TILE),
            vmem(NZ, *chunk),
            pltpu.VMEM((ext_tiles, KROWS, TILE), BF16),
            pltpu.VMEM((ext_tiles, TILE, KROWS), BF16),
            pltpu.VMEM((tiles, KROWS, TILE), BF16),
            vmem(tiles, 8, TILE),
            vmem(listed * TILE, TILE),
            vmem(listed * TILE, TILE),
        ]
        + scan_buffers
        + [vmem(len(near_slots()), *chunk)]
        + [DMA((3,))]
        + [one] * 6
        + [one, each] * 2
        + [one, DMA((2,)), one, DMA((len(near_offsets()),))]
        + [one] * 7,
        compiler_params=pltpu.CompilerParams(
            collective_id=0, has_side_effects=True, vmem_limit_bytes=24 * 2**20
        ),
        name="path_step",
    )(
        counts,
        hbm(neighbours.transpose(0, 2, 1).reshape(listed, tiles)),
        hbm(border_rows.reshape(border_rows.shape[1:])),
        hbm(section),
    )
    u, p = leapfrog(section, momentum, section_force)
    return u.reshape(shape), p.reshape(shape)


def solution(mesh):
    return jax.shard_map(
        step,
        mesh=mesh,
        in_specs=(
            P("bead", None, "slab"),
            P("bead", None, "slab"),
            P("slab", None, None),
            P("slab", None, None),
            P("slab"),
        ),
        out_specs=(P("bead", None, "slab"), P("bead", None, "slab")),
        check_vma=False,
    )
```
